32 devices in a mesh: seq: 8 (over y, x, core), tp: 4 (over z).
Axes of the slice: x: 2, y: 2, z: 4, core: 2. Of those that a mesh axis runs over, the one named last changes fastest.
Arguments:
- projected: bfloat16 [1, 8192, 3, 4096], P(None, 'seq', None, 'tp'), may hold values from -6 to 6
- short_kernel: float32 [3, 3, 4096], P(None, None, 'tp'), may hold values from -3 to 3
- filters: float32 [2, 4096, 8192], P(None, ('tp', 'seq')), may hold values from -2 to 2
- skip_gain: float32 [2, 4096], P(None, ('tp', 'seq')), may hold values from -3 to 3
- out_weight: bfloat16 [4096, 4096], P('tp'), may hold values from -0.09375 to 0.09375
- out_grad: bfloat16 [1, 8192, 4096], P(None, 'seq', 'tp'), may hold values from -6 to 6
Outputs:
- output: bfloat16 [1, 8192, 4096], P(None, 'seq', 'tp')
- projected_grad: bfloat16 [1, 8192, 3, 4096], P(None, 'seq', None, 'tp')
- filter_grad: float32 [2, 4096, 8192], P(None, ('tp', 'seq'))
The draws below stay inside these ranges and needn't reach their ends.
All inputs are finite; a program needn't handle non-finite values.
Results may differ from the reference program's by a relative error of at most 0.0095.
Values may be sent and summed in bfloat16 or wider, within the bound.
A program may use at most 384 MiB of HBM per device.

```python
import math
import jax
import jax.numpy as jnp
from jax import lax

D = 4096
LEN = 8192
SEQS = 1
N_TP = 4


def draw_filters(key, part):
    rate_key = jax.random.fold_in(key, 11)
    noise_key = jax.random.fold_in(key, 12)
    rates = jnp.exp(jax.random.uniform(rate_key, (2, D, 1), jnp.float32, math.log(0.5 / LEN), math.log(1.0 / 30.0)))
    positions = jnp.arange(LEN, dtype=jnp.float32)[None, None, :]
    noise = jnp.clip(jax.random.normal(noise_key, (2, D, LEN), jnp.float32), -6.0, 6.0)
    return noise * jnp.sqrt(rates) * jnp.exp(-rates * positions)


def block_scale(rng, extent, pieces, smallest, high):
    loudness, own = 1.0, jax.random.fold_in(rng, 6)
    for position, shards_of in pieces:
        draws = jnp.exp(jax.random.uniform(jax.random.fold_in(own, position), (shards_of,), jnp.float32, smallest / len(pieces), high / len(pieces)))
        loudness = loudness * jnp.repeat(draws, extent[position] // shards_of).reshape([-1 if axis == position else 1 for axis in range(len(extent))])
    return loudness


def gaussian(stream_key, extent, spread, limit, split=(), kind=jnp.bfloat16):
    drawn = jax.random.normal(stream_key, extent, jnp.float32) * spread
    if len(split) > 0:
        drawn = block_scale(stream_key, extent, split, -0.22, 0.18) * drawn
    return jnp.clip(drawn, min=-limit, max=limit).astype(kind)


def setup_inputs(seed: int = 0) -> dict:
    streams_of = jax.random.split(jax.random.key(seed), 7)
    return {
        "projected": gaussian(streams_of[0], (SEQS, LEN, 3, D), 1.0, 6.0, ((1, 8), (3, 4))),
        "short_kernel": gaussian(streams_of[1], (3, 3, D), 0.6, 3.0, ((2, 4),), jnp.float32),
        "filters": draw_filters(jax.random.fold_in(streams_of[6], 71), 0),
        "skip_gain": gaussian(streams_of[3], (2, D), 1.0, 3.0, ((1, 32),), jnp.float32),
        "out_weight": gaussian(streams_of[4], (D, D), D ** -0.5, 0.09375, ((0, 4),)),
        "out_grad": gaussian(streams_of[5], (SEQS, LEN, D), 1.0, 6.0, ((1, 8), (2, 4))),
    }


def causal_conv(signal, filter_spectrum, length):
    spectrum = jnp.fft.rfft(signal, n=2 * length, axis=-1)
    return jnp.fft.irfft(spectrum * filter_spectrum, n=2 * length, axis=-1)[..., :length]


def correlate(left_spectrum, right_spectrum, length):
    return jnp.fft.irfft(jnp.conj(left_spectrum) * right_spectrum, n=2 * length, axis=-1)[..., :length]


def forward_block(package):
    short_block, filt, gain = package
    short_v = short_block[0].astype(jnp.float32)
    short_x1 = short_block[1].astype(jnp.float32)
    spec_zero = jnp.fft.rfft(filt[0], n=2 * LEN, axis=-1)
    spec_one = jnp.fft.rfft(filt[1], n=2 * LEN, axis=-1)
    first_conv = gain[0][None, :, None] * short_v + causal_conv(short_v, spec_zero[None], LEN)
    middle = short_x1 * first_conv
    second = gain[1][None, :, None] * middle + causal_conv(middle, spec_one[None], LEN)
    return second.astype(jnp.bfloat16)


def backward_block(package):
    short_block, filt, gain, back_second = package
    short_v = short_block[0].astype(jnp.float32)
    short_x1 = short_block[1].astype(jnp.float32)
    spec_zero = jnp.fft.rfft(filt[0], n=2 * LEN, axis=-1)
    spec_one = jnp.fft.rfft(filt[1], n=2 * LEN, axis=-1)
    spec_short = jnp.fft.rfft(short_v, n=2 * LEN, axis=-1)
    first_conv = gain[0][None, :, None] * short_v + jnp.fft.irfft(spec_short * spec_zero[None], n=2 * LEN, axis=-1)[..., :LEN]
    middle = short_x1 * first_conv
    spec_middle = jnp.fft.rfft(middle, n=2 * LEN, axis=-1)
    back_sec = back_second.astype(jnp.float32)
    spec_back_sec = jnp.fft.rfft(back_sec, n=2 * LEN, axis=-1)
    back_middle = gain[1][None, :, None] * back_sec + correlate(spec_one[None], spec_back_sec, LEN)
    grad_one = jnp.sum(correlate(spec_middle, spec_back_sec, LEN), axis=0)
    back_x1 = (back_middle * first_conv).astype(jnp.bfloat16)
    back_first = back_middle * short_x1
    spec_back_first = jnp.fft.rfft(back_first, n=2 * LEN, axis=-1)
    back_v = (gain[0][None, :, None] * back_first + correlate(spec_zero[None], spec_back_first, LEN)).astype(jnp.bfloat16)
    grad_zero = jnp.sum(correlate(spec_short, spec_back_first, LEN), axis=0)
    return back_v, back_x1, jnp.stack([grad_zero, grad_one])


def reference(projected, short_kernel, filters, skip_gain, out_weight, out_grad):
    seq_count, length, _, width = projected.shape
    chan_block = math.gcd(width, 256)
    block_count = width // chan_block
    padded = jnp.pad(projected.astype(jnp.float32), ((0, 0), (2, 0), (0, 0), (0, 0)))
    short = sum(short_kernel[:, offset, :] * padded[:, 2 - offset:2 - offset + length] for offset in range(3)).astype(jnp.bfloat16)
    channel = jnp.transpose(short, (2, 0, 3, 1)).reshape(3, seq_count, block_count, chan_block, length).transpose(2, 0, 1, 3, 4)
    filt_blocks = filters.reshape(2, block_count, chan_block, length).transpose(1, 0, 2, 3)
    gain_blocks = skip_gain.reshape(2, block_count, chan_block).transpose(1, 0, 2)

    def unblock(blocked):
        return blocked.transpose(1, 0, 2, 3).reshape(seq_count, width, length).transpose(0, 2, 1)

    second = unblock(lax.map(forward_block, (channel, filt_blocks, gain_blocks)))
    short_x2 = short[:, :, 2, :].astype(jnp.float32)
    gated = (short_x2 * second.astype(jnp.float32)).astype(jnp.bfloat16)
    flat_gated = gated.reshape(seq_count * length, width)
    group = width // N_TP
    output = jnp.zeros((seq_count * length, width), jnp.float32)
    for member in range(N_TP):
        partial_out = jnp.dot(flat_gated[:, member * group:(member + 1) * group], out_weight[member * group:(member + 1) * group], preferred_element_type=jnp.float32)
        output = output + partial_out.astype(jnp.bfloat16).astype(jnp.float32)
    output = output.astype(jnp.bfloat16).reshape(seq_count, length, width)
    back_gated = lax.dot_general(out_grad.reshape(seq_count * length, width), out_weight, (((1,), (1,)), ((), ())), preferred_element_type=jnp.float32)
    back_gated = back_gated.astype(jnp.bfloat16).reshape(seq_count, length, width).astype(jnp.float32)
    back_second = (back_gated * short_x2).astype(jnp.bfloat16)
    back_x2 = (back_gated * second.astype(jnp.float32)).astype(jnp.bfloat16)
    back_blocks = back_second.transpose(0, 2, 1).reshape(seq_count, block_count, chan_block, length).transpose(1, 0, 2, 3)
    back_v, back_x1, grad_blocks = lax.map(backward_block, (channel, filt_blocks, gain_blocks, back_blocks))
    back_all = jnp.stack([unblock(back_v), unblock(back_x1), back_x2], axis=2)
    tail = jnp.pad(back_all.astype(jnp.float32), ((0, 0), (0, 2), (0, 0), (0, 0)))
    projected_grad = sum(short_kernel[:, offset, :] * tail[:, offset:offset + length] for offset in range(3)).astype(jnp.bfloat16)
    filter_grad = grad_blocks.transpose(1, 0, 2, 3).reshape(2, width, length) * (seq_count * length) ** -0.5
    return output, projected_grad, filter_grad
```

```python
import functools
import math

import jax
import jax.numpy as jnp
import ml_dtypes
import numpy as np
from jax import lax
from jax.experimental import pallas as pl
from jax.experimental.pallas import tpu as pltpu
from jax.sharding import PartitionSpec as P

F32 = jnp.float32
BF16 = jnp.bfloat16
INNER = 128
SUB = 8
ROWS = 16
SIDE = 8


def spread_table(outer, scale):
    freq = np.arange(2 * outer * SUB)[:, None]
    time = np.arange(outer * SUB)[None, :]
    row = freq // SUB
    turn = 4 * outer
    phase = (4 * (row % outer) + 1) * (time // SUB) + outer * (row // outer)
    value = np.cos((phase % turn) * (2.0 * math.pi / turn)) * scale
    return np.where(freq % SUB == time % SUB, value, 0.0)


def transform_tables(outer):
    total = outer * INNER
    ids = np.arange(INNER)
    twist = 2.0 * math.pi * (np.arange(outer)[:, None] + 0.25) * ids[None, :] / total
    inner = 2.0 * math.pi * (ids[:, None] * ids[None, :] % INNER) / INNER
    angle = twist[:, None, :] + inner[None]
    cos, sin = np.cos(angle), np.sin(angle)
    mix = np.concatenate(
        [np.concatenate([cos, sin], axis=2), np.concatenate([-sin, cos], axis=2)], axis=1
    )
    opening = spread_table(outer, 1.0)
    closing = spread_table(outer, 1.0 / total).T
    unmix = np.swapaxes(mix, 1, 2)
    return [jnp.asarray(np.ascontiguousarray(t).astype(ml_dtypes.bfloat16)) for t in (opening, closing, mix, unmix)]


def mul(a, b):
    return jnp.dot(a, b, preferred_element_type=F32)


def halves(spec):
    return spec[:INNER].astype(F32), spec[INNER:].astype(F32)


def cmul(a, b):
    (ar, ai), (br, bi) = a, b
    return ar * br - ai * bi, ar * bi + ai * br


def conj_mul(a, b):
    (ar, ai), (br, bi) = a, b
    return ar * br + ai * bi, ar * bi - ai * br


def packed(pair):
    return jnp.concatenate(pair, axis=0).astype(BF16)


def open_phase(opening, read, spec):
    twice, inner, lanes = spec.shape
    outer = twice // 2

    def step(at, carry):
        row = pl.multiple_of(at * ROWS, ROWS)
        signal = read(row)
        wide = jnp.concatenate([signal[:, :SUB], signal[:, SUB:]], axis=2)
        flat = wide.reshape(outer * SUB, 2 * lanes).astype(BF16)
        out = mul(opening[...], flat).reshape(twice, SUB, 2 * lanes)
        spec[:, pl.ds(row, SUB), :] = out[:, :, :lanes]
        spec[:, pl.ds(row + SUB, SUB), :] = out[:, :, lanes:]
        return carry

    lax.fori_loop(0, inner // ROWS, step, 0)


def close_phase(closing, spec, write):
    twice, inner, lanes = spec.shape
    outer = twice // 2

    def step(at, carry):
        row = pl.multiple_of(at * ROWS, ROWS)
        wide = jnp.concatenate([spec[:, pl.ds(row, SUB), :], spec[:, pl.ds(row + SUB, SUB), :]], axis=2)
        flat = wide.reshape(twice * SUB, 2 * lanes).astype(BF16)
        out = mul(closing[...], flat).reshape(outer, SUB, 2 * lanes)
        write(row, jnp.concatenate([out[:, :, :lanes], out[:, :, lanes:]], axis=1))
        return carry

    lax.fori_loop(0, inner // ROWS, step, 0)


def side_loop(outer, waits, body):
    def step(at, carry):
        for wait in waits:
            wait(at)
        base = pl.multiple_of(at * SIDE, SIDE)
        body([base + i for i in range(SIDE)])
        return carry

    lax.fori_loop(0, outer // SIDE, step, 0)


def fetch(sources, buffers, sems):
    outer = buffers[0].shape[0]

    def piece(which, at):
        rows = pl.ds(at * SIDE, SIDE)
        return pltpu.make_async_copy(sources[which].at[rows], buffers[which].at[rows], sems.at[which, at])

    for at in range(outer // SIDE):
        for which in range(len(sources)):
            piece(which, at).start()
    return [lambda at, which=which: piece(which, at).wait() for which in range(len(sources))]


def columns(spec, ids):
    outer = spec.shape[0] // 2
    return [packed([spec[i], spec[outer + i]]) for i in ids]


def put_columns(spec, ids, values):
    outer = spec.shape[0] // 2
    for i, value in zip(ids, values):
        spec[i] = value[:INNER]
        spec[outer + i] = value[INNER:]


def filters_body(opening, mix_hbm, filt, out, spec, sig, mix, sems):
    waits = fetch([mix_hbm], [mix], sems)
    outer = sig.shape[0]

    def turn(p, carry):
        sig[p] = jnp.transpose(filt[0, :, pl.ds(pl.multiple_of(p * INNER, INNER), INNER)])
        return carry

    lax.fori_loop(0, outer, turn, 0)
    open_phase(opening, lambda row: sig[:, pl.ds(row, ROWS), :], spec)

    def body(ids):
        results = [mul(mix[i], col) for i, col in zip(ids, columns(spec, ids))]
        for i, value in zip(ids, results):
            out[0, i] = value.astype(BF16)

    side_loop(outer, waits, body)


def conv_phase(spec, filt, mix, unmix, waits, kept, product):
    def body(ids):
        seen = [mul(mix[i], col) for i, col in zip(ids, columns(spec, ids))]
        mixed = [packed(product(halves(filt[i]), halves(x))) for i, x in zip(ids, seen)]
        done = [mul(unmix[i], y) for i, y in zip(ids, mixed)]
        for i, x in zip(ids, seen):
            kept[i] = x.astype(BF16)
        put_columns(spec, ids, done)

    side_loop(filt.shape[0], waits, body)


def first_body(which, opening, closing, gain, v, mix_hbm, unmix_hbm, filt_hbm, kept, first, spec, mix, unmix, filt, sems):
    waits = fetch([mix_hbm, unmix_hbm, filt_hbm.at[which]], [mix, unmix, filt], sems)
    open_phase(opening, lambda row: v[:, pl.ds(row, ROWS), :].astype(F32), spec)
    conv_phase(spec, filt, mix, unmix, waits, kept, cmul)
    g0 = gain[0:1, :][None]

    def write(row, value):
        rows = pl.ds(row, ROWS)
        first[:, rows, :] = g0 * v[:, rows, :].astype(F32) + value

    close_phase(closing, spec, write)


def second_body(
    which, opening, closing, gain, first, x1, mix_hbm, unmix_hbm, filt_hbm, kept, second, spec, mid, mix, unmix, filt, sems
):
    waits = fetch([mix_hbm, unmix_hbm, filt_hbm.at[which]], [mix, unmix, filt], sems)

    def read(row):
        rows = pl.ds(row, ROWS)
        value = x1[:, rows, :].astype(F32) * first[:, rows, :]
        mid[:, rows, :] = value
        return value

    open_phase(opening, read, spec)
    conv_phase(spec, filt, mix, unmix, waits, kept, cmul)
    g1 = gain[1:2, :][None]

    def write(row, value):
        rows = pl.ds(row, ROWS)
        second[:, rows, :] = (g1 * mid[:, rows, :] + value).astype(BF16)

    close_phase(closing, spec, write)


def back_second_body(
    which, opening, closing, gain, bs, first, x1, mix_hbm, unmix_hbm, filt_hbm, kept, bf, bx1, spec, mix, unmix, filt, sems
):
    waits = fetch([mix_hbm, unmix_hbm, filt_hbm.at[which]], [mix, unmix, filt], sems)
    open_phase(opening, lambda row: bs[:, pl.ds(row, ROWS), :].astype(F32), spec)
    conv_phase(spec, filt, mix, unmix, waits, kept, conj_mul)
    g1 = gain[1:2, :][None]

    def write(row, value):
        rows = pl.ds(row, ROWS)
        back_middle = g1 * bs[:, rows, :].astype(F32) + value
        bf[:, rows, :] = back_middle * x1[:, rows, :].astype(F32)
        bx1[:, rows, :] = (back_middle * first[:, rows, :]).astype(BF16)

    close_phase(closing, spec, write)


def back_first_body(which, opening, closing, gain, bf, mix_hbm, unmix_hbm, filt_hbm, kept, bv, spec, mix, unmix, filt, sems):
    waits = fetch([mix_hbm, unmix_hbm, filt_hbm.at[which]], [mix, unmix, filt], sems)
    open_phase(opening, lambda row: bf[:, pl.ds(row, ROWS), :], spec)
    conv_phase(spec, filt, mix, unmix, waits, kept, conj_mul)
    g0 = gain[0:1, :][None]

    def write(row, value):
        rows = pl.ds(row, ROWS)
        bv[:, rows, :] = (g0 * bf[:, rows, :] + value).astype(BF16)

    close_phase(closing, spec, write)


def grad_body(scale, has_prior, closing, unmix_hbm, left_hbm, right_hbm, *refs):
    out, spec, closed, unmix, left, right, sems = refs[has_prior:]
    waits = fetch([unmix_hbm, left_hbm, right_hbm], [unmix, left, right], sems)
    outer = closed.shape[0]

    def body(ids):
        mixed = [packed(conj_mul(halves(left[i]), halves(right[i]))) for i in ids]
        put_columns(spec, ids, [mul(unmix[i], y) for i, y in zip(ids, mixed)])

    side_loop(outer, waits, body)

    def write(row, value):
        closed[:, pl.ds(row, ROWS), :] = value * scale

    close_phase(closing, spec, write)

    def turn(p, carry):
        out[0, :, pl.ds(pl.multiple_of(p * INNER, INNER), INNER)] = jnp.transpose(closed[p])
        return carry

    lax.fori_loop(0, outer, turn, 0)


params = pltpu.CompilerParams(vmem_limit_bytes=58 << 20)
VMEM = pl.BlockSpec(memory_space=pltpu.VMEM)
ANY = pl.BlockSpec(memory_space=pl.ANY)


def table_buffer(outer):
    return pltpu.VMEM((outer, 2 * INNER, 2 * INNER), BF16)


def spectrum(outer, lanes):
    return (outer, 2 * INNER, lanes)


def cost(us):
    return pl.CostEstimate(flops=int(us * 0.8e9), bytes_accessed=int(us * 2e6), transcendentals=0)


def filter_spectra(tables, filters):
    opening, _, mix, _ = tables
    _, lanes, length = filters.shape
    outer = length // INNER
    return pl.pallas_call(
        filters_body,
        grid=(2,),
        in_specs=[
            pl.BlockSpec(opening.shape, lambda i: (0, 0)),
            ANY,
            pl.BlockSpec((1, lanes, length), lambda i: (i, 0, 0)),
        ],
        out_specs=pl.BlockSpec((1,) + spectrum(outer, lanes), lambda i: (i, 0, 0, 0)),
        out_shape=jax.ShapeDtypeStruct((2,) + spectrum(outer, lanes), BF16),
        scratch_shapes=[
            pltpu.VMEM((2 * outer, INNER, lanes), F32),
            pltpu.VMEM((outer, INNER, lanes), F32),
            table_buffer(outer),
            pltpu.SemaphoreType.DMA((1, outer // SIDE)),
        ],
        compiler_params=params,
        cost_estimate=cost(24),
        name="filter_spectra",
    )(opening, mix, filters)


def conv_pass(name, body, which, tables, gain, filt, signals, kinds, mids=0):
    opening, closing, mix, unmix = tables
    outer, inner, lanes = signals[0].shape
    shape = (outer, inner, lanes)
    spec = spectrum(outer, lanes)
    return pl.pallas_call(
        functools.partial(body, which),
        in_specs=[VMEM] * (3 + len(signals)) + [ANY] * 3,
        out_specs=[VMEM] * (1 + len(kinds)),
        out_shape=[jax.ShapeDtypeStruct(spec, BF16)] + [jax.ShapeDtypeStruct(shape, kind) for kind in kinds],
        scratch_shapes=[pltpu.VMEM((2 * outer, inner, lanes), F32)]
        + [pltpu.VMEM(shape, F32)] * mids
        + [table_buffer(outer), table_buffer(outer), pltpu.VMEM(spec, BF16)]
        + [pltpu.SemaphoreType.DMA((3, outer // SIDE))],
        compiler_params=params,
        cost_estimate=cost(20),
        name=name,
    )(opening, closing, gain, *signals, mix, unmix, filt)


def grad_pass(name, which, scale, tables, left, right, prior=None):
    _, closing, _, unmix = tables
    outer, _, lanes = left.shape
    length = outer * INNER
    priors = [] if prior is None else [prior]
    return pl.pallas_call(
        functools.partial(grad_body, scale, len(priors)),
        grid=(1,),
        in_specs=[pl.BlockSpec(closing.shape, lambda i: (0, 0)), ANY, ANY, ANY] + [ANY] * len(priors),
        out_specs=pl.BlockSpec((1, lanes, length), lambda i: (which, 0, 0)),
        out_shape=jax.ShapeDtypeStruct((2, lanes, length), F32),
        input_output_aliases={4: 0} if priors else {},
        scratch_shapes=[
            pltpu.VMEM((2 * outer, INNER, lanes), F32),
            pltpu.VMEM((outer, INNER, lanes), F32),
            table_buffer(outer),
            pltpu.VMEM(left.shape, BF16),
            pltpu.VMEM(left.shape, BF16),
            pltpu.SemaphoreType.DMA((3, outer // SIDE)),
        ],
        compiler_params=params,
        cost_estimate=cost(15),
        name=name,
    )(closing, unmix, left, right, *priors)


def copy_body(*refs):
    half = len(refs) // 2
    for source, target in zip(refs[:half], refs[half:]):
        target[...] = source[...].reshape(target.shape)


def split_width(block, count, at):
    _, frames, local_width = block.shape
    width = local_width // count
    if width % 128:
        return jnp.swapaxes(block[at].reshape(frames, count, width), 0, 1)
    return pl.pallas_call(
        copy_body,
        grid=(count,),
        in_specs=[pl.BlockSpec((1, frames, width), lambda i: (at, 0, i))],
        out_specs=pl.BlockSpec((1, frames, width), lambda i: (i, 0, 0)),
        out_shape=jax.ShapeDtypeStruct((count, frames, width), block.dtype),
        compiler_params=params,
        cost_estimate=cost(2),
        name="split_width",
    )(block)


def join_body(a, b, c, out):
    out[0] = a[0]
    out[1] = b[0]
    out[2] = c[0]


def join_width(blocks):
    count, frames, width = blocks[0].shape
    if width % 128:
        return jnp.stack([jnp.swapaxes(b, 0, 1).reshape(frames, count * width) for b in blocks])
    return pl.pallas_call(
        join_body,
        grid=(count,),
        in_specs=[pl.BlockSpec((1, frames, width), lambda i: (i, 0, 0))] * 3,
        out_specs=pl.BlockSpec((3, frames, width), lambda i: (0, 0, i)),
        out_shape=jax.ShapeDtypeStruct((3, frames, count * width), BF16),
        compiler_params=params,
        cost_estimate=cost(5),
        name="join_width",
    )(*blocks)


def swap(block):
    return lax.all_to_all(block, "seq", split_axis=0, concat_axis=0, tiled=True)


def to_frames(block):
    count = lax.axis_size("seq")
    length, width = block.shape
    return swap(block.reshape(count, length // count, width))


def short_filter(block, taps):
    wide = jnp.pad(block.astype(F32), ((2, 0), (0, 0)))
    length = block.shape[0]
    return sum(taps[j][None] * wide[2 - j : 2 - j + length] for j in range(3)).astype(BF16)


def short_filter_back(block, taps):
    wide = jnp.pad(block.astype(F32), ((0, 2), (0, 0)))
    length = block.shape[0]
    return sum(taps[j][None] * wide[j : j + length] for j in range(3)).astype(BF16)


def local(projected, short_kernel, filters, skip_gain, out_weight, out_grad):
    _, frames, _, local_width = projected.shape
    _, width, length = filters.shape
    count = lax.axis_size("seq")
    outer = length // INNER
    grid3 = (outer, INNER, width)
    scale = float(length) ** -0.5
    mine = lax.axis_index("seq") * width
    taps = lax.dynamic_slice_in_dim(short_kernel, mine, width, axis=2)
    tables = transform_tables(outer)

    branches = jnp.transpose(projected[0], (1, 0, 2))
    raw = [swap(split_width(branches, count, s)).reshape(length, width) for s in range(3)]
    gathered = lax.all_gather(out_grad[0], "tp", axis=1, tiled=True)

    filt = filter_spectra(tables, filters)
    v, x1, x2 = [short_filter(raw[s], taps[s]).reshape(grid3) for s in range(3)]
    spec_v, first = conv_pass("first", first_body, 0, tables, skip_gain, filt, [v], [F32])
    spec_m, second = conv_pass("second", second_body, 1, tables, skip_gain, filt, [first, x1], [BF16], mids=1)
    gated = (x2.astype(F32) * second.astype(F32)).astype(BF16)
    moved_gated = to_frames(gated.reshape(length, width))

    back_gated = lax.dot_general(
        gathered, out_weight, (((1,), (1,)), ((), ())), preferred_element_type=F32
    ).astype(BF16)
    bg = swap(split_width(back_gated[None], count, 0)).reshape(grid3).astype(F32)

    flat_gated = jnp.swapaxes(moved_gated, 0, 1).reshape(frames, local_width)
    summed = lax.psum_scatter(
        lax.dot_general(
            out_weight, flat_gated, (((0,), (1,)), ((), ())), preferred_element_type=F32
        ).astype(BF16),
        "tp",
        scatter_dimension=0,
        tiled=True,
    )
    output = jnp.transpose(summed)[None]

    bs = (bg * x2.astype(F32)).astype(BF16)
    bx2 = (bg * second.astype(F32)).astype(BF16)
    moved2 = to_frames(short_filter_back(bx2.reshape(length, width), taps[2]))
    spec_b, bf, bx1 = conv_pass("back_second", back_second_body, 1, tables, skip_gain, filt, [bs, first, x1], [F32, BF16])
    moved1 = to_frames(short_filter_back(bx1.reshape(length, width), taps[1]))
    spec_c, bv = conv_pass("back_first", back_first_body, 0, tables, skip_gain, filt, [bf], [BF16])
    moved0 = to_frames(short_filter_back(bv.reshape(length, width), taps[0]))
    grad = grad_pass("grad_second", 1, scale, tables, spec_m, spec_b)
    filter_grad = grad_pass("grad_first", 0, scale, tables, spec_v, spec_c, grad)

    projected_grad = jnp.transpose(join_width([moved0, moved1, moved2]), (1, 0, 2))[None]
    return (output, projected_grad, filter_grad)


def solution(mesh):
    in_specs = (
        P(None, "seq", None, "tp"),
        P(None, None, "tp"),
        P(None, ("tp", "seq"), None),
        P(None, ("tp", "seq")),
        P("tp", None),
        P(None, "seq", "tp"),
    )
    out_specs = (P(None, "seq", "tp"), P(None, "seq", None, "tp"), P(None, ("tp", "seq"), None))
    return jax.shard_map(local, mesh=mesh, in_specs=in_specs, out_specs=out_specs, check_vma=False)
```

```python
import functools
import math

import jax
import jax.numpy as jnp
import ml_dtypes
import numpy as np
from jax import lax
from jax.experimental import pallas as pl
from jax.experimental.pallas import tpu as pltpu
from jax.sharding import PartitionSpec as P

F32 = jnp.float32
BF16 = jnp.bfloat16
INNER = 128
SUB = 8
ROWS = 16
SIDE = 8


def spread_table(outer, scale):
    freq = np.arange(2 * outer * SUB)[:, None]
    time = np.arange(outer * SUB)[None, :]
    row = freq // SUB
    turn = 4 * outer
    phase = (4 * (row % outer) + 1) * (time // SUB) + outer * (row // outer)
    value = np.cos((phase % turn) * (2.0 * math.pi / turn)) * scale
    return np.where(freq % SUB == time % SUB, value, 0.0)


def transform_tables(outer):
    total = outer * INNER
    ids = np.arange(INNER)
    twist = 2.0 * math.pi * (np.arange(outer)[:, None] + 0.25) * ids[None, :] / total
    inner = 2.0 * math.pi * (ids[:, None] * ids[None, :] % INNER) / INNER
    angle = twist[:, None, :] + inner[None]
    cos, sin = np.cos(angle), np.sin(angle)
    mix = np.concatenate(
        [np.concatenate([cos, sin], axis=2), np.concatenate([-sin, cos], axis=2)], axis=1
    )
    opening = spread_table(outer, 1.0)
    closing = spread_table(outer, 1.0 / total).T
    unmix = np.swapaxes(mix, 1, 2)
    return [jnp.asarray(np.ascontiguousarray(t).astype(ml_dtypes.bfloat16)) for t in (opening, closing, mix, unmix)]


def mul(a, b):
    return jnp.dot(a, b, preferred_element_type=F32)


def halves(spec):
    return spec[:INNER].astype(F32), spec[INNER:].astype(F32)


def cmul(a, b):
    (ar, ai), (br, bi) = a, b
    return ar * br - ai * bi, ar * bi + ai * br


def conj_mul(a, b):
    (ar, ai), (br, bi) = a, b
    return ar * br + ai * bi, ar * bi - ai * br


def packed(pair):
    return jnp.concatenate(pair, axis=0).astype(BF16)


def open_phase(opening, read, spec):
    twice, inner, lanes = spec.shape
    outer = twice // 2

    def step(at, carry):
        row = pl.multiple_of(at * ROWS, ROWS)
        signal = read(row)
        wide = jnp.concatenate([signal[:, :SUB], signal[:, SUB:]], axis=2)
        flat = wide.reshape(outer * SUB, 2 * lanes).astype(BF16)
        out = mul(opening[...], flat).reshape(twice, SUB, 2 * lanes)
        spec[:, pl.ds(row, SUB), :] = out[:, :, :lanes]
        spec[:, pl.ds(row + SUB, SUB), :] = out[:, :, lanes:]
        return carry

    lax.fori_loop(0, inner // ROWS, step, 0)


def close_phase(closing, spec, write):
    twice, inner, lanes = spec.shape
    outer = twice // 2

    def step(at, carry):
        row = pl.multiple_of(at * ROWS, ROWS)
        wide = jnp.concatenate([spec[:, pl.ds(row, SUB), :], spec[:, pl.ds(row + SUB, SUB), :]], axis=2)
        flat = wide.reshape(twice * SUB, 2 * lanes).astype(BF16)
        out = mul(closing[...], flat).reshape(outer, SUB, 2 * lanes)
        write(row, jnp.concatenate([out[:, :, :lanes], out[:, :, lanes:]], axis=1))
        return carry

    lax.fori_loop(0, inner // ROWS, step, 0)


def side_loop(outer, waits, body):
    def step(at, carry):
        for wait in waits:
            wait(at)
        base = pl.multiple_of(at * SIDE, SIDE)
        body([base + i for i in range(SIDE)])
        return carry

    lax.fori_loop(0, outer // SIDE, step, 0)


def fetch(sources, buffers, sems):
    outer = buffers[0].shape[0]

    def piece(which, at):
        rows = pl.ds(at * SIDE, SIDE)
        return pltpu.make_async_copy(sources[which].at[rows], buffers[which].at[rows], sems.at[which, at])

    for at in range(outer // SIDE):
        for which in range(len(sources)):
            piece(which, at).start()
    return [lambda at, which=which: piece(which, at).wait() for which in range(len(sources))]


def columns(spec, ids):
    outer = spec.shape[0] // 2
    return [packed([spec[i], spec[outer + i]]) for i in ids]


def put_columns(spec, ids, values):
    outer = spec.shape[0] // 2
    for i, value in zip(ids, values):
        spec[i] = value[:INNER]
        spec[outer + i] = value[INNER:]


def short_phase(raw, taps, out):
    outer, inner, lanes = raw.shape

    def step(p, before):
        now = raw[p].astype(F32)
        wide = jnp.concatenate([before, now], axis=0)
        total = taps[0:1, :] * now
        for j in (1, 2):
            total = total + taps[j : j + 1, :] * wide[SUB - j : SUB - j + inner]
        out[p] = total.astype(BF16)
        return now[inner - SUB :]

    lax.fori_loop(0, outer, step, jnp.zeros((SUB, lanes), F32))


def short_back_phase(raw, taps, out):
    outer, inner, lanes = raw.shape

    def step(at, after):
        p = outer - 1 - at
        now = raw[p].astype(F32)
        wide = jnp.concatenate([now, after], axis=0)
        total = taps[0:1, :] * now
        for j in (1, 2):
            total = total + taps[j : j + 1, :] * wide[j : j + inner]
        out[p] = total.astype(BF16)
        return now[:SUB]

    lax.fori_loop(0, outer, step, jnp.zeros((SUB, lanes), F32))


def filters_body(opening, mix_hbm, filt, out, spec, sig, mix, sems):
    waits = fetch([mix_hbm], [mix], sems)
    outer = sig.shape[0]

    def turn(p, carry):
        sig[p] = jnp.transpose(filt[0, :, pl.ds(pl.multiple_of(p * INNER, INNER), INNER)])
        return carry

    lax.fori_loop(0, outer, turn, 0)
    open_phase(opening, lambda row: sig[:, pl.ds(row, ROWS), :], spec)

    def body(ids):
        results = [mul(mix[i], col) for i, col in zip(ids, columns(spec, ids))]
        for i, value in zip(ids, results):
            out[0, i] = value.astype(BF16)

    side_loop(outer, waits, body)


def conv_phase(spec, filt, mix, unmix, waits, kept, product):
    def body(ids):
        seen = [mul(mix[i], col) for i, col in zip(ids, columns(spec, ids))]
        mixed = [packed(product(halves(filt[i]), halves(x))) for i, x in zip(ids, seen)]
        done = [mul(unmix[i], y) for i, y in zip(ids, mixed)]
        for i, x in zip(ids, seen):
            kept[i] = x.astype(BF16)
        put_columns(spec, ids, done)

    side_loop(filt.shape[0], waits, body)


def first_body(
    which, opening, closing, gain, taps, raw, mix_hbm, unmix_hbm, filt_hbm, kept, first, spec, v, mix, unmix, filt, sems
):
    waits = fetch([mix_hbm, unmix_hbm, filt_hbm.at[which]], [mix, unmix, filt], sems)
    short_phase(raw, taps, v)
    open_phase(opening, lambda row: v[:, pl.ds(row, ROWS), :].astype(F32), spec)
    conv_phase(spec, filt, mix, unmix, waits, kept, cmul)
    g0 = gain[0:1, :][None]

    def write(row, value):
        rows = pl.ds(row, ROWS)
        first[:, rows, :] = g0 * v[:, rows, :].astype(F32) + value

    close_phase(closing, spec, write)


def second_body(
    which, opening, closing, gain, taps, first, raw, mix_hbm, unmix_hbm, filt_hbm,
    kept, second, x1, spec, mid, mix, unmix, filt, sems
):
    waits = fetch([mix_hbm, unmix_hbm, filt_hbm.at[which]], [mix, unmix, filt], sems)
    short_phase(raw, taps, x1)

    def read(row):
        rows = pl.ds(row, ROWS)
        value = x1[:, rows, :].astype(F32) * first[:, rows, :]
        mid[:, rows, :] = value
        return value

    open_phase(opening, read, spec)
    conv_phase(spec, filt, mix, unmix, waits, kept, cmul)
    g1 = gain[1:2, :][None]

    def write(row, value):
        rows = pl.ds(row, ROWS)
        second[:, rows, :] = (g1 * mid[:, rows, :] + value).astype(BF16)

    close_phase(closing, spec, write)


def back_second_body(
    which, opening, closing, gain, taps, bs, first, x1, mix_hbm, unmix_hbm, filt_hbm,
    kept, bf, grad_x1, spec, bx1, mix, unmix, filt, sems
):
    waits = fetch([mix_hbm, unmix_hbm, filt_hbm.at[which]], [mix, unmix, filt], sems)
    open_phase(opening, lambda row: bs[:, pl.ds(row, ROWS), :].astype(F32), spec)
    conv_phase(spec, filt, mix, unmix, waits, kept, conj_mul)
    g1 = gain[1:2, :][None]

    def write(row, value):
        rows = pl.ds(row, ROWS)
        back_middle = g1 * bs[:, rows, :].astype(F32) + value
        bf[:, rows, :] = back_middle * x1[:, rows, :].astype(F32)
        bx1[:, rows, :] = (back_middle * first[:, rows, :]).astype(BF16)

    close_phase(closing, spec, write)
    short_back_phase(bx1, taps, grad_x1)


def back_first_body(
    which, opening, closing, gain, taps, bf, mix_hbm, unmix_hbm, filt_hbm, kept, grad_v, spec, bv, mix, unmix, filt, sems
):
    waits = fetch([mix_hbm, unmix_hbm, filt_hbm.at[which]], [mix, unmix, filt], sems)
    open_phase(opening, lambda row: bf[:, pl.ds(row, ROWS), :], spec)
    conv_phase(spec, filt, mix, unmix, waits, kept, conj_mul)
    g0 = gain[0:1, :][None]

    def write(row, value):
        rows = pl.ds(row, ROWS)
        bv[:, rows, :] = (g0 * bf[:, rows, :] + value).astype(BF16)

    close_phase(closing, spec, write)
    short_back_phase(bv, taps, grad_v)


def grad_body(scale, has_prior, closing, unmix_hbm, left_hbm, right_hbm, *refs):
    out, spec, closed, unmix, left, right, sems = refs[has_prior:]
    waits = fetch([unmix_hbm, left_hbm, right_hbm], [unmix, left, right], sems)
    outer = closed.shape[0]

    def body(ids):
        mixed = [packed(conj_mul(halves(left[i]), halves(right[i]))) for i in ids]
        put_columns(spec, ids, [mul(unmix[i], y) for i, y in zip(ids, mixed)])

    side_loop(outer, waits, body)

    def write(row, value):
        closed[:, pl.ds(row, ROWS), :] = value * scale

    close_phase(closing, spec, write)

    def turn(p, carry):
        out[0, :, pl.ds(pl.multiple_of(p * INNER, INNER), INNER)] = jnp.transpose(closed[p])
        return carry

    lax.fori_loop(0, outer, turn, 0)


params = pltpu.CompilerParams(vmem_limit_bytes=58 << 20)
VMEM = pl.BlockSpec(memory_space=pltpu.VMEM)
ANY = pl.BlockSpec(memory_space=pl.ANY)


def table_buffer(outer):
    return pltpu.VMEM((outer, 2 * INNER, 2 * INNER), BF16)


def spectrum(outer, lanes):
    return (outer, 2 * INNER, lanes)


def cost(us):
    return pl.CostEstimate(flops=int(us * 0.8e9), bytes_accessed=int(us * 2e6), transcendentals=0)


def filter_spectra(tables, filters):
    opening, _, mix, _ = tables
    _, lanes, length = filters.shape
    outer = length // INNER
    return pl.pallas_call(
        filters_body,
        grid=(2,),
        in_specs=[
            pl.BlockSpec(opening.shape, lambda i: (0, 0)),
            ANY,
            pl.BlockSpec((1, lanes, length), lambda i: (i, 0, 0)),
        ],
        out_specs=pl.BlockSpec((1,) + spectrum(outer, lanes), lambda i: (i, 0, 0, 0)),
        out_shape=jax.ShapeDtypeStruct((2,) + spectrum(outer, lanes), BF16),
        scratch_shapes=[
            pltpu.VMEM((2 * outer, INNER, lanes), F32),
            pltpu.VMEM((outer, INNER, lanes), F32),
            table_buffer(outer),
            pltpu.SemaphoreType.DMA((1, outer // SIDE)),
        ],
        compiler_params=params,
        cost_estimate=cost(24),
        name="filter_spectra",
    )(opening, mix, filters)


def conv_pass(name, body, which, tables, gain, taps, filt, signals, kinds, hold):
    opening, closing, mix, unmix = tables
    outer, inner, lanes = signals[0].shape
    shape = (outer, inner, lanes)
    spec = spectrum(outer, lanes)
    return pl.pallas_call(
        functools.partial(body, which),
        in_specs=[VMEM] * (4 + len(signals)) + [ANY] * 3,
        out_specs=[VMEM] * (1 + len(kinds)),
        out_shape=[jax.ShapeDtypeStruct(spec, BF16)] + [jax.ShapeDtypeStruct(shape, kind) for kind in kinds],
        scratch_shapes=[pltpu.VMEM((2 * outer, inner, lanes), F32)]
        + [pltpu.VMEM(shape, hold)]
        + [table_buffer(outer), table_buffer(outer), pltpu.VMEM(spec, BF16)]
        + [pltpu.SemaphoreType.DMA((3, outer // SIDE))],
        compiler_params=params,
        cost_estimate=cost(20),
        name=name,
    )(opening, closing, gain, taps, *signals, mix, unmix, filt)


def grad_pass(name, which, scale, tables, left, right, prior=None):
    _, closing, _, unmix = tables
    outer, _, lanes = left.shape
    length = outer * INNER
    priors = [] if prior is None else [prior]
    return pl.pallas_call(
        functools.partial(grad_body, scale, len(priors)),
        grid=(1,),
        in_specs=[pl.BlockSpec(closing.shape, lambda i: (0, 0)), ANY, ANY, ANY] + [ANY] * len(priors),
        out_specs=pl.BlockSpec((1, lanes, length), lambda i: (which, 0, 0)),
        out_shape=jax.ShapeDtypeStruct((2, lanes, length), F32),
        input_output_aliases={4: 0} if priors else {},
        scratch_shapes=[
            pltpu.VMEM((2 * outer, INNER, lanes), F32),
            pltpu.VMEM((outer, INNER, lanes), F32),
            table_buffer(outer),
            pltpu.VMEM(left.shape, BF16),
            pltpu.VMEM(left.shape, BF16),
            pltpu.SemaphoreType.DMA((3, outer // SIDE)),
        ],
        compiler_params=params,
        cost_estimate=cost(15),
        name=name,
    )(closing, unmix, left, right, *priors)


def split_body(source, target):
    count, _, width = target.shape
    for i in range(count):
        target[i] = source[0, :, i * width : (i + 1) * width]


def rows_of(frames):
    return min(frames, 256)


def flat_width(block):
    count, frames, width = block.shape
    return jnp.swapaxes(block, 0, 1).reshape(frames, count * width)


def split_flat(block, count):
    frames, local_width = block.shape
    return jnp.swapaxes(block.reshape(frames, count, local_width // count), 0, 1)


def split_width(block, count, at):
    _, frames, local_width = block.shape
    width = local_width // count
    if width % 128:
        return split_flat(block[at], count)
    rows = rows_of(frames)
    return pl.pallas_call(
        split_body,
        grid=(frames // rows,),
        in_specs=[pl.BlockSpec((1, rows, local_width), lambda i: (at, i, 0))],
        out_specs=pl.BlockSpec((count, rows, width), lambda i: (0, i, 0)),
        out_shape=jax.ShapeDtypeStruct((count, frames, width), block.dtype),
        compiler_params=params,
        cost_estimate=cost(2),
        name="split_width",
    )(block)


def join_body(a, b, c, out):
    count, _, width = a.shape
    for i in range(count):
        lanes = slice(i * width, (i + 1) * width)
        out[0, :, lanes] = a[i]
        out[1, :, lanes] = b[i]
    out[2] = c[...]


def join_width(a, b, flat):
    count, frames, width = a.shape
    if width % 128:
        return jnp.stack([flat_width(a), flat_width(b), flat])
    rows = rows_of(frames)
    split = pl.BlockSpec((count, rows, width), lambda i: (0, i, 0))
    return pl.pallas_call(
        join_body,
        grid=(frames // rows,),
        in_specs=[split, split, pl.BlockSpec((rows, count * width), lambda i: (i, 0))],
        out_specs=pl.BlockSpec((3, rows, count * width), lambda i: (0, i, 0)),
        out_shape=jax.ShapeDtypeStruct((3, frames, count * width), BF16),
        compiler_params=params,
        cost_estimate=cost(5),
        name="join_width",
    )(a, b, flat)


def output_body(second, x2, weight, out, gated):
    count, frames, width = second.shape
    rows = rows_of(frames)

    @pl.when(pl.program_id(0) == 0)
    def _():
        for i in range(count):
            lanes = slice(i * width, (i + 1) * width)
            gated[:, lanes] = (x2[:, lanes].astype(F32) * second[i].astype(F32)).astype(BF16)

    def step(at, carry):
        here = pl.ds(pl.multiple_of(at * rows, rows), rows)
        out[here, :] = mul(gated[here, :], weight[...]).astype(BF16)
        return carry

    lax.fori_loop(0, frames // rows, step, 0)


def output_partial(second, x2, weight):
    count, frames, width = second.shape
    local_width, model = weight.shape
    if width % 128:
        gated = (x2.astype(F32) * flat_width(second).astype(F32)).astype(BF16)
        return mul(gated, weight).astype(BF16)
    cols = 512
    return pl.pallas_call(
        output_body,
        grid=(model // cols,),
        in_specs=[
            pl.BlockSpec(second.shape, lambda i: (0, 0, 0)),
            pl.BlockSpec(x2.shape, lambda i: (0, 0)),
            pl.BlockSpec((local_width, cols), lambda i: (0, i)),
        ],
        out_specs=pl.BlockSpec((frames, cols), lambda i: (0, i)),
        out_shape=jax.ShapeDtypeStruct((frames, model), BF16),
        scratch_shapes=[pltpu.VMEM((frames, local_width), BF16)],
        compiler_params=params,
        cost_estimate=cost(12),
        name="output_partial",
    )(second, x2, weight)


def back_gate_body(gathered, weight, x2, second, bs, bx2):
    pairs, frames, width = second.shape
    rows = min(frames, 512)

    def step(at, carry):
        here = pl.ds(pl.multiple_of(at * rows, rows), rows)
        full = lax.dot_general(
            gathered[here, :], weight[...], (((1,), (1,)), ((), ())), preferred_element_type=F32
        )
        full = full.astype(BF16).astype(F32)
        for i in range(pairs):
            lanes = slice(i * width, (i + 1) * width)
            bs[i, here, :] = (full[:, lanes] * x2[here, lanes].astype(F32)).astype(BF16)
            bx2[here, lanes] = (full[:, lanes] * second[i, here, :].astype(F32)).astype(BF16)
        return carry

    lax.fori_loop(0, frames // rows, step, 0)


def back_gate(gathered, weight, x2, second):
    count, frames, width = second.shape
    local_width, model = weight.shape
    if width % 128:
        full = lax.dot_general(gathered, weight, (((1,), (1,)), ((), ())), preferred_element_type=F32)
        full = full.astype(BF16).astype(F32)
        bs = split_flat((full * x2.astype(F32)).astype(BF16), count)
        return bs, (full * flat_width(second).astype(F32)).astype(BF16)
    pairs = 2
    wide = pairs * width
    flat = pl.BlockSpec((frames, wide), lambda i: (0, i))
    split = pl.BlockSpec((pairs, frames, width), lambda i: (i, 0, 0))
    return pl.pallas_call(
        back_gate_body,
        grid=(count // pairs,),
        in_specs=[
            pl.BlockSpec(gathered.shape, lambda i: (0, 0)),
            pl.BlockSpec((wide, model), lambda i: (i, 0)),
            flat,
            split,
        ],
        out_specs=[split, flat],
        out_shape=[
            jax.ShapeDtypeStruct((count, frames, width), BF16),
            jax.ShapeDtypeStruct((frames, local_width), BF16),
        ],
        compiler_params=params,
        cost_estimate=cost(14),
        name="back_gate",
    )(gathered, weight, x2, second)


def swap(block):
    return lax.all_to_all(block, "seq", split_axis=0, concat_axis=0, tiled=True)


def to_frames(block):
    count = lax.axis_size("seq")
    length, width = block.shape
    return swap(block.reshape(count, length // count, width))


def neighbour_rows(rows, shift):
    count = lax.axis_size("seq")
    pairs = [(i, i + shift) for i in range(count) if 0 <= i + shift < count]
    return lax.ppermute(rows, "seq", pairs)


def short_filter(block, taps):
    length = block.shape[0]
    before = neighbour_rows(block[length - 2 :], 1)
    wide = jnp.concatenate([before, block], axis=0).astype(F32)
    return sum(taps[j][None] * wide[2 - j : 2 - j + length] for j in range(3)).astype(BF16)


def short_filter_back(block, taps):
    length = block.shape[0]
    after = neighbour_rows(block[:2], -1)
    wide = jnp.concatenate([block, after], axis=0).astype(F32)
    return sum(taps[j][None] * wide[j : j + length] for j in range(3)).astype(BF16)


def local(projected, short_kernel, filters, skip_gain, out_weight, out_grad):
    _, frames, _, local_width = projected.shape
    _, width, length = filters.shape
    count = lax.axis_size("seq")
    outer = length // INNER
    grid3 = (outer, INNER, width)
    scale = float(length) ** -0.5
    mine = lax.axis_index("seq") * width
    taps = lax.dynamic_slice_in_dim(short_kernel, mine, width, axis=2)
    tables = transform_tables(outer)

    branches = jnp.transpose(projected[0], (1, 0, 2))
    raw_v, raw_x1 = [swap(split_width(branches, count, s)).reshape(grid3) for s in range(2)]
    gathered = lax.all_gather(out_grad[0], "tp", axis=1, tiled=True)
    filt = filter_spectra(tables, filters)
    x2 = short_filter(branches[2], short_kernel[2])

    spec_v, first = conv_pass("first", first_body, 0, tables, skip_gain, taps[0], filt, [raw_v], [F32], BF16)
    raw_x1, first = lax.optimization_barrier((raw_x1, first))
    spec_m, second, x1 = conv_pass(
        "second", second_body, 1, tables, skip_gain, taps[1], filt, [first, raw_x1], [BF16, BF16], F32
    )
    second = to_frames(second.reshape(length, width))
    partial = output_partial(second, x2, out_weight)
    output = lax.psum_scatter(partial, "tp", scatter_dimension=1, tiled=True)[None]

    gathered, _ = lax.optimization_barrier((gathered, partial))
    bs, bx2 = back_gate(gathered, out_weight, x2, second)
    bs = swap(bs).reshape(grid3)
    grad_x2 = short_filter_back(bx2, short_kernel[2])
    spec_b, bf, grad_x1 = conv_pass(
        "back_second", back_second_body, 1, tables, skip_gain, taps[1], filt, [bs, first, x1], [F32, BF16], BF16
    )
    moved1 = to_frames(grad_x1.reshape(length, width))
    spec_c, grad_v = conv_pass(
        "back_first", back_first_body, 0, tables, skip_gain, taps[0], filt, [bf], [BF16], BF16
    )
    moved0 = to_frames(grad_v.reshape(length, width))
    grad = grad_pass("grad_second", 1, scale, tables, spec_m, spec_b)
    filter_grad = grad_pass("grad_first", 0, scale, tables, spec_v, spec_c, grad)

    projected_grad = jnp.transpose(join_width(moved0, moved1, grad_x2), (1, 0, 2))[None]
    return (output, projected_grad, filter_grad)


def solution(mesh):
    in_specs = (
        P(None, "seq", None, "tp"),
        P(None, None, "tp"),
        P(None, ("tp", "seq"), None),
        P(None, ("tp", "seq")),
        P("tp", None),
        P(None, "seq", "tp"),
    )
    out_specs = (P(None, "seq", "tp"), P(None, "seq", None, "tp"), P(None, ("tp", "seq"), None))
    return jax.shard_map(local, mesh=mesh, in_specs=in_specs, out_specs=out_specs, check_vma=False)
```

```python
import functools
import math

import jax
import jax.numpy as jnp
import ml_dtypes
import numpy as np
from jax import lax
from jax.experimental import pallas as pl
from jax.experimental.pallas import tpu as pltpu
from jax.sharding import PartitionSpec as P

F32 = jnp.float32
BF16 = jnp.bfloat16
INNER = 128
SUB = 8
ROWS = 16
SIDE = 8
N_TP = 4


def spread_table(outer, scale):
    freq = np.arange(2 * outer * SUB)[:, None]
    time = np.arange(outer * SUB)[None, :]
    row = freq // SUB
    turn = 4 * outer
    phase = (4 * (row % outer) + 1) * (time // SUB) + outer * (row // outer)
    value = np.cos((phase % turn) * (2.0 * math.pi / turn)) * scale
    return np.where(freq % SUB == time % SUB, value, 0.0)


def transform_tables(outer):
    total = outer * INNER
    ids = np.arange(INNER)
    twist = 2.0 * math.pi * (np.arange(outer)[:, None] + 0.25) * ids[None, :] / total
    inner = 2.0 * math.pi * (ids[:, None] * ids[None, :] % INNER) / INNER
    angle = twist[:, None, :] + inner[None]
    cos, sin = np.cos(angle), np.sin(angle)
    mix = np.concatenate(
        [np.concatenate([cos, sin], axis=2), np.concatenate([-sin, cos], axis=2)], axis=1
    )
    opening = spread_table(outer, 1.0)
    closing = spread_table(outer, 1.0 / total).T
    unmix = np.swapaxes(mix, 1, 2)
    return [jnp.asarray(np.ascontiguousarray(t).astype(ml_dtypes.bfloat16)) for t in (opening, closing, mix, unmix)]


def mul(a, b):
    return jnp.dot(a, b, preferred_element_type=F32)


def halves(spec):
    return spec[:INNER].astype(F32), spec[INNER:].astype(F32)


def cmul(a, b):
    (ar, ai), (br, bi) = a, b
    return ar * br - ai * bi, ar * bi + ai * br


def conj_mul(a, b):
    (ar, ai), (br, bi) = a, b
    return ar * br + ai * bi, ar * bi - ai * br


def packed(pair):
    return jnp.concatenate(pair, axis=0).astype(BF16)


def open_phase(opening, read, spec):
    twice, inner, lanes = spec.shape
    outer = twice // 2

    def step(at, carry):
        row = pl.multiple_of(at * ROWS, ROWS)
        signal = read(row)
        wide = jnp.concatenate([signal[:, :SUB], signal[:, SUB:]], axis=2)
        flat = wide.reshape(outer * SUB, 2 * lanes).astype(BF16)
        out = mul(opening[...], flat).reshape(twice, SUB, 2 * lanes)
        spec[:, pl.ds(row, SUB), :] = out[:, :, :lanes]
        spec[:, pl.ds(row + SUB, SUB), :] = out[:, :, lanes:]
        return carry

    lax.fori_loop(0, inner // ROWS, step, 0)


def close_phase(closing, spec, write):
    twice, inner, lanes = spec.shape
    outer = twice // 2

    def step(at, carry):
        row = pl.multiple_of(at * ROWS, ROWS)
        wide = jnp.concatenate([spec[:, pl.ds(row, SUB), :], spec[:, pl.ds(row + SUB, SUB), :]], axis=2)
        flat = wide.reshape(twice * SUB, 2 * lanes).astype(BF16)
        out = mul(closing[...], flat).reshape(outer, SUB, 2 * lanes)
        write(row, jnp.concatenate([out[:, :, :lanes], out[:, :, lanes:]], axis=1))
        return carry

    lax.fori_loop(0, inner // ROWS, step, 0)


def side_loop(outer, waits, body):
    def step(at, carry):
        for wait in waits:
            wait(at)
        base = pl.multiple_of(at * SIDE, SIDE)
        body([base + i for i in range(SIDE)])
        return carry

    lax.fori_loop(0, outer // SIDE, step, 0)


def fetch(sources, buffers, sems):
    outer = buffers[0].shape[0]

    def piece(which, at):
        rows = pl.ds(at * SIDE, SIDE)
        return pltpu.make_async_copy(sources[which].at[rows], buffers[which].at[rows], sems.at[which, at])

    for at in range(outer // SIDE):
        for which in range(len(sources)):
            piece(which, at).start()
    return [lambda at, which=which: piece(which, at).wait() for which in range(len(sources))]


def columns(spec, ids):
    outer = spec.shape[0] // 2
    return [packed([spec[i], spec[outer + i]]) for i in ids]


def put_columns(spec, ids, values):
    outer = spec.shape[0] // 2
    for i, value in zip(ids, values):
        spec[i] = value[:INNER]
        spec[outer + i] = value[INNER:]


def short_phase(raw, taps, out):
    outer, inner, lanes = raw.shape

    def step(p, before):
        now = raw[p].astype(F32)
        wide = jnp.concatenate([before, now], axis=0)
        total = taps[0:1, :] * now
        for j in (1, 2):
            total = total + taps[j : j + 1, :] * wide[SUB - j : SUB - j + inner]
        out[p] = total.astype(BF16)
        return now[inner - SUB :]

    lax.fori_loop(0, outer, step, jnp.zeros((SUB, lanes), F32))


def short_back_phase(raw, taps, out):
    outer, inner, lanes = raw.shape

    def step(at, after):
        p = outer - 1 - at
        now = raw[p].astype(F32)
        wide = jnp.concatenate([now, after], axis=0)
        total = taps[0:1, :] * now
        for j in (1, 2):
            total = total + taps[j : j + 1, :] * wide[j : j + inner]
        out[p] = total.astype(BF16)
        return now[:SUB]

    lax.fori_loop(0, outer, step, jnp.zeros((SUB, lanes), F32))


def filters_body(opening, mix_hbm, filt, out, spec, sig, mix, sems):
    waits = fetch([mix_hbm], [mix], sems)
    outer = sig.shape[0]

    def turn(p, carry):
        sig[p] = jnp.transpose(filt[0, :, pl.ds(pl.multiple_of(p * INNER, INNER), INNER)])
        return carry

    lax.fori_loop(0, outer, turn, 0)
    open_phase(opening, lambda row: sig[:, pl.ds(row, ROWS), :], spec)

    def body(ids):
        results = [mul(mix[i], col) for i, col in zip(ids, columns(spec, ids))]
        for i, value in zip(ids, results):
            out[0, i] = value.astype(BF16)

    side_loop(outer, waits, body)


def conv_phase(spec, filt, mix, unmix, waits, kept, product):
    def body(ids):
        seen = [mul(mix[i], col) for i, col in zip(ids, columns(spec, ids))]
        mixed = [packed(product(halves(filt[i]), halves(x))) for i, x in zip(ids, seen)]
        done = [mul(unmix[i], y) for i, y in zip(ids, mixed)]
        for i, x in zip(ids, seen):
            kept[i] = x.astype(BF16)
        put_columns(spec, ids, done)

    side_loop(filt.shape[0], waits, body)


def first_body(
    which, opening, closing, gain, taps, raw, mix_hbm, unmix_hbm, filt_hbm, kept, first, spec, v, mix, unmix, filt, sems
):
    waits = fetch([mix_hbm, unmix_hbm, filt_hbm.at[which]], [mix, unmix, filt], sems)
    short_phase(raw, taps, v)
    open_phase(opening, lambda row: v[:, pl.ds(row, ROWS), :].astype(F32), spec)
    conv_phase(spec, filt, mix, unmix, waits, kept, cmul)
    g0 = gain[0:1, :][None]

    def write(row, value):
        rows = pl.ds(row, ROWS)
        first[:, rows, :] = g0 * v[:, rows, :].astype(F32) + value

    close_phase(closing, spec, write)


def second_body(
    which, opening, closing, gain, taps, first, raw, mix_hbm, unmix_hbm, filt_hbm,
    kept, second, x1, spec, mid, mix, unmix, filt, sems
):
    waits = fetch([mix_hbm, unmix_hbm, filt_hbm.at[which]], [mix, unmix, filt], sems)
    short_phase(raw, taps, x1)

    def read(row):
        rows = pl.ds(row, ROWS)
        value = x1[:, rows, :].astype(F32) * first[:, rows, :]
        mid[:, rows, :] = value
        return value

    open_phase(opening, read, spec)
    conv_phase(spec, filt, mix, unmix, waits, kept, cmul)
    g1 = gain[1:2, :][None]

    def write(row, value):
        rows = pl.ds(row, ROWS)
        second[:, rows, :] = (g1 * mid[:, rows, :] + value).astype(BF16)

    close_phase(closing, spec, write)


def back_second_body(
    which, opening, closing, gain, taps, bs, first, x1, mix_hbm, unmix_hbm, filt_hbm,
    kept, bf, grad_x1, spec, bx1, mix, unmix, filt, sems
):
    waits = fetch([mix_hbm, unmix_hbm, filt_hbm.at[which]], [mix, unmix, filt], sems)
    open_phase(opening, lambda row: bs[:, pl.ds(row, ROWS), :].astype(F32), spec)
    conv_phase(spec, filt, mix, unmix, waits, kept, conj_mul)
    g1 = gain[1:2, :][None]

    def write(row, value):
        rows = pl.ds(row, ROWS)
        back_middle = g1 * bs[:, rows, :].astype(F32) + value
        bf[:, rows, :] = back_middle * x1[:, rows, :].astype(F32)
        bx1[:, rows, :] = (back_middle * first[:, rows, :]).astype(BF16)

    close_phase(closing, spec, write)
    short_back_phase(bx1, taps, grad_x1)


def back_first_body(
    which, opening, closing, gain, taps, bf, mix_hbm, unmix_hbm, filt_hbm, kept, grad_v, spec, bv, mix, unmix, filt, sems
):
    waits = fetch([mix_hbm, unmix_hbm, filt_hbm.at[which]], [mix, unmix, filt], sems)
    open_phase(opening, lambda row: bf[:, pl.ds(row, ROWS), :], spec)
    conv_phase(spec, filt, mix, unmix, waits, kept, conj_mul)
    g0 = gain[0:1, :][None]

    def write(row, value):
        rows = pl.ds(row, ROWS)
        bv[:, rows, :] = (g0 * bf[:, rows, :] + value).astype(BF16)

    close_phase(closing, spec, write)
    short_back_phase(bv, taps, grad_v)


def grad_body(scale, has_prior, closing, unmix_hbm, left_hbm, right_hbm, *refs):
    out, spec, closed, unmix, left, right, sems = refs[has_prior:]
    waits = fetch([unmix_hbm, left_hbm, right_hbm], [unmix, left, right], sems)
    outer = closed.shape[0]

    def body(ids):
        mixed = [packed(conj_mul(halves(left[i]), halves(right[i]))) for i in ids]
        put_columns(spec, ids, [mul(unmix[i], y) for i, y in zip(ids, mixed)])

    side_loop(outer, waits, body)

    def write(row, value):
        closed[:, pl.ds(row, ROWS), :] = value * scale

    close_phase(closing, spec, write)

    def turn(p, carry):
        out[0, :, pl.ds(pl.multiple_of(p * INNER, INNER), INNER)] = jnp.transpose(closed[p])
        return carry

    lax.fori_loop(0, outer, turn, 0)


params = pltpu.CompilerParams(vmem_limit_bytes=58 << 20)
VMEM = pl.BlockSpec(memory_space=pltpu.VMEM)
ANY = pl.BlockSpec(memory_space=pl.ANY)


def table_buffer(outer):
    return pltpu.VMEM((outer, 2 * INNER, 2 * INNER), BF16)


def spectrum(outer, lanes):
    return (outer, 2 * INNER, lanes)


def cost(us):
    return pl.CostEstimate(flops=int(us * 0.8e6), bytes_accessed=int(us * 1e5), transcendentals=0)


def filter_spectra(tables, filters):
    opening, _, mix, _ = tables
    _, lanes, length = filters.shape
    outer = length // INNER
    return pl.pallas_call(
        filters_body,
        grid=(2,),
        in_specs=[
            pl.BlockSpec(opening.shape, lambda i: (0, 0)),
            ANY,
            pl.BlockSpec((1, lanes, length), lambda i: (i, 0, 0)),
        ],
        out_specs=pl.BlockSpec((1,) + spectrum(outer, lanes), lambda i: (i, 0, 0, 0)),
        out_shape=jax.ShapeDtypeStruct((2,) + spectrum(outer, lanes), BF16),
        scratch_shapes=[
            pltpu.VMEM((2 * outer, INNER, lanes), F32),
            pltpu.VMEM((outer, INNER, lanes), F32),
            table_buffer(outer),
            pltpu.SemaphoreType.DMA((1, outer // SIDE)),
        ],
        compiler_params=params,
        cost_estimate=cost(24),
        name="filter_spectra",
    )(opening, mix, filters)


def conv_pass(name, body, which, tables, gain, taps, filt, signals, kinds, hold):
    opening, closing, mix, unmix = tables
    outer, inner, lanes = signals[0].shape
    shape = (outer, inner, lanes)
    spec = spectrum(outer, lanes)
    return pl.pallas_call(
        functools.partial(body, which),
        in_specs=[VMEM] * (4 + len(signals)) + [ANY] * 3,
        out_specs=[VMEM] * (1 + len(kinds)),
        out_shape=[jax.ShapeDtypeStruct(spec, BF16)] + [jax.ShapeDtypeStruct(shape, kind) for kind in kinds],
        scratch_shapes=[pltpu.VMEM((2 * outer, inner, lanes), F32)]
        + [pltpu.VMEM(shape, hold)]
        + [table_buffer(outer), table_buffer(outer), pltpu.VMEM(spec, BF16)]
        + [pltpu.SemaphoreType.DMA((3, outer // SIDE))],
        compiler_params=params,
        cost_estimate=cost(20),
        name=name,
    )(opening, closing, gain, taps, *signals, mix, unmix, filt)


def grad_pass(name, which, scale, tables, left, right, prior=None):
    _, closing, _, unmix = tables
    outer, _, lanes = left.shape
    length = outer * INNER
    priors = [] if prior is None else [prior]
    return pl.pallas_call(
        functools.partial(grad_body, scale, len(priors)),
        grid=(1,),
        in_specs=[pl.BlockSpec(closing.shape, lambda i: (0, 0)), ANY, ANY, ANY] + [ANY] * len(priors),
        out_specs=pl.BlockSpec((1, lanes, length), lambda i: (which, 0, 0)),
        out_shape=jax.ShapeDtypeStruct((2, lanes, length), F32),
        input_output_aliases={4: 0} if priors else {},
        scratch_shapes=[
            pltpu.VMEM((2 * outer, INNER, lanes), F32),
            pltpu.VMEM((outer, INNER, lanes), F32),
            table_buffer(outer),
            pltpu.VMEM(left.shape, BF16),
            pltpu.VMEM(left.shape, BF16),
            pltpu.SemaphoreType.DMA((3, outer // SIDE)),
        ],
        compiler_params=params,
        cost_estimate=cost(15),
        name=name,
    )(closing, unmix, left, right, *priors)


def split_body(source, target):
    count, _, width = target.shape
    for i in range(count):
        target[i] = source[0, :, i * width : (i + 1) * width]


def rows_of(frames):
    return min(frames, 256)


def flat_width(block):
    count, frames, width = block.shape
    return jnp.swapaxes(block, 0, 1).reshape(frames, count * width)


def split_flat(block, count):
    frames, local_width = block.shape
    return jnp.swapaxes(block.reshape(frames, count, local_width // count), 0, 1)


def split_width(block, count, at):
    _, frames, local_width = block.shape
    width = local_width // count
    if width % 128:
        return split_flat(block[at], count)
    rows = rows_of(frames)
    return pl.pallas_call(
        split_body,
        grid=(frames // rows,),
        in_specs=[pl.BlockSpec((1, rows, local_width), lambda i: (at, i, 0))],
        out_specs=pl.BlockSpec((count, rows, width), lambda i: (0, i, 0)),
        out_shape=jax.ShapeDtypeStruct((count, frames, width), block.dtype),
        compiler_params=params,
        cost_estimate=cost(2),
        name="split_width",
    )(block)


def join_body(a, b, c, out):
    count, _, width = a.shape
    for i in range(count):
        lanes = slice(i * width, (i + 1) * width)
        out[0, :, lanes] = a[i]
        out[1, :, lanes] = b[i]
    out[2] = c[...]


def join_width(a, b, flat):
    count, frames, width = a.shape
    if width % 128:
        return jnp.stack([flat_width(a), flat_width(b), flat])
    rows = rows_of(frames)
    split = pl.BlockSpec((count, rows, width), lambda i: (0, i, 0))
    return pl.pallas_call(
        join_body,
        grid=(frames // rows,),
        in_specs=[split, split, pl.BlockSpec((rows, count * width), lambda i: (i, 0))],
        out_specs=pl.BlockSpec((3, rows, count * width), lambda i: (0, i, 0)),
        out_shape=jax.ShapeDtypeStruct((3, frames, count * width), BF16),
        compiler_params=params,
        cost_estimate=cost(5),
        name="join_width",
    )(a, b, flat)


def output_body(second, x2, weight, out, gated):
    count, frames, width = second.shape
    rows = rows_of(frames)

    @pl.when(pl.program_id(0) == 0)
    def _():
        for i in range(count):
            lanes = slice(i * width, (i + 1) * width)
            gated[:, lanes] = (x2[:, lanes].astype(F32) * second[i].astype(F32)).astype(BF16)

    def step(at, carry):
        here = pl.ds(pl.multiple_of(at * rows, rows), rows)
        out[here, :] = mul(gated[here, :], weight[...]).astype(BF16)
        return carry

    lax.fori_loop(0, frames // rows, step, 0)


def output_partial(second, x2, weight):
    count, frames, width = second.shape
    local_width, model = weight.shape
    if width % 128:
        gated = (x2.astype(F32) * flat_width(second).astype(F32)).astype(BF16)
        return mul(gated, weight).astype(BF16)
    cols = 512
    return pl.pallas_call(
        output_body,
        grid=(model // cols,),
        in_specs=[
            pl.BlockSpec(second.shape, lambda i: (0, 0, 0)),
            pl.BlockSpec(x2.shape, lambda i: (0, 0)),
            pl.BlockSpec((local_width, cols), lambda i: (0, i)),
        ],
        out_specs=pl.BlockSpec((frames, cols), lambda i: (0, i)),
        out_shape=jax.ShapeDtypeStruct((frames, model), BF16),
        scratch_shapes=[pltpu.VMEM((frames, local_width), BF16)],
        compiler_params=params,
        cost_estimate=cost(12),
        name="output_partial",
    )(second, x2, weight)


def back_gate_body(place, own, right1, left1, right2, left2, far, weight, x2, second, bs, bx2, blocks, sems):
    pairs, frames, width = second.shape
    rows = min(frames, 512)
    depth = own.shape[1]
    me = place[0]
    last = N_TP - 1

    def copy(source, slot):
        return pltpu.make_async_copy(source, blocks.at[slot], sems.at[slot])

    def fetch_one(slot, where, source, other):
        @pl.when(where)
        def _():
            copy(source, slot).start()

        @pl.when(jnp.logical_not(where))
        def _():
            copy(other, slot).start()

    @pl.when(pl.program_id(0) == 0)
    def _():
        copy(own, 0).start()
        fetch_one(1, me == 0, far, right1)
        fetch_one(2, me == last, far, left1)
        fetch_one(3, me <= 1, left2, right2)
        for slot in range(4):
            copy(own, slot).wait()

    at_depth = [
        me,
        jnp.where(me == 0, last, me - 1),
        jnp.where(me == last, 0, me + 1),
        jnp.where(me <= 1, me + 2, me - 2),
    ]

    def step(at, carry):
        here = pl.ds(pl.multiple_of(at * rows, rows), rows)
        full = None
        for slot in range(4):
            there = pl.ds(pl.multiple_of(at_depth[slot] * depth, depth), depth)
            part = lax.dot_general(
                blocks[slot, here, :], weight[:, there], (((1,), (1,)), ((), ())), preferred_element_type=F32
            )
            full = part if full is None else full + part
        full = full.astype(BF16).astype(F32)
        for i in range(pairs):
            lanes = slice(i * width, (i + 1) * width)
            bs[i, here, :] = (full[:, lanes] * x2[here, lanes].astype(F32)).astype(BF16)
            bx2[here, lanes] = (full[:, lanes] * second[i, here, :].astype(F32)).astype(BF16)
        return carry

    lax.fori_loop(0, frames // rows, step, 0)


def back_gate(landed, weight, x2, second):
    count, frames, width = second.shape
    local_width, model = weight.shape
    pairs = 2
    wide = pairs * width
    flat = pl.BlockSpec((frames, wide), lambda i: (0, i))
    split = pl.BlockSpec((pairs, frames, width), lambda i: (i, 0, 0))
    return pl.pallas_call(
        back_gate_body,
        grid=(count // pairs,),
        in_specs=[pl.BlockSpec(memory_space=pltpu.SMEM)]
        + [ANY] * 6
        + [pl.BlockSpec((wide, model), lambda i: (i, 0)), flat, split],
        out_specs=[split, flat],
        out_shape=[
            jax.ShapeDtypeStruct((count, frames, width), BF16),
            jax.ShapeDtypeStruct((frames, local_width), BF16),
        ],
        scratch_shapes=[pltpu.VMEM((4,) + landed[0].shape, BF16), pltpu.SemaphoreType.DMA((4,))],
        compiler_params=params,
        cost_estimate=cost(14),
        name="back_gate",
    )(lax.axis_index("tp").reshape(1), *landed, weight, x2, second)


def back_gate_plain(gathered, weight, x2, second):
    full = lax.dot_general(gathered, weight, (((1,), (1,)), ((), ())), preferred_element_type=F32)
    full = full.astype(BF16).astype(F32)
    bs = split_flat((full * x2.astype(F32)).astype(BF16), second.shape[0])
    return bs, (full * flat_width(second).astype(F32)).astype(BF16)


def after(value, *others):
    return lax.optimization_barrier((value, *others))[0]


def send(block, *pairs):
    return lax.ppermute(block, "tp", pairs)


def swap(block):
    return lax.all_to_all(block, "seq", split_axis=0, concat_axis=0, tiled=True)


def to_frames(block):
    count = lax.axis_size("seq")
    length, width = block.shape
    return swap(block.reshape(count, length // count, width))


def neighbour_rows(rows, shift):
    count = lax.axis_size("seq")
    pairs = [(i, i + shift) for i in range(count) if 0 <= i + shift < count]
    return lax.ppermute(rows, "seq", pairs)


def short_filter(block, taps):
    length = block.shape[0]
    before = neighbour_rows(block[length - 2 :], 1)
    wide = jnp.concatenate([before, block], axis=0).astype(F32)
    return sum(taps[j][None] * wide[2 - j : 2 - j + length] for j in range(3)).astype(BF16)


def short_filter_back(block, taps):
    length = block.shape[0]
    after = neighbour_rows(block[:2], -1)
    wide = jnp.concatenate([block, after], axis=0).astype(F32)
    return sum(taps[j][None] * wide[j : j + length] for j in range(3)).astype(BF16)


def local(projected, short_kernel, filters, skip_gain, out_weight, out_grad):
    _, frames, _, local_width = projected.shape
    _, width, length = filters.shape
    count = lax.axis_size("seq")
    outer = length // INNER
    grid3 = (outer, INNER, width)
    scale = float(length) ** -0.5
    mine = lax.axis_index("seq") * width
    taps = lax.dynamic_slice_in_dim(short_kernel, mine, width, axis=2)
    tables = transform_tables(outer)

    branches = jnp.transpose(projected[0], (1, 0, 2))
    own = out_grad[0]
    ring = width % 128 == 0 and lax.axis_size("tp") == N_TP
    raw_v = swap(split_width(branches, count, 0)).reshape(grid3)
    if ring:
        right1 = send(own, (0, 1), (1, 2), (2, 3))
        left1 = send(own, (1, 0), (2, 1), (3, 2))
    filt = filter_spectra(tables, filters)
    raw_v = after(raw_v, filt)
    if ring:
        far = send(after(own, filt), (0, 3), (3, 0))
    split_x1 = after(split_width(branches, count, 1), raw_v)
    raw_x1 = swap(split_x1).reshape(grid3)

    spec_v, first = conv_pass("first", first_body, 0, tables, skip_gain, taps[0], filt, [raw_v], [F32], BF16)
    raw_x1, first = lax.optimization_barrier((raw_x1, first))
    if ring:
        right1, left1, first = lax.optimization_barrier((right1, left1, first))
        right2 = send(right1, (1, 2), (2, 3))
        left2 = send(left1, (2, 1), (1, 0))
    spec_m, second, x1 = conv_pass(
        "second", second_body, 1, tables, skip_gain, taps[1], filt, [first, raw_x1], [BF16, BF16], F32
    )
    second_moved = to_frames(second.reshape(length, width))
    branch_x2 = branches[2]
    if ring:
        right2, left2, second, branch_x2 = lax.optimization_barrier((right2, left2, second, branch_x2))
    x2 = short_filter(branch_x2, short_kernel[2])
    partial = output_partial(second_moved, x2, out_weight)
    if ring:
        far, partial = lax.optimization_barrier((far, partial))
    output = lax.psum_scatter(partial, "tp", scatter_dimension=1, tiled=True)[None]

    if ring:
        landed = [own, right1, left1, right2, left2, far]
        bs, bx2 = back_gate(landed, out_weight, x2, second_moved)
    else:
        bs, bx2 = back_gate_plain(lax.all_gather(own, "tp", axis=1, tiled=True), out_weight, x2, second_moved)
    bs = swap(bs).reshape(grid3)
    grad_x2 = short_filter_back(bx2, short_kernel[2])
    spec_b, bf, grad_x1 = conv_pass(
        "back_second", back_second_body, 1, tables, skip_gain, taps[1], filt, [bs, first, x1], [F32, BF16], BF16
    )
    moved1 = to_frames(grad_x1.reshape(length, width))
    spec_c, grad_v = conv_pass(
        "back_first", back_first_body, 0, tables, skip_gain, taps[0], filt, [bf], [BF16], BF16
    )
    moved1, grad_v, spec_b = lax.optimization_barrier((moved1, grad_v, spec_b))
    moved0 = to_frames(grad_v.reshape(length, width))
    grad = grad_pass("grad_second", 1, scale, tables, spec_m, spec_b)
    filter_grad = grad_pass("grad_first", 0, scale, tables, spec_v, spec_c, grad)

    projected_grad = jnp.transpose(join_width(moved0, moved1, grad_x2), (1, 0, 2))[None]
    return (output, projected_grad, filter_grad)


def solution(mesh):
    in_specs = (
        P(None, "seq", None, "tp"),
        P(None, None, "tp"),
        P(None, ("tp", "seq"), None),
        P(None, ("tp", "seq")),
        P("tp", None),
        P(None, "seq", "tp"),
    )
    out_specs = (P(None, "seq", "tp"), P(None, "seq", None, "tp"), P(None, ("tp", "seq"), None))
    return jax.shard_map(local, mesh=mesh, in_specs=in_specs, out_specs=out_specs, check_vma=False)
```

```python
import functools
import math

import jax
import jax.numpy as jnp
import ml_dtypes
import numpy as np
from jax import lax
from jax.experimental import pallas as pl
from jax.experimental.pallas import tpu as pltpu
from jax.sharding import PartitionSpec as P

F32 = jnp.float32
BF16 = jnp.bfloat16
INNER = 128
SUB = 8
ROWS = 16
SIDE = 8


def spread_table(outer, scale):
    freq = np.arange(2 * outer * SUB)[:, None]
    time = np.arange(outer * SUB)[None, :]
    row = freq // SUB
    turn = 4 * outer
    phase = (4 * (row % outer) + 1) * (time // SUB) + outer * (row // outer)
    value = np.cos((phase % turn) * (2.0 * math.pi / turn)) * scale
    return np.where(freq % SUB == time % SUB, value, 0.0)


def transform_tables(outer):
    total = outer * INNER
    ids = np.arange(INNER)
    twist = 2.0 * math.pi * (np.arange(outer)[:, None] + 0.25) * ids[None, :] / total
    inner = 2.0 * math.pi * (ids[:, None] * ids[None, :] % INNER) / INNER
    angle = twist[:, None, :] + inner[None]
    cos, sin = np.cos(angle), np.sin(angle)
    mix = np.concatenate(
        [np.concatenate([cos, sin], axis=2), np.concatenate([-sin, cos], axis=2)], axis=1
    )
    opening = spread_table(outer, 1.0)
    closing = spread_table(outer, 1.0 / total).T
    unmix = np.swapaxes(mix, 1, 2)
    return [jnp.asarray(np.ascontiguousarray(t).astype(ml_dtypes.bfloat16)) for t in (opening, closing, mix, unmix)]


def mul(a, b):
    return jnp.dot(a, b, preferred_element_type=F32)


def halves(spec):
    return spec[:INNER].astype(F32), spec[INNER:].astype(F32)


def cmul(a, b):
    (ar, ai), (br, bi) = a, b
    return ar * br - ai * bi, ar * bi + ai * br


def conj_mul(a, b):
    (ar, ai), (br, bi) = a, b
    return ar * br + ai * bi, ar * bi - ai * br


def packed(pair):
    return jnp.concatenate(pair, axis=0).astype(BF16)


def open_phase(opening, read, spec):
    twice, inner, lanes = spec.shape
    outer = twice // 2

    def step(at, carry):
        row = pl.multiple_of(at * ROWS, ROWS)
        signal = read(row)
        wide = jnp.concatenate([signal[:, :SUB], signal[:, SUB:]], axis=2)
        flat = wide.reshape(outer * SUB, 2 * lanes).astype(BF16)
        out = mul(opening[...], flat).reshape(twice, SUB, 2 * lanes)
        spec[:, pl.ds(row, SUB), :] = out[:, :, :lanes]
        spec[:, pl.ds(row + SUB, SUB), :] = out[:, :, lanes:]
        return carry

    lax.fori_loop(0, inner // ROWS, step, 0)


def close_phase(closing, spec, write):
    twice, inner, lanes = spec.shape
    outer = twice // 2

    def step(at, carry):
        row = pl.multiple_of(at * ROWS, ROWS)
        wide = jnp.concatenate([spec[:, pl.ds(row, SUB), :], spec[:, pl.ds(row + SUB, SUB), :]], axis=2)
        flat = wide.reshape(twice * SUB, 2 * lanes).astype(BF16)
        out = mul(closing[...], flat).reshape(outer, SUB, 2 * lanes)
        write(row, jnp.concatenate([out[:, :, :lanes], out[:, :, lanes:]], axis=1))
        return carry

    lax.fori_loop(0, inner // ROWS, step, 0)


def side_loop(outer, waits, body):
    def step(at, carry):
        for wait in waits:
            wait(at)
        base = pl.multiple_of(at * SIDE, SIDE)
        body([base + i for i in range(SIDE)])
        return carry

    lax.fori_loop(0, outer // SIDE, step, 0)


def fetch(sources, buffers, sems):
    outer = buffers[0].shape[0]

    def piece(which, at):
        rows = pl.ds(at * SIDE, SIDE)
        return pltpu.make_async_copy(sources[which].at[rows], buffers[which].at[rows], sems.at[which, at])

    for at in range(outer // SIDE):
        for which in range(len(sources)):
            piece(which, at).start()
    return [lambda at, which=which: piece(which, at).wait() for which in range(len(sources))]


def columns(spec, ids):
    outer = spec.shape[0] // 2
    return [packed([spec[i], spec[outer + i]]) for i in ids]


def put_columns(spec, ids, values):
    outer = spec.shape[0] // 2
    for i, value in zip(ids, values):
        spec[i] = value[:INNER]
        spec[outer + i] = value[INNER:]


def short_phase(raw, taps, out):
    outer, inner, lanes = raw.shape

    def step(p, before):
        now = raw[p].astype(F32)
        wide = jnp.concatenate([before, now], axis=0)
        total = taps[0:1, :] * now
        for j in (1, 2):
            total = total + taps[j : j + 1, :] * wide[SUB - j : SUB - j + inner]
        out[p] = total.astype(BF16)
        return now[inner - SUB :]

    lax.fori_loop(0, outer, step, jnp.zeros((SUB, lanes), F32))


def short_back_phase(raw, taps, out):
    outer, inner, lanes = raw.shape

    def step(at, after):
        p = outer - 1 - at
        now = raw[p].astype(F32)
        wide = jnp.concatenate([now, after], axis=0)
        total = taps[0:1, :] * now
        for j in (1, 2):
            total = total + taps[j : j + 1, :] * wide[j : j + inner]
        out[p] = total.astype(BF16)
        return now[:SUB]

    lax.fori_loop(0, outer, step, jnp.zeros((SUB, lanes), F32))


def filters_body(opening, mix_hbm, filt, out, spec, sig, mix, sems):
    waits = fetch([mix_hbm], [mix], sems)
    outer = sig.shape[0]

    def turn(p, carry):
        sig[p] = jnp.transpose(filt[0, :, pl.ds(pl.multiple_of(p * INNER, INNER), INNER)])
        return carry

    lax.fori_loop(0, outer, turn, 0)
    open_phase(opening, lambda row: sig[:, pl.ds(row, ROWS), :], spec)

    def body(ids):
        results = [mul(mix[i], col) for i, col in zip(ids, columns(spec, ids))]
        for i, value in zip(ids, results):
            out[0, i] = value.astype(BF16)

    side_loop(outer, waits, body)


def conv_phase(spec, filt, mix, unmix, waits, kept, product):
    def body(ids):
        seen = [mul(mix[i], col) for i, col in zip(ids, columns(spec, ids))]
        mixed = [packed(product(halves(filt[i]), halves(x))) for i, x in zip(ids, seen)]
        done = [mul(unmix[i], y) for i, y in zip(ids, mixed)]
        for i, x in zip(ids, seen):
            kept[i] = x.astype(BF16)
        put_columns(spec, ids, done)

    side_loop(filt.shape[0], waits, body)


def first_body(
    which, opening, closing, gain, taps, raw, mix_hbm, unmix_hbm, filt_hbm, kept, first, spec, v, mix, unmix, filt, sems
):
    waits = fetch([mix_hbm, unmix_hbm, filt_hbm.at[which]], [mix, unmix, filt], sems)
    short_phase(raw, taps, v)
    open_phase(opening, lambda row: v[:, pl.ds(row, ROWS), :].astype(F32), spec)
    conv_phase(spec, filt, mix, unmix, waits, kept, cmul)
    g0 = gain[0:1, :][None]

    def write(row, value):
        rows = pl.ds(row, ROWS)
        first[:, rows, :] = g0 * v[:, rows, :].astype(F32) + value

    close_phase(closing, spec, write)


def second_body(
    which, opening, closing, gain, taps, first, raw, mix_hbm, unmix_hbm, filt_hbm,
    kept, second, x1, spec, mid, mix, unmix, filt, sems
):
    waits = fetch([mix_hbm, unmix_hbm, filt_hbm.at[which]], [mix, unmix, filt], sems)
    short_phase(raw, taps, x1)

    def read(row):
        rows = pl.ds(row, ROWS)
        value = x1[:, rows, :].astype(F32) * first[:, rows, :]
        mid[:, rows, :] = value
        return value

    open_phase(opening, read, spec)
    conv_phase(spec, filt, mix, unmix, waits, kept, cmul)
    g1 = gain[1:2, :][None]

    def write(row, value):
        rows = pl.ds(row, ROWS)
        second[:, rows, :] = (g1 * mid[:, rows, :] + value).astype(BF16)

    close_phase(closing, spec, write)


def back_second_body(
    which, opening, closing, gain, taps, bs, first, x1, mix_hbm, unmix_hbm, filt_hbm,
    kept, bf, grad_x1, spec, bx1, mix, unmix, filt, sems
):
    waits = fetch([mix_hbm, unmix_hbm, filt_hbm.at[which]], [mix, unmix, filt], sems)
    open_phase(opening, lambda row: bs[:, pl.ds(row, ROWS), :].astype(F32), spec)
    conv_phase(spec, filt, mix, unmix, waits, kept, conj_mul)
    g1 = gain[1:2, :][None]

    def write(row, value):
        rows = pl.ds(row, ROWS)
        back_middle = g1 * bs[:, rows, :].astype(F32) + value
        bf[:, rows, :] = back_middle * x1[:, rows, :].astype(F32)
        bx1[:, rows, :] = (back_middle * first[:, rows, :]).astype(BF16)

    close_phase(closing, spec, write)
    short_back_phase(bx1, taps, grad_x1)


def back_first_body(
    which, opening, closing, gain, taps, bf, mix_hbm, unmix_hbm, filt_hbm, kept, grad_v, spec, bv, mix, unmix, filt, sems
):
    waits = fetch([mix_hbm, unmix_hbm, filt_hbm.at[which]], [mix, unmix, filt], sems)
    open_phase(opening, lambda row: bf[:, pl.ds(row, ROWS), :], spec)
    conv_phase(spec, filt, mix, unmix, waits, kept, conj_mul)
    g0 = gain[0:1, :][None]

    def write(row, value):
        rows = pl.ds(row, ROWS)
        bv[:, rows, :] = (g0 * bf[:, rows, :] + value).astype(BF16)

    close_phase(closing, spec, write)
    short_back_phase(bv, taps, grad_v)


def grad_body(scale, has_prior, closing, unmix_hbm, left_hbm, right_hbm, *refs):
    out, spec, closed, unmix, left, right, sems = refs[has_prior:]
    waits = fetch([unmix_hbm, left_hbm, right_hbm], [unmix, left, right], sems)
    outer = closed.shape[0]

    def body(ids):
        mixed = [packed(conj_mul(halves(left[i]), halves(right[i]))) for i in ids]
        put_columns(spec, ids, [mul(unmix[i], y) for i, y in zip(ids, mixed)])

    side_loop(outer, waits, body)

    def write(row, value):
        closed[:, pl.ds(row, ROWS), :] = value * scale

    close_phase(closing, spec, write)

    def turn(p, carry):
        out[0, :, pl.ds(pl.multiple_of(p * INNER, INNER), INNER)] = jnp.transpose(closed[p])
        return carry

    lax.fori_loop(0, outer, turn, 0)


params = pltpu.CompilerParams(vmem_limit_bytes=58 << 20)
VMEM = pl.BlockSpec(memory_space=pltpu.VMEM)
ANY = pl.BlockSpec(memory_space=pl.ANY)


def table_buffer(outer):
    return pltpu.VMEM((outer, 2 * INNER, 2 * INNER), BF16)


def spectrum(outer, lanes):
    return (outer, 2 * INNER, lanes)


def cost(us):
    return pl.CostEstimate(flops=int(us * 0.8e6), bytes_accessed=int(us * 1e5), transcendentals=0)


def filter_spectra(tables, filters):
    opening, _, mix, _ = tables
    _, lanes, length = filters.shape
    outer = length // INNER
    return pl.pallas_call(
        filters_body,
        grid=(2,),
        in_specs=[
            pl.BlockSpec(opening.shape, lambda i: (0, 0)),
            ANY,
            pl.BlockSpec((1, lanes, length), lambda i: (i, 0, 0)),
        ],
        out_specs=pl.BlockSpec((1,) + spectrum(outer, lanes), lambda i: (i, 0, 0, 0)),
        out_shape=jax.ShapeDtypeStruct((2,) + spectrum(outer, lanes), BF16),
        scratch_shapes=[
            pltpu.VMEM((2 * outer, INNER, lanes), F32),
            pltpu.VMEM((outer, INNER, lanes), F32),
            table_buffer(outer),
            pltpu.SemaphoreType.DMA((1, outer // SIDE)),
        ],
        compiler_params=params,
        cost_estimate=cost(24),
        name="filter_spectra",
    )(opening, mix, filters)


def conv_pass(name, body, which, tables, gain, taps, filt, signals, kinds, hold):
    opening, closing, mix, unmix = tables
    outer, inner, lanes = signals[0].shape
    shape = (outer, inner, lanes)
    spec = spectrum(outer, lanes)
    return pl.pallas_call(
        functools.partial(body, which),
        in_specs=[VMEM] * (4 + len(signals)) + [ANY] * 3,
        out_specs=[VMEM] * (1 + len(kinds)),
        out_shape=[jax.ShapeDtypeStruct(spec, BF16)] + [jax.ShapeDtypeStruct(shape, kind) for kind in kinds],
        scratch_shapes=[pltpu.VMEM((2 * outer, inner, lanes), F32)]
        + [pltpu.VMEM(shape, hold)]
        + [table_buffer(outer), table_buffer(outer), pltpu.VMEM(spec, BF16)]
        + [pltpu.SemaphoreType.DMA((3, outer // SIDE))],
        compiler_params=params,
        cost_estimate=cost(20),
        name=name,
    )(opening, closing, gain, taps, *signals, mix, unmix, filt)


def grad_pass(name, which, scale, tables, left, right, prior=None):
    _, closing, _, unmix = tables
    outer, _, lanes = left.shape
    length = outer * INNER
    priors = [] if prior is None else [prior]
    return pl.pallas_call(
        functools.partial(grad_body, scale, len(priors)),
        grid=(1,),
        in_specs=[pl.BlockSpec(closing.shape, lambda i: (0, 0)), ANY, ANY, ANY] + [ANY] * len(priors),
        out_specs=pl.BlockSpec((1, lanes, length), lambda i: (which, 0, 0)),
        out_shape=jax.ShapeDtypeStruct((2, lanes, length), F32),
        input_output_aliases={4: 0} if priors else {},
        scratch_shapes=[
            pltpu.VMEM((2 * outer, INNER, lanes), F32),
            pltpu.VMEM((outer, INNER, lanes), F32),
            table_buffer(outer),
            pltpu.VMEM(left.shape, BF16),
            pltpu.VMEM(left.shape, BF16),
            pltpu.SemaphoreType.DMA((3, outer // SIDE)),
        ],
        compiler_params=params,
        cost_estimate=cost(15),
        name=name,
    )(closing, unmix, left, right, *priors)


def split_body(source, target):
    count, _, width = target.shape
    for i in range(count):
        target[i] = source[0, :, i * width : (i + 1) * width]


def rows_of(frames):
    return min(frames, 256)


def flat_width(block):
    count, frames, width = block.shape
    return jnp.swapaxes(block, 0, 1).reshape(frames, count * width)


def split_flat(block, count):
    frames, local_width = block.shape
    return jnp.swapaxes(block.reshape(frames, count, local_width // count), 0, 1)


def split_width(block, count, at):
    _, frames, local_width = block.shape
    width = local_width // count
    if width % 128:
        return split_flat(block[at], count)
    rows = rows_of(frames)
    return pl.pallas_call(
        split_body,
        grid=(frames // rows,),
        in_specs=[pl.BlockSpec((1, rows, local_width), lambda i: (at, i, 0))],
        out_specs=pl.BlockSpec((count, rows, width), lambda i: (0, i, 0)),
        out_shape=jax.ShapeDtypeStruct((count, frames, width), block.dtype),
        compiler_params=params,
        cost_estimate=cost(2),
        name="split_width",
    )(block)


def join_body(a, b, c, out):
    count, _, width = a.shape
    for i in range(count):
        lanes = slice(i * width, (i + 1) * width)
        out[0, :, lanes] = a[i]
        out[1, :, lanes] = b[i]
    out[2] = c[...]


def join_width(a, b, flat):
    count, frames, width = a.shape
    if width % 128:
        return jnp.stack([flat_width(a), flat_width(b), flat])
    rows = rows_of(frames)
    split = pl.BlockSpec((count, rows, width), lambda i: (0, i, 0))
    return pl.pallas_call(
        join_body,
        grid=(frames // rows,),
        in_specs=[split, split, pl.BlockSpec((rows, count * width), lambda i: (i, 0))],
        out_specs=pl.BlockSpec((3, rows, count * width), lambda i: (0, i, 0)),
        out_shape=jax.ShapeDtypeStruct((3, frames, count * width), BF16),
        compiler_params=params,
        cost_estimate=cost(5),
        name="join_width",
    )(a, b, flat)


def output_body(second, x2, weight, out, gated):
    count, frames, width = second.shape
    rows = rows_of(frames)

    @pl.when(pl.program_id(0) == 0)
    def _():
        for i in range(count):
            lanes = slice(i * width, (i + 1) * width)
            gated[:, lanes] = (x2[:, lanes].astype(F32) * second[i].astype(F32)).astype(BF16)

    def step(at, carry):
        here = pl.ds(pl.multiple_of(at * rows, rows), rows)
        out[here, :] = mul(gated[here, :], weight[...]).astype(BF16)
        return carry

    lax.fori_loop(0, frames // rows, step, 0)


def output_partial(second, x2, weight):
    count, frames, width = second.shape
    local_width, model = weight.shape
    if width % 128:
        gated = (x2.astype(F32) * flat_width(second).astype(F32)).astype(BF16)
        return mul(gated, weight).astype(BF16)
    cols = 512
    return pl.pallas_call(
        output_body,
        grid=(model // cols,),
        in_specs=[
            pl.BlockSpec(second.shape, lambda i: (0, 0, 0)),
            pl.BlockSpec(x2.shape, lambda i: (0, 0)),
            pl.BlockSpec((local_width, cols), lambda i: (0, i)),
        ],
        out_specs=pl.BlockSpec((frames, cols), lambda i: (0, i)),
        out_shape=jax.ShapeDtypeStruct((frames, model), BF16),
        scratch_shapes=[pltpu.VMEM((frames, local_width), BF16)],
        compiler_params=params,
        cost_estimate=cost(12),
        name="output_partial",
    )(second, x2, weight)


def back_gate_body(gathered, weight, x2, second, bs, bx2):
    pairs, frames, width = second.shape
    rows = min(frames, 512)

    def step(at, carry):
        here = pl.ds(pl.multiple_of(at * rows, rows), rows)
        full = lax.dot_general(
            gathered[here, :], weight[...], (((1,), (1,)), ((), ())), preferred_element_type=F32
        )
        full = full.astype(BF16).astype(F32)
        for i in range(pairs):
            lanes = slice(i * width, (i + 1) * width)
            bs[i, here, :] = (full[:, lanes] * x2[here, lanes].astype(F32)).astype(BF16)
            bx2[here, lanes] = (full[:, lanes] * second[i, here, :].astype(F32)).astype(BF16)
        return carry

    lax.fori_loop(0, frames // rows, step, 0)


def back_gate(gathered, weight, x2, second):
    count, frames, width = second.shape
    local_width, model = weight.shape
    if width % 128:
        full = lax.dot_general(gathered, weight, (((1,), (1,)), ((), ())), preferred_element_type=F32)
        full = full.astype(BF16).astype(F32)
        bs = split_flat((full * x2.astype(F32)).astype(BF16), count)
        return bs, (full * flat_width(second).astype(F32)).astype(BF16)
    pairs = 2
    wide = pairs * width
    flat = pl.BlockSpec((frames, wide), lambda i: (0, i))
    split = pl.BlockSpec((pairs, frames, width), lambda i: (i, 0, 0))
    return pl.pallas_call(
        back_gate_body,
        grid=(count // pairs,),
        in_specs=[
            pl.BlockSpec(gathered.shape, lambda i: (0, 0)),
            pl.BlockSpec((wide, model), lambda i: (i, 0)),
            flat,
            split,
        ],
        out_specs=[split, flat],
        out_shape=[
            jax.ShapeDtypeStruct((count, frames, width), BF16),
            jax.ShapeDtypeStruct((frames, local_width), BF16),
        ],
        compiler_params=params,
        cost_estimate=cost(14),
        name="back_gate",
    )(gathered, weight, x2, second)


def after(value, *others):
    return lax.optimization_barrier((value, *others))[0]


def swap(block):
    return lax.all_to_all(block, "seq", split_axis=0, concat_axis=0, tiled=True)


def to_frames(block):
    count = lax.axis_size("seq")
    length, width = block.shape
    return swap(block.reshape(count, length // count, width))


def neighbour_rows(rows, shift):
    count = lax.axis_size("seq")
    pairs = [(i, i + shift) for i in range(count) if 0 <= i + shift < count]
    return lax.ppermute(rows, "seq", pairs)


def short_filter(block, taps):
    length = block.shape[0]
    before = neighbour_rows(block[length - 2 :], 1)
    wide = jnp.concatenate([before, block], axis=0).astype(F32)
    return sum(taps[j][None] * wide[2 - j : 2 - j + length] for j in range(3)).astype(BF16)


def short_filter_back(block, taps):
    length = block.shape[0]
    after = neighbour_rows(block[:2], -1)
    wide = jnp.concatenate([block, after], axis=0).astype(F32)
    return sum(taps[j][None] * wide[j : j + length] for j in range(3)).astype(BF16)


def local(projected, short_kernel, filters, skip_gain, out_weight, out_grad):
    _, frames, _, local_width = projected.shape
    _, width, length = filters.shape
    count = lax.axis_size("seq")
    outer = length // INNER
    grid3 = (outer, INNER, width)
    scale = float(length) ** -0.5
    mine = lax.axis_index("seq") * width
    taps = lax.dynamic_slice_in_dim(short_kernel, mine, width, axis=2)
    tables = transform_tables(outer)

    branches = jnp.transpose(projected[0], (1, 0, 2))
    raw_v = swap(split_width(branches, count, 0)).reshape(grid3)
    gathered = lax.all_gather(out_grad[0], "tp", axis=1, tiled=True)
    filt = filter_spectra(tables, filters)
    raw_v = after(raw_v, filt)
    raw_x1 = swap(after(split_width(branches, count, 1), raw_v)).reshape(grid3)

    spec_v, first = conv_pass("first", first_body, 0, tables, skip_gain, taps[0], filt, [raw_v], [F32], BF16)
    raw_x1, first = lax.optimization_barrier((raw_x1, first))
    spec_m, second, x1 = conv_pass(
        "second", second_body, 1, tables, skip_gain, taps[1], filt, [first, raw_x1], [BF16, BF16], F32
    )
    branch_x2, second = lax.optimization_barrier((branches[2], second))
    x2 = short_filter(branch_x2, short_kernel[2])
    second = to_frames(second.reshape(length, width))
    partial = output_partial(second, x2, out_weight)
    output = lax.psum_scatter(partial, "tp", scatter_dimension=1, tiled=True)[None]

    gathered, _ = lax.optimization_barrier((gathered, partial))
    bs, bx2 = back_gate(gathered, out_weight, x2, second)
    bs = swap(bs).reshape(grid3)
    grad_x2 = short_filter_back(bx2, short_kernel[2])
    spec_b, bf, grad_x1 = conv_pass(
        "back_second", back_second_body, 1, tables, skip_gain, taps[1], filt, [bs, first, x1], [F32, BF16], BF16
    )
    moved1 = to_frames(grad_x1.reshape(length, width))
    spec_c, grad_v = conv_pass(
        "back_first", back_first_body, 0, tables, skip_gain, taps[0], filt, [bf], [BF16], BF16
    )
    moved1, grad_v, spec_b = lax.optimization_barrier((moved1, grad_v, spec_b))
    moved0 = to_frames(grad_v.reshape(length, width))
    grad = grad_pass("grad_second", 1, scale, tables, spec_m, spec_b)
    filter_grad = grad_pass("grad_first", 0, scale, tables, spec_v, spec_c, grad)

    projected_grad = jnp.transpose(join_width(moved0, moved1, grad_x2), (1, 0, 2))[None]
    return (output, projected_grad, filter_grad)


def solution(mesh):
    in_specs = (
        P(None, "seq", None, "tp"),
        P(None, None, "tp"),
        P(None, ("tp", "seq"), None),
        P(None, ("tp", "seq")),
        P("tp", None),
        P(None, "seq", "tp"),
    )
    out_specs = (P(None, "seq", "tp"), P(None, "seq", None, "tp"), P(None, ("tp", "seq"), None))
    return jax.shard_map(local, mesh=mesh, in_specs=in_specs, out_specs=out_specs, check_vma=False)
```

```python
import functools
import math

import jax
import jax.numpy as jnp
import ml_dtypes
import numpy as np
from jax import lax
from jax.experimental import pallas as pl
from jax.experimental.pallas import tpu as pltpu
from jax.sharding import PartitionSpec as P

F32 = jnp.float32
BF16 = jnp.bfloat16
INNER = 128
SUB = 8
ROWS = 16
SIDE = 8


def spread_table(outer, scale):
    freq = np.arange(2 * outer * SUB)[:, None]
    time = np.arange(outer * SUB)[None, :]
    row = freq // SUB
    turn = 4 * outer
    phase = (4 * (row % outer) + 1) * (time // SUB) + outer * (row // outer)
    value = np.cos((phase % turn) * (2.0 * math.pi / turn)) * scale
    return np.where(freq % SUB == time % SUB, value, 0.0)


def transform_tables(outer):
    total = outer * INNER
    ids = np.arange(INNER)
    twist = 2.0 * math.pi * (np.arange(outer)[:, None] + 0.25) * ids[None, :] / total
    inner = 2.0 * math.pi * (ids[:, None] * ids[None, :] % INNER) / INNER
    angle = twist[:, None, :] + inner[None]
    cos, sin = np.cos(angle), np.sin(angle)
    mix = np.concatenate(
        [np.concatenate([cos, sin], axis=2), np.concatenate([-sin, cos], axis=2)], axis=1
    )
    opening = spread_table(outer, 1.0)
    closing = spread_table(outer, 1.0 / total).T
    unmix = np.swapaxes(mix, 1, 2)
    return [jnp.asarray(np.ascontiguousarray(t).astype(ml_dtypes.bfloat16)) for t in (opening, closing, mix, unmix)]


def mul(a, b):
    return jnp.dot(a, b, preferred_element_type=F32)


def halves(spec):
    return spec[:INNER].astype(F32), spec[INNER:].astype(F32)


def cmul(a, b):
    (ar, ai), (br, bi) = a, b
    return ar * br - ai * bi, ar * bi + ai * br


def conj_mul(a, b):
    (ar, ai), (br, bi) = a, b
    return ar * br + ai * bi, ar * bi - ai * br


def packed(pair):
    return jnp.concatenate(pair, axis=0).astype(BF16)


def open_phase(opening, read, spec):
    twice, inner, lanes = spec.shape
    outer = twice // 2

    def step(at, carry):
        row = pl.multiple_of(at * ROWS, ROWS)
        signal = read(row)
        wide = jnp.concatenate([signal[:, :SUB], signal[:, SUB:]], axis=2)
        flat = wide.reshape(outer * SUB, 2 * lanes).astype(BF16)
        out = mul(opening[...], flat).reshape(twice, SUB, 2 * lanes)
        spec[:, pl.ds(row, SUB), :] = out[:, :, :lanes]
        spec[:, pl.ds(row + SUB, SUB), :] = out[:, :, lanes:]
        return carry

    lax.fori_loop(0, inner // ROWS, step, 0)


def close_phase(closing, spec, write):
    twice, inner, lanes = spec.shape
    outer = twice // 2

    def step(at, carry):
        row = pl.multiple_of(at * ROWS, ROWS)
        wide = jnp.concatenate([spec[:, pl.ds(row, SUB), :], spec[:, pl.ds(row + SUB, SUB), :]], axis=2)
        flat = wide.reshape(twice * SUB, 2 * lanes).astype(BF16)
        out = mul(closing[...], flat).reshape(outer, SUB, 2 * lanes)
        write(row, jnp.concatenate([out[:, :, :lanes], out[:, :, lanes:]], axis=1))
        return carry

    lax.fori_loop(0, inner // ROWS, step, 0)


def side_loop(outer, waits, body):
    def step(at, carry):
        for wait in waits:
            wait(at)
        base = pl.multiple_of(at * SIDE, SIDE)
        body([base + i for i in range(SIDE)])
        return carry

    lax.fori_loop(0, outer // SIDE, step, 0)


def fetch(sources, buffers, sems):
    outer = buffers[0].shape[0]

    def piece(which, at):
        rows = pl.ds(at * SIDE, SIDE)
        return pltpu.make_async_copy(sources[which].at[rows], buffers[which].at[rows], sems.at[which, at])

    for at in range(outer // SIDE):
        for which in range(len(sources)):
            piece(which, at).start()
    return [lambda at, which=which: piece(which, at).wait() for which in range(len(sources))]


def columns(spec, ids):
    outer = spec.shape[0] // 2
    return [packed([spec[i], spec[outer + i]]) for i in ids]


def put_columns(spec, ids, values):
    outer = spec.shape[0] // 2
    for i, value in zip(ids, values):
        spec[i] = value[:INNER]
        spec[outer + i] = value[INNER:]


def short_phase(raw, taps, out):
    outer, inner, lanes = raw.shape

    def step(p, before):
        now = raw[p].astype(F32)
        wide = jnp.concatenate([before, now], axis=0)
        total = taps[0:1, :] * now
        for j in (1, 2):
            total = total + taps[j : j + 1, :] * wide[SUB - j : SUB - j + inner]
        out[p] = total.astype(BF16)
        return now[inner - SUB :]

    lax.fori_loop(0, outer, step, jnp.zeros((SUB, lanes), F32))


def short_back_phase(raw, taps, out):
    outer, inner, lanes = raw.shape

    def step(at, after):
        p = outer - 1 - at
        now = raw[p].astype(F32)
        wide = jnp.concatenate([now, after], axis=0)
        total = taps[0:1, :] * now
        for j in (1, 2):
            total = total + taps[j : j + 1, :] * wide[j : j + inner]
        out[p] = total.astype(BF16)
        return now[:SUB]

    lax.fori_loop(0, outer, step, jnp.zeros((SUB, lanes), F32))


def filters_body(opening, mix_hbm, filt, out, spec, sig, mix, sems):
    waits = fetch([mix_hbm], [mix], sems)
    outer = sig.shape[0]

    def turn(p, carry):
        sig[p] = jnp.transpose(filt[0, :, pl.ds(pl.multiple_of(p * INNER, INNER), INNER)])
        return carry

    lax.fori_loop(0, outer, turn, 0)
    open_phase(opening, lambda row: sig[:, pl.ds(row, ROWS), :], spec)

    def body(ids):
        results = [mul(mix[i], col) for i, col in zip(ids, columns(spec, ids))]
        for i, value in zip(ids, results):
            out[0, i] = value.astype(BF16)

    side_loop(outer, waits, body)


def conv_phase(spec, filt, mix, unmix, waits, kept, product):
    def body(ids):
        seen = [mul(mix[i], col) for i, col in zip(ids, columns(spec, ids))]
        mixed = [packed(product(halves(filt[i]), halves(x))) for i, x in zip(ids, seen)]
        done = [mul(unmix[i], y) for i, y in zip(ids, mixed)]
        for i, x in zip(ids, seen):
            kept[i] = x.astype(BF16)
        put_columns(spec, ids, done)

    side_loop(filt.shape[0], waits, body)


def first_body(
    which, opening, closing, gain, taps, raw, mix_hbm, unmix_hbm, filt_hbm, kept, first, spec, v, mix, unmix, filt, sems
):
    waits = fetch([mix_hbm, unmix_hbm, filt_hbm.at[which]], [mix, unmix, filt], sems)
    short_phase(raw, taps, v)
    open_phase(opening, lambda row: v[:, pl.ds(row, ROWS), :].astype(F32), spec)
    conv_phase(spec, filt, mix, unmix, waits, kept, cmul)
    g0 = gain[0:1, :][None]

    def write(row, value):
        rows = pl.ds(row, ROWS)
        first[:, rows, :] = g0 * v[:, rows, :].astype(F32) + value

    close_phase(closing, spec, write)


def second_body(
    which, opening, closing, gain, taps, first, raw, mix_hbm, unmix_hbm, filt_hbm,
    kept, second, x1, spec, mid, mix, unmix, filt, sems
):
    waits = fetch([mix_hbm, unmix_hbm, filt_hbm.at[which]], [mix, unmix, filt], sems)
    short_phase(raw, taps, x1)

    def read(row):
        rows = pl.ds(row, ROWS)
        value = x1[:, rows, :].astype(F32) * first[:, rows, :]
        mid[:, rows, :] = value
        return value

    open_phase(opening, read, spec)
    conv_phase(spec, filt, mix, unmix, waits, kept, cmul)
    g1 = gain[1:2, :][None]

    def write(row, value):
        rows = pl.ds(row, ROWS)
        second[:, rows, :] = (g1 * mid[:, rows, :] + value).astype(BF16)

    close_phase(closing, spec, write)


def back_second_body(
    which, opening, closing, gain, taps, bs, first, x1, mix_hbm, unmix_hbm, filt_hbm,
    kept, bf, grad_x1, spec, bx1, mix, unmix, filt, sems
):
    waits = fetch([mix_hbm, unmix_hbm, filt_hbm.at[which]], [mix, unmix, filt], sems)
    open_phase(opening, lambda row: bs[:, pl.ds(row, ROWS), :].astype(F32), spec)
    conv_phase(spec, filt, mix, unmix, waits, kept, conj_mul)
    g1 = gain[1:2, :][None]

    def write(row, value):
        rows = pl.ds(row, ROWS)
        back_middle = g1 * bs[:, rows, :].astype(F32) + value
        bf[:, rows, :] = back_middle * x1[:, rows, :].astype(F32)
        bx1[:, rows, :] = (back_middle * first[:, rows, :]).astype(BF16)

    close_phase(closing, spec, write)
    short_back_phase(bx1, taps, grad_x1)


def back_first_body(
    which, opening, closing, gain, taps, bf, mix_hbm, unmix_hbm, filt_hbm, kept, grad_v, spec, bv, mix, unmix, filt, sems
):
    waits = fetch([mix_hbm, unmix_hbm, filt_hbm.at[which]], [mix, unmix, filt], sems)
    open_phase(opening, lambda row: bf[:, pl.ds(row, ROWS), :], spec)
    conv_phase(spec, filt, mix, unmix, waits, kept, conj_mul)
    g0 = gain[0:1, :][None]

    def write(row, value):
        rows = pl.ds(row, ROWS)
        bv[:, rows, :] = (g0 * bf[:, rows, :] + value).astype(BF16)

    close_phase(closing, spec, write)
    short_back_phase(bv, taps, grad_v)


def grad_body(scale, closing, unmix_hbm, v_hbm, m_hbm, c_hbm, b_hbm, out_hbm, spec, closed, out, unmix, pieces, sems, out_sems):
    outer, inner, both = closed.shape
    lanes = both // 2
    steps = outer // SIDE
    slots = unmix.shape[0]

    def copies(at):
        rows, slot = pl.ds(at * SIDE, SIDE), lax.rem(at, slots)
        found = [pltpu.make_async_copy(unmix_hbm.at[rows], unmix.at[slot], sems.at[0, slot])]
        for which, source in enumerate((v_hbm, m_hbm, c_hbm, b_hbm)):
            target = pieces.at[which, slot]
            found.append(pltpu.make_async_copy(source.at[rows], target, sems.at[1 + which, slot]))
        return found

    for at in range(min(slots, steps)):
        for copy in copies(at):
            copy.start()

    def step(at, carry):
        slot = lax.rem(at, slots)
        for copy in copies(at):
            copy.wait()
        mixed = []
        for i in range(SIDE):
            left, right = [packed(conj_mul(halves(pieces[k, slot, i]), halves(pieces[2 + k, slot, i]))) for k in range(2)]
            mixed.append(jnp.concatenate([left, right], axis=1))
        done = [mul(unmix[slot, i], y) for i, y in enumerate(mixed)]
        put_columns(spec, [at * SIDE + i for i in range(SIDE)], done)

        @pl.when(at + slots < steps)
        def _():
            for copy in copies(at + slots):
                copy.start()

        return carry

    lax.fori_loop(0, steps, step, 0)

    def write(row, value):
        closed[:, pl.ds(row, ROWS), :] = value * scale

    close_phase(closing, spec, write)
    parts = out_sems.shape[0]
    span = outer // parts

    def leave(part):
        columns_of = pl.ds(pl.multiple_of(part * span * inner, inner), span * inner)
        return pltpu.make_async_copy(out.at[:, :, columns_of], out_hbm.at[:, :, columns_of], out_sems.at[part])

    def turn(part, carry):
        for q in range(span):
            p = part * span + q
            here = pl.ds(pl.multiple_of(p * inner, inner), inner)
            out[0, :, here] = jnp.transpose(closed[p, :, :lanes])
            out[1, :, here] = jnp.transpose(closed[p, :, lanes:])
        leave(part).start()
        return carry

    lax.fori_loop(0, parts, turn, 0)

    def settle(part, carry):
        leave(part).wait()
        return carry

    lax.fori_loop(0, parts, settle, 0)


params = pltpu.CompilerParams(vmem_limit_bytes=58 << 20)
VMEM = pl.BlockSpec(memory_space=pltpu.VMEM)
ANY = pl.BlockSpec(memory_space=pl.ANY)


def table_buffer(outer):
    return pltpu.VMEM((outer, 2 * INNER, 2 * INNER), BF16)


def spectrum(outer, lanes):
    return (outer, 2 * INNER, lanes)


def cost(us):
    return pl.CostEstimate(flops=int(us * 0.8e6), bytes_accessed=int(us * 1e5), transcendentals=0)


def filter_spectra(tables, filters):
    opening, _, mix, _ = tables
    _, lanes, length = filters.shape
    outer = length // INNER
    return pl.pallas_call(
        filters_body,
        grid=(2,),
        in_specs=[
            pl.BlockSpec(opening.shape, lambda i: (0, 0)),
            ANY,
            pl.BlockSpec((1, lanes, length), lambda i: (i, 0, 0)),
        ],
        out_specs=pl.BlockSpec((1,) + spectrum(outer, lanes), lambda i: (i, 0, 0, 0)),
        out_shape=jax.ShapeDtypeStruct((2,) + spectrum(outer, lanes), BF16),
        scratch_shapes=[
            pltpu.VMEM((2 * outer, INNER, lanes), F32),
            pltpu.VMEM((outer, INNER, lanes), F32),
            table_buffer(outer),
            pltpu.SemaphoreType.DMA((1, outer // SIDE)),
        ],
        compiler_params=params,
        cost_estimate=cost(24),
        name="filter_spectra",
    )(opening, mix, filters)


def conv_pass(name, body, which, tables, gain, taps, filt, signals, kinds, hold):
    opening, closing, mix, unmix = tables
    outer, inner, lanes = signals[0].shape
    shape = (outer, inner, lanes)
    spec = spectrum(outer, lanes)
    return pl.pallas_call(
        functools.partial(body, which),
        in_specs=[VMEM] * (4 + len(signals)) + [ANY] * 3,
        out_specs=[VMEM] * (1 + len(kinds)),
        out_shape=[jax.ShapeDtypeStruct(spec, BF16)] + [jax.ShapeDtypeStruct(shape, kind) for kind in kinds],
        scratch_shapes=[pltpu.VMEM((2 * outer, inner, lanes), F32)]
        + [pltpu.VMEM(shape, hold)]
        + [table_buffer(outer), table_buffer(outer), pltpu.VMEM(spec, BF16)]
        + [pltpu.SemaphoreType.DMA((3, outer // SIDE))],
        compiler_params=params,
        cost_estimate=cost(20),
        name=name,
    )(opening, closing, gain, taps, *signals, mix, unmix, filt)


def grad_pass(scale, tables, spec_v, spec_m, spec_c, spec_b):
    _, closing, _, unmix = tables
    outer, _, lanes = spec_v.shape
    length = outer * INNER
    slots = 3
    return pl.pallas_call(
        functools.partial(grad_body, scale),
        in_specs=[VMEM] + [ANY] * 5,
        out_specs=ANY,
        out_shape=jax.ShapeDtypeStruct((2, lanes, length), F32),
        scratch_shapes=[
            pltpu.VMEM((2 * outer, INNER, 2 * lanes), F32),
            pltpu.VMEM((outer, INNER, 2 * lanes), F32),
            pltpu.VMEM((2, lanes, length), F32),
            pltpu.VMEM((slots, SIDE, 2 * INNER, 2 * INNER), BF16),
            pltpu.VMEM((4, slots, SIDE, 2 * INNER, lanes), BF16),
            pltpu.SemaphoreType.DMA((5, slots)),
            pltpu.SemaphoreType.DMA((8,)),
        ],
        compiler_params=params,
        cost_estimate=cost(28),
        name="filter_grads",
    )(closing, unmix, spec_v, spec_m, spec_c, spec_b)


def split_body(source, target):
    count, _, width = target.shape
    for i in range(count):
        target[i] = source[0, :, i * width : (i + 1) * width]


def rows_of(frames):
    return min(frames, 256)


def flat_width(block):
    count, frames, width = block.shape
    return jnp.swapaxes(block, 0, 1).reshape(frames, count * width)


def split_flat(block, count):
    frames, local_width = block.shape
    return jnp.swapaxes(block.reshape(frames, count, local_width // count), 0, 1)


def split_width(block, count, at):
    _, frames, local_width = block.shape
    width = local_width // count
    if width % 128:
        return split_flat(block[at], count)
    rows = rows_of(frames)
    return pl.pallas_call(
        split_body,
        grid=(frames // rows,),
        in_specs=[pl.BlockSpec((1, rows, local_width), lambda i: (at, i, 0))],
        out_specs=pl.BlockSpec((count, rows, width), lambda i: (0, i, 0)),
        out_shape=jax.ShapeDtypeStruct((count, frames, width), block.dtype),
        compiler_params=params,
        cost_estimate=cost(2),
        name="split_width",
    )(block)


def join_body(a, b, flat, halo, taps, out, carry):
    count, rows, width = a.shape

    @pl.when(pl.program_id(0) == 0)
    def _():
        carry[...] = halo[...]

    for i in range(count):
        lanes = slice(i * width, (i + 1) * width)
        out[0, :, lanes] = a[i]
        out[1, :, lanes] = b[i]
        now = flat[:, lanes].astype(F32)
        wide = jnp.concatenate([now, carry[:, lanes]], axis=0)
        total = taps[0:1, lanes] * now
        for j in (1, 2):
            total = total + taps[j : j + 1, lanes] * wide[j : j + rows]
        out[2, :, lanes] = total.astype(BF16)
        carry[:, lanes] = now[:SUB]


def join_width(a, b, flat, halo, taps):
    count, frames, width = a.shape
    if width % 128:
        wide = jnp.concatenate([flat, halo], axis=0).astype(F32)
        third = sum(taps[j][None] * wide[j : j + frames] for j in range(3)).astype(BF16)
        return jnp.stack([flat_width(a), flat_width(b), third])
    rows = rows_of(frames)
    last = frames // rows - 1
    halo = jnp.pad(halo.astype(F32), ((0, SUB - halo.shape[0]), (0, 0)))
    split = pl.BlockSpec((count, rows, width), lambda i: (0, last - i, 0))
    return pl.pallas_call(
        join_body,
        grid=(frames // rows,),
        in_specs=[
            split,
            split,
            pl.BlockSpec((rows, count * width), lambda i: (last - i, 0)),
            pl.BlockSpec(halo.shape, lambda i: (0, 0)),
            pl.BlockSpec(taps.shape, lambda i: (0, 0)),
        ],
        out_specs=pl.BlockSpec((3, rows, count * width), lambda i: (0, last - i, 0)),
        out_shape=jax.ShapeDtypeStruct((3, frames, count * width), BF16),
        scratch_shapes=[pltpu.VMEM(halo.shape, F32)],
        compiler_params=params,
        cost_estimate=cost(5),
        name="join_width",
    )(a, b, flat, halo, taps)


def output_body(second, x2, weight, out, gated):
    count, frames, width = second.shape
    rows = rows_of(frames)

    @pl.when(pl.program_id(0) == 0)
    def _():
        for i in range(count):
            lanes = slice(i * width, (i + 1) * width)
            gated[:, lanes] = (x2[:, lanes].astype(F32) * second[i].astype(F32)).astype(BF16)

    def step(at, carry):
        here = pl.ds(pl.multiple_of(at * rows, rows), rows)
        out[here, :] = mul(gated[here, :], weight[...]).astype(BF16)
        return carry

    lax.fori_loop(0, frames // rows, step, 0)


def output_partial(second, x2, weight):
    count, frames, width = second.shape
    local_width, model = weight.shape
    if width % 128:
        gated = (x2.astype(F32) * flat_width(second).astype(F32)).astype(BF16)
        return mul(gated, weight).astype(BF16)
    cols = 512
    return pl.pallas_call(
        output_body,
        grid=(model // cols,),
        in_specs=[
            pl.BlockSpec(second.shape, lambda i: (0, 0, 0)),
            pl.BlockSpec(x2.shape, lambda i: (0, 0)),
            pl.BlockSpec((local_width, cols), lambda i: (0, i)),
        ],
        out_specs=pl.BlockSpec((frames, cols), lambda i: (0, i)),
        out_shape=jax.ShapeDtypeStruct((frames, model), BF16),
        scratch_shapes=[pltpu.VMEM((frames, local_width), BF16)],
        compiler_params=params,
        cost_estimate=cost(12),
        name="output_partial",
    )(second, x2, weight)


def back_gate_body(gathered, weight, x2, second, bs, bx2):
    pairs, frames, width = second.shape
    rows = min(frames, 512)

    def step(at, carry):
        here = pl.ds(pl.multiple_of(at * rows, rows), rows)
        full = lax.dot_general(
            gathered[here, :], weight[...], (((1,), (1,)), ((), ())), preferred_element_type=F32
        )
        full = full.astype(BF16).astype(F32)
        for i in range(pairs):
            lanes = slice(i * width, (i + 1) * width)
            bs[i, here, :] = (full[:, lanes] * x2[here, lanes].astype(F32)).astype(BF16)
            bx2[here, lanes] = (full[:, lanes] * second[i, here, :].astype(F32)).astype(BF16)
        return carry

    lax.fori_loop(0, frames // rows, step, 0)


def back_gate(gathered, weight, x2, second):
    count, frames, width = second.shape
    local_width, model = weight.shape
    if width % 128:
        full = lax.dot_general(gathered, weight, (((1,), (1,)), ((), ())), preferred_element_type=F32)
        full = full.astype(BF16).astype(F32)
        bs = split_flat((full * x2.astype(F32)).astype(BF16), count)
        return bs, (full * flat_width(second).astype(F32)).astype(BF16)
    pairs = 2
    wide = pairs * width
    flat = pl.BlockSpec((frames, wide), lambda i: (0, i))
    split = pl.BlockSpec((pairs, frames, width), lambda i: (i, 0, 0))
    return pl.pallas_call(
        back_gate_body,
        grid=(count // pairs,),
        in_specs=[
            pl.BlockSpec(gathered.shape, lambda i: (0, 0)),
            pl.BlockSpec((wide, model), lambda i: (i, 0)),
            flat,
            split,
        ],
        out_specs=[split, flat],
        out_shape=[
            jax.ShapeDtypeStruct((count, frames, width), BF16),
            jax.ShapeDtypeStruct((frames, local_width), BF16),
        ],
        compiler_params=params,
        cost_estimate=cost(14),
        name="back_gate",
    )(gathered, weight, x2, second)


def after(value, *others):
    return lax.optimization_barrier((value, *others))[0]


def swap(block):
    return lax.all_to_all(block, "seq", split_axis=0, concat_axis=0, tiled=True)


def to_frames(block):
    count = lax.axis_size("seq")
    length, width = block.shape
    return swap(block.reshape(count, length // count, width))


def neighbour_rows(rows, shift):
    count = lax.axis_size("seq")
    pairs = [(i, i + shift) for i in range(count) if 0 <= i + shift < count]
    return lax.ppermute(rows, "seq", pairs)


def short_filter(block, before, taps):
    length = block.shape[0]
    wide = jnp.concatenate([before, block], axis=0).astype(F32)
    return sum(taps[j][None] * wide[2 - j : 2 - j + length] for j in range(3)).astype(BF16)


def local(projected, short_kernel, filters, skip_gain, out_weight, out_grad):
    _, frames, _, local_width = projected.shape
    _, width, length = filters.shape
    count = lax.axis_size("seq")
    outer = length // INNER
    grid3 = (outer, INNER, width)
    scale = float(length) ** -0.5
    mine = lax.axis_index("seq") * width
    taps = lax.dynamic_slice_in_dim(short_kernel, mine, width, axis=2)
    tables = transform_tables(outer)

    branches = jnp.transpose(projected[0], (1, 0, 2))
    before_x2 = neighbour_rows(branches[2, frames - 2 :], 1)
    raw_v = swap(after(split_width(branches, count, 0), before_x2)).reshape(grid3)
    gathered = lax.all_gather(out_grad[0], "tp", axis=1, tiled=True)
    filt = filter_spectra(tables, filters)
    raw_v = after(raw_v, filt)
    raw_x1 = swap(after(split_width(branches, count, 1), raw_v)).reshape(grid3)

    spec_v, first = conv_pass("first", first_body, 0, tables, skip_gain, taps[0], filt, [raw_v], [F32], BF16)
    raw_x1, first = lax.optimization_barrier((raw_x1, first))
    spec_m, second, x1 = conv_pass(
        "second", second_body, 1, tables, skip_gain, taps[1], filt, [first, raw_x1], [BF16, BF16], F32
    )
    branch_x2, second = lax.optimization_barrier((branches[2], second))
    x2 = short_filter(branch_x2, before_x2, short_kernel[2])
    second = to_frames(second.reshape(length, width))
    partial = output_partial(second, x2, out_weight)
    output = lax.psum_scatter(partial, "tp", scatter_dimension=1, tiled=True)[None]

    gathered, _ = lax.optimization_barrier((gathered, partial))
    bs, bx2 = back_gate(gathered, out_weight, x2, second)
    bs, after_x2 = lax.optimization_barrier((swap(bs).reshape(grid3), neighbour_rows(bx2[:2], -1)))
    spec_b, bf, grad_x1 = conv_pass(
        "back_second", back_second_body, 1, tables, skip_gain, taps[1], filt, [bs, first, x1], [F32, BF16], BF16
    )
    moved1 = to_frames(grad_x1.reshape(length, width))
    spec_c, grad_v = conv_pass(
        "back_first", back_first_body, 0, tables, skip_gain, taps[0], filt, [bf], [BF16], BF16
    )
    moved1, grad_v, spec_b = lax.optimization_barrier((moved1, grad_v, spec_b))
    moved0 = to_frames(grad_v.reshape(length, width))
    filter_grad = grad_pass(scale, tables, spec_v, spec_m, spec_c, spec_b)

    joined = join_width(moved0, moved1, bx2, after_x2, short_kernel[2])
    projected_grad = jnp.transpose(joined, (1, 0, 2))[None]
    return (output, projected_grad, filter_grad)


def solution(mesh):
    in_specs = (
        P(None, "seq", None, "tp"),
        P(None, None, "tp"),
        P(None, ("tp", "seq"), None),
        P(None, ("tp", "seq")),
        P("tp", None),
        P(None, "seq", "tp"),
    )
    out_specs = (P(None, "seq", "tp"), P(None, "seq", None, "tp"), P(None, ("tp", "seq"), None))
    return jax.shard_map(local, mesh=mesh, in_specs=in_specs, out_specs=out_specs, check_vma=False)
```

```python
import functools
import math

import jax
import jax.numpy as jnp
import ml_dtypes
import numpy as np
from jax import lax
from jax.experimental import pallas as pl
from jax.experimental.pallas import tpu as pltpu
from jax.sharding import PartitionSpec as P

F32 = jnp.float32
BF16 = jnp.bfloat16
INNER = 128
SUB = 8
ROWS = 16
SIDE = 8


def spread_table(outer, scale):
    freq = np.arange(2 * outer * SUB)[:, None]
    time = np.arange(outer * SUB)[None, :]
    row = freq // SUB
    turn = 4 * outer
    phase = (4 * (row % outer) + 1) * (time // SUB) + outer * (row // outer)
    value = np.cos((phase % turn) * (2.0 * math.pi / turn)) * scale
    return np.where(freq % SUB == time % SUB, value, 0.0)


def transform_tables(outer):
    total = outer * INNER
    ids = np.arange(INNER)
    twist = 2.0 * math.pi * (np.arange(outer)[:, None] + 0.25) * ids[None, :] / total
    inner = 2.0 * math.pi * (ids[:, None] * ids[None, :] % INNER) / INNER
    angle = twist[:, None, :] + inner[None]
    cos, sin = np.cos(angle), np.sin(angle)
    mix = np.concatenate(
        [np.concatenate([cos, sin], axis=2), np.concatenate([-sin, cos], axis=2)], axis=1
    )
    opening = spread_table(outer, 1.0)
    closing = spread_table(outer, 1.0 / total).T
    unmix = np.swapaxes(mix, 1, 2)
    return [jnp.asarray(np.ascontiguousarray(t).astype(ml_dtypes.bfloat16)) for t in (opening, closing, mix, unmix)]


def mul(a, b):
    return jnp.dot(a, b, preferred_element_type=F32)


def halves(spec):
    return spec[:INNER].astype(F32), spec[INNER:].astype(F32)


def cmul(a, b):
    (ar, ai), (br, bi) = a, b
    return ar * br - ai * bi, ar * bi + ai * br


def conj_mul(a, b):
    (ar, ai), (br, bi) = a, b
    return ar * br + ai * bi, ar * bi - ai * br


def packed(pair):
    return jnp.concatenate(pair, axis=0).astype(BF16)


def open_phase(opening, read, spec):
    twice, inner, lanes = spec.shape
    outer = twice // 2

    def step(at, carry):
        row = pl.multiple_of(at * ROWS, ROWS)
        signal = read(row)
        wide = jnp.concatenate([signal[:, :SUB], signal[:, SUB:]], axis=2)
        flat = wide.reshape(outer * SUB, 2 * lanes).astype(BF16)
        out = mul(opening[...], flat).reshape(twice, SUB, 2 * lanes)
        spec[:, pl.ds(row, SUB), :] = out[:, :, :lanes]
        spec[:, pl.ds(row + SUB, SUB), :] = out[:, :, lanes:]
        return carry

    lax.fori_loop(0, inner // ROWS, step, 0)


def close_phase(closing, spec, write):
    twice, inner, lanes = spec.shape
    outer = twice // 2

    def step(at, carry):
        row = pl.multiple_of(at * ROWS, ROWS)
        wide = jnp.concatenate([spec[:, pl.ds(row, SUB), :], spec[:, pl.ds(row + SUB, SUB), :]], axis=2)
        flat = wide.reshape(twice * SUB, 2 * lanes).astype(BF16)
        out = mul(closing[...], flat).reshape(outer, SUB, 2 * lanes)
        write(at, row, jnp.concatenate([out[:, :, :lanes], out[:, :, lanes:]], axis=1))
        return carry

    lax.fori_loop(0, inner // ROWS, step, 0)


def fetch(sources, buffers, sems):
    outer = buffers[0].shape[0]

    def piece(which, at):
        rows = pl.ds(at * SIDE, SIDE)
        return pltpu.make_async_copy(sources[which].at[rows], buffers[which].at[rows], sems.at[which, at])

    for at in range(outer // SIDE):
        for which in range(len(sources)):
            piece(which, at).start()
    return [lambda at, which=which: piece(which, at).wait() for which in range(len(sources))]


def columns(spec, ids):
    outer = spec.shape[0] // 2
    return [packed([spec[i], spec[outer + i]]) for i in ids]


def put_columns(spec, ids, values):
    outer = spec.shape[0] // 2
    for i, value in zip(ids, values):
        spec[i] = value[:INNER]
        spec[outer + i] = value[INNER:]


def short_phase(raw, taps, out):
    outer, inner, lanes = raw.shape

    def step(p, before):
        now = raw[p].astype(F32)
        wide = jnp.concatenate([before, now], axis=0)
        total = taps[0:1, :] * now
        for j in (1, 2):
            total = total + taps[j : j + 1, :] * wide[SUB - j : SUB - j + inner]
        out[p] = total.astype(BF16)
        return now[inner - SUB :]

    lax.fori_loop(0, outer, step, jnp.zeros((SUB, lanes), F32))


def short_back_phase(raw, taps, out, leave):
    outer, inner, lanes = raw.shape

    def step(at, after):
        p = outer - 1 - at
        now = raw[p].astype(F32)
        wide = jnp.concatenate([now, after], axis=0)
        total = taps[0:1, :] * now
        for j in (1, 2):
            total = total + taps[j : j + 1, :] * wide[j : j + inner]
        out[p] = total.astype(BF16)
        return now[:SUB]

    def group(at, after):
        for i in range(SIDE):
            after = step(at * SIDE + i, after)
        leave(outer // SIDE - 1 - at).start()
        return after

    lax.fori_loop(0, outer // SIDE, group, jnp.zeros((SUB, lanes), F32))


def leave_sides(buffer, target, sems, which):
    def copy(at):
        rows = pl.ds(at * SIDE, SIDE)
        return pltpu.make_async_copy(buffer.at[rows], target.at[rows], sems.at[which, at])

    return copy


def leave_rows(buffer, target, sems, which):
    def copy(at):
        rows = pl.ds(pl.multiple_of(at * ROWS, ROWS), ROWS)
        return pltpu.make_async_copy(buffer.at[:, rows], target.at[:, rows], sems.at[which, at])

    return copy


def settle(copy, steps):
    def step(at, carry):
        copy(at).wait()
        return carry

    lax.fori_loop(0, steps, step, 0)


def filters_body(opening, mix_hbm, filt_hbm, out_hbm, spec, sig, filt, mix, out, sems, filt_sems, out_sems):
    waits = fetch([mix_hbm], [mix], sems)
    outer, inner, both = sig.shape
    lanes = both // 2
    parts = outer // SIDE

    def arrive(part):
        frames = pl.ds(pl.multiple_of(part * SIDE * inner, SIDE * inner), SIDE * inner)
        return pltpu.make_async_copy(filt_hbm.at[:, :, frames], filt.at[:, :, frames], filt_sems.at[part])

    for part in range(parts):
        arrive(part).start()

    def turn(part, carry):
        arrive(part).wait()
        for q in range(SIDE):
            p = part * SIDE + q
            here = pl.ds(pl.multiple_of(p * inner, inner), inner)
            sig[p, :, :lanes] = jnp.transpose(filt[0, :, here])
            sig[p, :, lanes:] = jnp.transpose(filt[1, :, here])
        return carry

    lax.fori_loop(0, parts, turn, 0)
    open_phase(opening, lambda row: sig[:, pl.ds(row, ROWS), :], spec)

    def leave(at):
        rows = pl.ds(at * SIDE, SIDE)
        return pltpu.make_async_copy(out.at[:, rows], out_hbm.at[:, rows], out_sems.at[at])

    def step(at, carry):
        waits[0](at)
        ids = [at * SIDE + i for i in range(SIDE)]
        results = [mul(mix[i], col) for i, col in zip(ids, columns(spec, ids))]
        for i, value in zip(ids, results):
            out[0, i] = value[:, :lanes].astype(BF16)
            out[1, i] = value[:, lanes:].astype(BF16)
        leave(at).start()
        return carry

    lax.fori_loop(0, parts, step, 0)
    settle(leave, parts)


def conv_phase(spec, filt, mix, unmix, waits, kept, product, leave):
    def step(at, carry):
        for wait in waits:
            wait(at)
        ids = [at * SIDE + i for i in range(SIDE)]
        seen = [mul(mix[i], col) for i, col in zip(ids, columns(spec, ids))]
        mixed = [packed(product(halves(filt[i]), halves(x))) for i, x in zip(ids, seen)]
        done = [mul(unmix[i], y) for i, y in zip(ids, mixed)]
        for i, x in zip(ids, seen):
            kept[i] = x.astype(BF16)
        leave(at).start()
        put_columns(spec, ids, done)
        return carry

    lax.fori_loop(0, filt.shape[0] // SIDE, step, 0)


def first_body(
    which, opening, closing, gain, taps, raw, mix_hbm, unmix_hbm, filt_hbm, kept_hbm, first_hbm,
    spec, v, mix, unmix, filt, sems, out_sems, kept, first
):
    waits = fetch([mix_hbm, unmix_hbm, filt_hbm.at[which]], [mix, unmix, filt], sems)
    leave_kept = leave_sides(kept, kept_hbm, out_sems, 0)
    leave_first = leave_rows(first, first_hbm, out_sems, 1)
    short_phase(raw, taps, v)
    open_phase(opening, lambda row: v[:, pl.ds(row, ROWS), :].astype(F32), spec)
    conv_phase(spec, filt, mix, unmix, waits, kept, cmul, leave_kept)
    g0 = gain[0:1, :][None]

    def write(at, row, value):
        rows = pl.ds(row, ROWS)
        first[:, rows, :] = g0 * v[:, rows, :].astype(F32) + value
        leave_first(at).start()

    close_phase(closing, spec, write)
    settle(leave_kept, kept.shape[0] // SIDE)
    settle(leave_first, first.shape[1] // ROWS)


def second_body(
    which, opening, closing, gain, taps, first, raw, mix_hbm, unmix_hbm, filt_hbm, kept_hbm, second_hbm, x1_hbm,
    spec, mid, mix, unmix, filt, sems, out_sems, kept, second, x1
):
    waits = fetch([mix_hbm, unmix_hbm, filt_hbm.at[which]], [mix, unmix, filt], sems)
    leave_kept = leave_sides(kept, kept_hbm, out_sems, 0)
    leave_second = leave_rows(second, second_hbm, out_sems, 1)
    leave_x1 = pltpu.make_async_copy(x1, x1_hbm, out_sems.at[2, 0])
    short_phase(raw, taps, x1)
    leave_x1.start()

    def read(row):
        rows = pl.ds(row, ROWS)
        value = x1[:, rows, :].astype(F32) * first[:, rows, :]
        mid[:, rows, :] = value
        return value

    open_phase(opening, read, spec)
    conv_phase(spec, filt, mix, unmix, waits, kept, cmul, leave_kept)
    g1 = gain[1:2, :][None]

    def write(at, row, value):
        rows = pl.ds(row, ROWS)
        second[:, rows, :] = (g1 * mid[:, rows, :] + value).astype(BF16)
        leave_second(at).start()

    close_phase(closing, spec, write)
    leave_x1.wait()
    settle(leave_kept, kept.shape[0] // SIDE)
    settle(leave_second, second.shape[1] // ROWS)


def back_second_body(
    which, opening, closing, gain, taps, bs, first, x1, mix_hbm, unmix_hbm, filt_hbm, kept_hbm, bf_hbm, grad_hbm,
    spec, bx1, mix, unmix, filt, sems, out_sems, kept, bf, grad_x1
):
    waits = fetch([mix_hbm, unmix_hbm, filt_hbm.at[which]], [mix, unmix, filt], sems)
    leave_kept = leave_sides(kept, kept_hbm, out_sems, 0)
    leave_bf = leave_rows(bf, bf_hbm, out_sems, 1)
    leave_grad = leave_sides(grad_x1, grad_hbm, out_sems, 2)
    open_phase(opening, lambda row: bs[:, pl.ds(row, ROWS), :].astype(F32), spec)
    conv_phase(spec, filt, mix, unmix, waits, kept, conj_mul, leave_kept)
    g1 = gain[1:2, :][None]

    def write(at, row, value):
        rows = pl.ds(row, ROWS)
        back_middle = g1 * bs[:, rows, :].astype(F32) + value
        bf[:, rows, :] = back_middle * x1[:, rows, :].astype(F32)
        bx1[:, rows, :] = (back_middle * first[:, rows, :]).astype(BF16)
        leave_bf(at).start()

    close_phase(closing, spec, write)
    short_back_phase(bx1, taps, grad_x1, leave_grad)
    settle(leave_kept, kept.shape[0] // SIDE)
    settle(leave_bf, bf.shape[1] // ROWS)
    settle(leave_grad, kept.shape[0] // SIDE)


def back_first_body(
    which, opening, closing, gain, taps, bf, mix_hbm, unmix_hbm, filt_hbm, kept_hbm, grad_hbm,
    spec, bv, mix, unmix, filt, sems, out_sems, kept, grad_v
):
    waits = fetch([mix_hbm, unmix_hbm, filt_hbm.at[which]], [mix, unmix, filt], sems)
    leave_kept = leave_sides(kept, kept_hbm, out_sems, 0)
    leave_grad = leave_sides(grad_v, grad_hbm, out_sems, 1)
    open_phase(opening, lambda row: bf[:, pl.ds(row, ROWS), :], spec)
    conv_phase(spec, filt, mix, unmix, waits, kept, conj_mul, leave_kept)
    g0 = gain[0:1, :][None]

    def write(at, row, value):
        rows = pl.ds(row, ROWS)
        bv[:, rows, :] = (g0 * bf[:, rows, :] + value).astype(BF16)

    close_phase(closing, spec, write)
    short_back_phase(bv, taps, grad_v, leave_grad)
    settle(leave_kept, kept.shape[0] // SIDE)
    settle(leave_grad, kept.shape[0] // SIDE)


def grad_body(scale, closing, unmix_hbm, v_hbm, m_hbm, c_hbm, b_hbm, out_hbm, spec, closed, out, unmix, pieces, sems, out_sems):
    outer, inner, both = closed.shape
    lanes = both // 2
    steps = outer // SIDE
    slots = unmix.shape[0]

    def copies(at):
        rows, slot = pl.ds(at * SIDE, SIDE), lax.rem(at, slots)
        found = [pltpu.make_async_copy(unmix_hbm.at[rows], unmix.at[slot], sems.at[0, slot])]
        for which, source in enumerate((v_hbm, m_hbm, c_hbm, b_hbm)):
            target = pieces.at[which, slot]
            found.append(pltpu.make_async_copy(source.at[rows], target, sems.at[1 + which, slot]))
        return found

    for at in range(min(slots, steps)):
        for copy in copies(at):
            copy.start()

    def step(at, carry):
        slot = lax.rem(at, slots)
        for copy in copies(at):
            copy.wait()
        mixed = []
        for i in range(SIDE):
            left, right = [packed(conj_mul(halves(pieces[k, slot, i]), halves(pieces[2 + k, slot, i]))) for k in range(2)]
            mixed.append(jnp.concatenate([left, right], axis=1))
        done = [mul(unmix[slot, i], y) for i, y in enumerate(mixed)]
        put_columns(spec, [at * SIDE + i for i in range(SIDE)], done)

        @pl.when(at + slots < steps)
        def _():
            for copy in copies(at + slots):
                copy.start()

        return carry

    lax.fori_loop(0, steps, step, 0)

    def write(at, row, value):
        closed[:, pl.ds(row, ROWS), :] = value * scale

    close_phase(closing, spec, write)
    parts = out_sems.shape[0]
    span = outer // parts

    def leave(part):
        columns_of = pl.ds(pl.multiple_of(part * span * inner, inner), span * inner)
        return pltpu.make_async_copy(out.at[:, :, columns_of], out_hbm.at[:, :, columns_of], out_sems.at[part])

    def turn(part, carry):
        for q in range(span):
            p = part * span + q
            here = pl.ds(pl.multiple_of(p * inner, inner), inner)
            out[0, :, here] = jnp.transpose(closed[p, :, :lanes])
            out[1, :, here] = jnp.transpose(closed[p, :, lanes:])
        leave(part).start()
        return carry

    lax.fori_loop(0, parts, turn, 0)

    settle(leave, parts)


params = pltpu.CompilerParams(vmem_limit_bytes=58 << 20)
VMEM = pl.BlockSpec(memory_space=pltpu.VMEM)
ANY = pl.BlockSpec(memory_space=pl.ANY)


def table_buffer(outer):
    return pltpu.VMEM((outer, 2 * INNER, 2 * INNER), BF16)


def spectrum(outer, lanes):
    return (outer, 2 * INNER, lanes)


def cost(us):
    return pl.CostEstimate(flops=int(us * 0.8e6), bytes_accessed=int(us * 1e5), transcendentals=0)


def filter_spectra(tables, filters):
    opening, _, mix, _ = tables
    _, lanes, length = filters.shape
    outer = length // INNER
    steps = outer // SIDE
    shape = (2,) + spectrum(outer, lanes)
    return pl.pallas_call(
        filters_body,
        in_specs=[VMEM, ANY, ANY],
        out_specs=ANY,
        out_shape=jax.ShapeDtypeStruct(shape, BF16),
        scratch_shapes=[
            pltpu.VMEM((2 * outer, INNER, 2 * lanes), F32),
            pltpu.VMEM((outer, INNER, 2 * lanes), F32),
            pltpu.VMEM(filters.shape, F32),
            table_buffer(outer),
            pltpu.VMEM(shape, BF16),
            pltpu.SemaphoreType.DMA((1, steps)),
            pltpu.SemaphoreType.DMA((steps,)),
            pltpu.SemaphoreType.DMA((steps,)),
        ],
        compiler_params=params,
        cost_estimate=cost(24),
        name="filter_spectra",
    )(opening, mix, filters)


def conv_pass(name, body, which, tables, gain, taps, filt, signals, kinds, hold):
    opening, closing, mix, unmix = tables
    outer, inner, lanes = signals[0].shape
    shape = (outer, inner, lanes)
    spec = spectrum(outer, lanes)
    return pl.pallas_call(
        functools.partial(body, which),
        in_specs=[VMEM] * (4 + len(signals)) + [ANY] * 3,
        out_specs=[ANY] * (1 + len(kinds)),
        out_shape=[jax.ShapeDtypeStruct(spec, BF16)] + [jax.ShapeDtypeStruct(shape, kind) for kind in kinds],
        scratch_shapes=[pltpu.VMEM((2 * outer, inner, lanes), F32)]
        + [pltpu.VMEM(shape, hold)]
        + [table_buffer(outer), table_buffer(outer), pltpu.VMEM(spec, BF16)]
        + [pltpu.SemaphoreType.DMA((3, outer // SIDE))]
        + [pltpu.SemaphoreType.DMA((3, max(outer // SIDE, inner // ROWS)))]
        + [pltpu.VMEM(spec, BF16)]
        + [pltpu.VMEM(shape, kind) for kind in kinds],
        compiler_params=params,
        cost_estimate=cost(20),
        name=name,
    )(opening, closing, gain, taps, *signals, mix, unmix, filt)


def grad_pass(scale, tables, spec_v, spec_m, spec_c, spec_b):
    _, closing, _, unmix = tables
    outer, _, lanes = spec_v.shape
    length = outer * INNER
    slots = 3
    return pl.pallas_call(
        functools.partial(grad_body, scale),
        in_specs=[VMEM] + [ANY] * 5,
        out_specs=ANY,
        out_shape=jax.ShapeDtypeStruct((2, lanes, length), F32),
        scratch_shapes=[
            pltpu.VMEM((2 * outer, INNER, 2 * lanes), F32),
            pltpu.VMEM((outer, INNER, 2 * lanes), F32),
            pltpu.VMEM((2, lanes, length), F32),
            pltpu.VMEM((slots, SIDE, 2 * INNER, 2 * INNER), BF16),
            pltpu.VMEM((4, slots, SIDE, 2 * INNER, lanes), BF16),
            pltpu.SemaphoreType.DMA((5, slots)),
            pltpu.SemaphoreType.DMA((8,)),
        ],
        compiler_params=params,
        cost_estimate=cost(28),
        name="filter_grads",
    )(closing, unmix, spec_v, spec_m, spec_c, spec_b)


def split_body(source, target):
    count, _, width = target.shape
    for i in range(count):
        target[i] = source[0, :, i * width : (i + 1) * width]


def rows_of(frames):
    return min(frames, 256)


def flat_width(block):
    count, frames, width = block.shape
    return jnp.swapaxes(block, 0, 1).reshape(frames, count * width)


def split_flat(block, count):
    frames, local_width = block.shape
    return jnp.swapaxes(block.reshape(frames, count, local_width // count), 0, 1)


def split_width(block, count, at):
    _, frames, local_width = block.shape
    width = local_width // count
    if width % 128:
        return split_flat(block[at], count)
    rows = rows_of(frames)
    return pl.pallas_call(
        split_body,
        grid=(frames // rows,),
        in_specs=[pl.BlockSpec((1, rows, local_width), lambda i: (at, i, 0))],
        out_specs=pl.BlockSpec((count, rows, width), lambda i: (0, i, 0)),
        out_shape=jax.ShapeDtypeStruct((count, frames, width), block.dtype),
        compiler_params=params,
        cost_estimate=cost(2),
        name="split_width",
    )(block)


def join_body(a, b, flat, halo, taps, out, carry):
    count, rows, width = a.shape

    @pl.when(pl.program_id(0) == 0)
    def _():
        carry[...] = halo[...]

    for i in range(count):
        lanes = slice(i * width, (i + 1) * width)
        out[0, :, lanes] = a[i]
        out[1, :, lanes] = b[i]
        now = flat[:, lanes].astype(F32)
        wide = jnp.concatenate([now, carry[:, lanes]], axis=0)
        total = taps[0:1, lanes] * now
        for j in (1, 2):
            total = total + taps[j : j + 1, lanes] * wide[j : j + rows]
        out[2, :, lanes] = total.astype(BF16)
        carry[:, lanes] = now[:SUB]


def join_width(a, b, flat, halo, taps):
    count, frames, width = a.shape
    if width % 128:
        wide = jnp.concatenate([flat, halo], axis=0).astype(F32)
        third = sum(taps[j][None] * wide[j : j + frames] for j in range(3)).astype(BF16)
        return jnp.stack([flat_width(a), flat_width(b), third])
    rows = rows_of(frames)
    last = frames // rows - 1
    halo = jnp.pad(halo.astype(F32), ((0, SUB - halo.shape[0]), (0, 0)))
    split = pl.BlockSpec((count, rows, width), lambda i: (0, last - i, 0))
    return pl.pallas_call(
        join_body,
        grid=(frames // rows,),
        in_specs=[
            split,
            split,
            pl.BlockSpec((rows, count * width), lambda i: (last - i, 0)),
            pl.BlockSpec(halo.shape, lambda i: (0, 0)),
            pl.BlockSpec(taps.shape, lambda i: (0, 0)),
        ],
        out_specs=pl.BlockSpec((3, rows, count * width), lambda i: (0, last - i, 0)),
        out_shape=jax.ShapeDtypeStruct((3, frames, count * width), BF16),
        scratch_shapes=[pltpu.VMEM(halo.shape, F32)],
        compiler_params=params,
        cost_estimate=cost(5),
        name="join_width",
    )(a, b, flat, halo, taps)


def output_body(second, x2, weight, out, gated):
    count, frames, width = second.shape
    rows = min(frames, 512)

    @pl.when(pl.program_id(0) == 0)
    def _():
        for i in range(count):
            lanes = slice(i * width, (i + 1) * width)
            gated[:, lanes] = (x2[:, lanes].astype(F32) * second[i].astype(F32)).astype(BF16)

    def step(at, carry):
        here = pl.ds(pl.multiple_of(at * rows, rows), rows)
        out[here, :] = mul(gated[here, :], weight[...]).astype(BF16)
        return carry

    lax.fori_loop(0, frames // rows, step, 0)


def output_partial(second, x2, weight):
    count, frames, width = second.shape
    local_width, model = weight.shape
    if width % 128:
        gated = (x2.astype(F32) * flat_width(second).astype(F32)).astype(BF16)
        return mul(gated, weight).astype(BF16)
    cols = 512
    return pl.pallas_call(
        output_body,
        grid=(model // cols,),
        in_specs=[
            pl.BlockSpec(second.shape, lambda i: (0, 0, 0)),
            pl.BlockSpec(x2.shape, lambda i: (0, 0)),
            pl.BlockSpec((local_width, cols), lambda i: (0, i)),
        ],
        out_specs=pl.BlockSpec((frames, cols), lambda i: (0, i)),
        out_shape=jax.ShapeDtypeStruct((frames, model), BF16),
        scratch_shapes=[pltpu.VMEM((frames, local_width), BF16)],
        compiler_params=params,
        cost_estimate=cost(12),
        name="output_partial",
    )(second, x2, weight)


def back_gate_body(gathered, weight, x2, second, bs, bx2):
    pairs, frames, width = second.shape
    rows = min(frames, 512)

    def step(at, carry):
        here = pl.ds(pl.multiple_of(at * rows, rows), rows)
        full = lax.dot_general(
            gathered[here, :], weight[...], (((1,), (1,)), ((), ())), preferred_element_type=F32
        )
        full = full.astype(BF16).astype(F32)
        for i in range(pairs):
            lanes = slice(i * width, (i + 1) * width)
            bs[i, here, :] = (full[:, lanes] * x2[here, lanes].astype(F32)).astype(BF16)
            bx2[here, lanes] = (full[:, lanes] * second[i, here, :].astype(F32)).astype(BF16)
        return carry

    lax.fori_loop(0, frames // rows, step, 0)


def back_gate(gathered, weight, x2, second):
    count, frames, width = second.shape
    local_width, model = weight.shape
    if width % 128:
        full = lax.dot_general(gathered, weight, (((1,), (1,)), ((), ())), preferred_element_type=F32)
        full = full.astype(BF16).astype(F32)
        bs = split_flat((full * x2.astype(F32)).astype(BF16), count)
        return bs, (full * flat_width(second).astype(F32)).astype(BF16)
    pairs = 2
    wide = pairs * width
    flat = pl.BlockSpec((frames, wide), lambda i: (0, i))
    split = pl.BlockSpec((pairs, frames, width), lambda i: (i, 0, 0))
    return pl.pallas_call(
        back_gate_body,
        grid=(count // pairs,),
        in_specs=[
            pl.BlockSpec(gathered.shape, lambda i: (0, 0)),
            pl.BlockSpec((wide, model), lambda i: (i, 0)),
            flat,
            split,
        ],
        out_specs=[split, flat],
        out_shape=[
            jax.ShapeDtypeStruct((count, frames, width), BF16),
            jax.ShapeDtypeStruct((frames, local_width), BF16),
        ],
        compiler_params=params,
        cost_estimate=cost(14),
        name="back_gate",
    )(gathered, weight, x2, second)


def after(value, *others):
    return lax.optimization_barrier((value, *others))[0]


def swap(block):
    return lax.all_to_all(block, "seq", split_axis=0, concat_axis=0, tiled=True)


def to_frames(block):
    count = lax.axis_size("seq")
    length, width = block.shape
    return swap(block.reshape(count, length // count, width))


def neighbour_rows(rows, shift):
    count = lax.axis_size("seq")
    pairs = [(i, i + shift) for i in range(count) if 0 <= i + shift < count]
    return lax.ppermute(rows, "seq", pairs)


def short_filter(block, before, taps):
    length = block.shape[0]
    wide = jnp.concatenate([before, block], axis=0).astype(F32)
    return sum(taps[j][None] * wide[2 - j : 2 - j + length] for j in range(3)).astype(BF16)


def local(projected, short_kernel, filters, skip_gain, out_weight, out_grad):
    _, frames, _, local_width = projected.shape
    _, width, length = filters.shape
    count = lax.axis_size("seq")
    outer = length // INNER
    grid3 = (outer, INNER, width)
    scale = float(length) ** -0.5
    mine = lax.axis_index("seq") * width
    taps = lax.dynamic_slice_in_dim(short_kernel, mine, width, axis=2)
    tables = transform_tables(outer)

    branches = jnp.transpose(projected[0], (1, 0, 2))
    before_x2 = neighbour_rows(branches[2, frames - 2 :], 1)
    raw_v = swap(after(split_width(branches, count, 0), before_x2)).reshape(grid3)
    gathered = lax.all_gather(out_grad[0], "tp", axis=1, tiled=True)
    filt = filter_spectra(tables, filters)
    raw_v = after(raw_v, filt)
    raw_x1 = swap(after(split_width(branches, count, 1), raw_v)).reshape(grid3)

    spec_v, first = conv_pass("first", first_body, 0, tables, skip_gain, taps[0], filt, [raw_v], [F32], BF16)
    raw_x1, first = lax.optimization_barrier((raw_x1, first))
    spec_m, second, x1 = conv_pass(
        "second", second_body, 1, tables, skip_gain, taps[1], filt, [first, raw_x1], [BF16, BF16], F32
    )
    branch_x2, second = lax.optimization_barrier((branches[2], second))
    x2 = short_filter(branch_x2, before_x2, short_kernel[2])
    second = to_frames(second.reshape(length, width))
    partial = output_partial(second, x2, out_weight)
    output = lax.psum_scatter(partial, "tp", scatter_dimension=1, tiled=True)[None]

    gathered, _ = lax.optimization_barrier((gathered, partial))
    bs, bx2 = back_gate(gathered, out_weight, x2, second)
    bs, after_x2 = lax.optimization_barrier((swap(bs).reshape(grid3), neighbour_rows(bx2[:2], -1)))
    spec_b, bf, grad_x1 = conv_pass(
        "back_second", back_second_body, 1, tables, skip_gain, taps[1], filt, [bs, first, x1], [F32, BF16], BF16
    )
    moved1 = to_frames(grad_x1.reshape(length, width))
    spec_c, grad_v = conv_pass(
        "back_first", back_first_body, 0, tables, skip_gain, taps[0], filt, [bf], [BF16], BF16
    )
    moved1, grad_v, spec_b = lax.optimization_barrier((moved1, grad_v, spec_b))
    moved0 = to_frames(grad_v.reshape(length, width))
    filter_grad = grad_pass(scale, tables, spec_v, spec_m, spec_c, spec_b)

    joined = join_width(moved0, moved1, bx2, after_x2, short_kernel[2])
    projected_grad = jnp.transpose(joined, (1, 0, 2))[None]
    return (output, projected_grad, filter_grad)


def solution(mesh):
    in_specs = (
        P(None, "seq", None, "tp"),
        P(None, None, "tp"),
        P(None, ("tp", "seq"), None),
        P(None, ("tp", "seq")),
        P("tp", None),
        P(None, "seq", "tp"),
    )
    out_specs = (P(None, "seq", "tp"), P(None, "seq", None, "tp"), P(None, ("tp", "seq"), None))
    return jax.shard_map(local, mesh=mesh, in_specs=in_specs, out_specs=out_specs, check_vma=False)
```

```python
import functools
import math

import jax
import jax.numpy as jnp
import ml_dtypes
import numpy as np
from jax import lax
from jax.experimental import pallas as pl
from jax.experimental.pallas import tpu as pltpu
from jax.sharding import PartitionSpec as P

F32 = jnp.float32
BF16 = jnp.bfloat16
INNER = 128
SUB = 8
ROWS = 16
SIDE = 8
N_TP = 4


def spread_table(outer, scale):
    freq = np.arange(2 * outer * SUB)[:, None]
    time = np.arange(outer * SUB)[None, :]
    row = freq // SUB
    turn = 4 * outer
    phase = (4 * (row % outer) + 1) * (time // SUB) + outer * (row // outer)
    value = np.cos((phase % turn) * (2.0 * math.pi / turn)) * scale
    return np.where(freq % SUB == time % SUB, value, 0.0)


def transform_tables(outer):
    total = outer * INNER
    ids = np.arange(INNER)
    twist = 2.0 * math.pi * (np.arange(outer)[:, None] + 0.25) * ids[None, :] / total
    inner = 2.0 * math.pi * (ids[:, None] * ids[None, :] % INNER) / INNER
    angle = twist[:, None, :] + inner[None]
    cos, sin = np.cos(angle), np.sin(angle)
    mix = np.concatenate(
        [np.concatenate([cos, sin], axis=2), np.concatenate([-sin, cos], axis=2)], axis=1
    )
    opening = spread_table(outer, 1.0)
    closing = spread_table(outer, 1.0 / total).T
    unmix = np.swapaxes(mix, 1, 2)
    return [jnp.asarray(np.ascontiguousarray(t).astype(ml_dtypes.bfloat16)) for t in (opening, closing, mix, unmix)]


def mul(a, b):
    return jnp.dot(a, b, preferred_element_type=F32)


def halves(spec):
    return spec[:INNER].astype(F32), spec[INNER:].astype(F32)


def cmul(a, b):
    (ar, ai), (br, bi) = a, b
    return ar * br - ai * bi, ar * bi + ai * br


def conj_mul(a, b):
    (ar, ai), (br, bi) = a, b
    return ar * br + ai * bi, ar * bi - ai * br


def packed(pair):
    return jnp.concatenate(pair, axis=0).astype(BF16)


def open_phase(opening, read, spec):
    twice, inner, lanes = spec.shape
    outer = twice // 2

    def step(at, carry):
        row = pl.multiple_of(at * ROWS, ROWS)
        signal = read(row)
        wide = jnp.concatenate([signal[:, :SUB], signal[:, SUB:]], axis=2)
        flat = wide.reshape(outer * SUB, 2 * lanes).astype(BF16)
        out = mul(opening[...], flat).reshape(twice, SUB, 2 * lanes)
        spec[:, pl.ds(row, SUB), :] = out[:, :, :lanes]
        spec[:, pl.ds(row + SUB, SUB), :] = out[:, :, lanes:]
        return carry

    lax.fori_loop(0, inner // ROWS, step, 0)


def close_phase(closing, spec, write):
    twice, inner, lanes = spec.shape
    outer = twice // 2

    def step(at, carry):
        row = pl.multiple_of(at * ROWS, ROWS)
        wide = jnp.concatenate([spec[:, pl.ds(row, SUB), :], spec[:, pl.ds(row + SUB, SUB), :]], axis=2)
        flat = wide.reshape(twice * SUB, 2 * lanes).astype(BF16)
        out = mul(closing[...], flat).reshape(outer, SUB, 2 * lanes)
        write(at, row, jnp.concatenate([out[:, :, :lanes], out[:, :, lanes:]], axis=1))
        return carry

    lax.fori_loop(0, inner // ROWS, step, 0)


def fetch(sources, buffers, sems):
    outer = buffers[0].shape[0]

    def piece(which, at):
        rows = pl.ds(at * SIDE, SIDE)
        return pltpu.make_async_copy(sources[which].at[rows], buffers[which].at[rows], sems.at[which, at])

    for at in range(outer // SIDE):
        for which in range(len(sources)):
            piece(which, at).start()
    return [lambda at, which=which: piece(which, at).wait() for which in range(len(sources))]


def columns(spec, ids):
    outer = spec.shape[0] // 2
    return [packed([spec[i], spec[outer + i]]) for i in ids]


def put_columns(spec, ids, values):
    outer = spec.shape[0] // 2
    for i, value in zip(ids, values):
        spec[i] = value[:INNER]
        spec[outer + i] = value[INNER:]


def short_phase(raw, taps, out):
    outer, inner, lanes = raw.shape

    def step(p, before):
        now = raw[p].astype(F32)
        wide = jnp.concatenate([before, now], axis=0)
        total = taps[0:1, :] * now
        for j in (1, 2):
            total = total + taps[j : j + 1, :] * wide[SUB - j : SUB - j + inner]
        out[p] = total.astype(BF16)
        return now[inner - SUB :]

    lax.fori_loop(0, outer, step, jnp.zeros((SUB, lanes), F32))


def short_back_phase(raw, taps, out, leave):
    outer, inner, lanes = raw.shape

    def step(at, after):
        p = outer - 1 - at
        now = raw[p].astype(F32)
        wide = jnp.concatenate([now, after], axis=0)
        total = taps[0:1, :] * now
        for j in (1, 2):
            total = total + taps[j : j + 1, :] * wide[j : j + inner]
        out[p] = total.astype(BF16)
        return now[:SUB]

    def group(at, after):
        for i in range(SIDE):
            after = step(at * SIDE + i, after)
        leave(outer // SIDE - 1 - at).start()
        return after

    lax.fori_loop(0, outer // SIDE, group, jnp.zeros((SUB, lanes), F32))


def leave_sides(buffer, target, sems, which):
    def copy(at):
        rows = pl.ds(at * SIDE, SIDE)
        return pltpu.make_async_copy(buffer.at[rows], target.at[rows], sems.at[which, at])

    return copy


def leave_rows(buffer, target, sems, which):
    def copy(at):
        rows = pl.ds(pl.multiple_of(at * ROWS, ROWS), ROWS)
        return pltpu.make_async_copy(buffer.at[:, rows], target.at[:, rows], sems.at[which, at])

    return copy


def settle(copy, steps):
    def step(at, carry):
        copy(at).wait()
        return carry

    lax.fori_loop(0, steps, step, 0)


def filters_body(opening, mix_hbm, filt_hbm, out_hbm, spec, sig, filt, mix, out, sems, filt_sems, out_sems):
    waits = fetch([mix_hbm], [mix], sems)
    outer, inner, both = sig.shape
    lanes = both // 2
    parts = outer // SIDE

    def arrive(part):
        frames = pl.ds(pl.multiple_of(part * SIDE * inner, SIDE * inner), SIDE * inner)
        return pltpu.make_async_copy(filt_hbm.at[:, :, frames], filt.at[:, :, frames], filt_sems.at[part])

    for part in range(parts):
        arrive(part).start()

    def turn(part, carry):
        arrive(part).wait()
        for q in range(SIDE):
            p = part * SIDE + q
            here = pl.ds(pl.multiple_of(p * inner, inner), inner)
            sig[p, :, :lanes] = jnp.transpose(filt[0, :, here])
            sig[p, :, lanes:] = jnp.transpose(filt[1, :, here])
        return carry

    lax.fori_loop(0, parts, turn, 0)
    open_phase(opening, lambda row: sig[:, pl.ds(row, ROWS), :], spec)

    def leave(at):
        rows = pl.ds(at * SIDE, SIDE)
        return pltpu.make_async_copy(out.at[:, rows], out_hbm.at[:, rows], out_sems.at[at])

    def step(at, carry):
        waits[0](at)
        ids = [at * SIDE + i for i in range(SIDE)]
        results = [mul(mix[i], col) for i, col in zip(ids, columns(spec, ids))]
        for i, value in zip(ids, results):
            out[0, i] = value[:, :lanes].astype(BF16)
            out[1, i] = value[:, lanes:].astype(BF16)
        leave(at).start()
        return carry

    lax.fori_loop(0, parts, step, 0)
    settle(leave, parts)


def conv_phase(spec, filt, mix, unmix, waits, kept, product, leave):
    def step(at, carry):
        for wait in waits:
            wait(at)
        ids = [at * SIDE + i for i in range(SIDE)]
        seen = [mul(mix[i], col) for i, col in zip(ids, columns(spec, ids))]
        mixed = [packed(product(halves(filt[i]), halves(x))) for i, x in zip(ids, seen)]
        done = [mul(unmix[i], y) for i, y in zip(ids, mixed)]
        for i, x in zip(ids, seen):
            kept[i] = x.astype(BF16)
        leave(at).start()
        put_columns(spec, ids, done)
        return carry

    lax.fori_loop(0, filt.shape[0] // SIDE, step, 0)


def first_body(
    which, opening, closing, gain, taps, raw, mix_hbm, unmix_hbm, filt_hbm, kept_hbm, first_hbm,
    spec, v, mix, unmix, filt, sems, out_sems, kept, first
):
    waits = fetch([mix_hbm, unmix_hbm, filt_hbm.at[which]], [mix, unmix, filt], sems)
    leave_kept = leave_sides(kept, kept_hbm, out_sems, 0)
    leave_first = leave_rows(first, first_hbm, out_sems, 1)
    short_phase(raw, taps, v)
    open_phase(opening, lambda row: v[:, pl.ds(row, ROWS), :].astype(F32), spec)
    conv_phase(spec, filt, mix, unmix, waits, kept, cmul, leave_kept)
    g0 = gain[0:1, :][None]

    def write(at, row, value):
        rows = pl.ds(row, ROWS)
        first[:, rows, :] = g0 * v[:, rows, :].astype(F32) + value
        leave_first(at).start()

    close_phase(closing, spec, write)
    settle(leave_kept, kept.shape[0] // SIDE)
    settle(leave_first, first.shape[1] // ROWS)


def second_body(
    which, opening, closing, gain, taps, first, raw, mix_hbm, unmix_hbm, filt_hbm, kept_hbm, second_hbm, x1_hbm,
    spec, mid, mix, unmix, filt, sems, out_sems, kept, second, x1
):
    waits = fetch([mix_hbm, unmix_hbm, filt_hbm.at[which]], [mix, unmix, filt], sems)
    leave_kept = leave_sides(kept, kept_hbm, out_sems, 0)
    leave_second = leave_rows(second, second_hbm, out_sems, 1)
    leave_x1 = pltpu.make_async_copy(x1, x1_hbm, out_sems.at[2, 0])
    short_phase(raw, taps, x1)
    leave_x1.start()

    def read(row):
        rows = pl.ds(row, ROWS)
        value = x1[:, rows, :].astype(F32) * first[:, rows, :]
        mid[:, rows, :] = value
        return value

    open_phase(opening, read, spec)
    conv_phase(spec, filt, mix, unmix, waits, kept, cmul, leave_kept)
    g1 = gain[1:2, :][None]

    def write(at, row, value):
        rows = pl.ds(row, ROWS)
        second[:, rows, :] = (g1 * mid[:, rows, :] + value).astype(BF16)
        leave_second(at).start()

    close_phase(closing, spec, write)
    leave_x1.wait()
    settle(leave_kept, kept.shape[0] // SIDE)
    settle(leave_second, second.shape[1] // ROWS)


def back_second_body(
    which, opening, closing, gain, taps, bs, first, x1, mix_hbm, unmix_hbm, filt_hbm, kept_hbm, bf_hbm, grad_hbm,
    spec, bx1, mix, unmix, filt, sems, out_sems, kept, bf, grad_x1
):
    waits = fetch([mix_hbm, unmix_hbm, filt_hbm.at[which]], [mix, unmix, filt], sems)
    leave_kept = leave_sides(kept, kept_hbm, out_sems, 0)
    leave_bf = leave_rows(bf, bf_hbm, out_sems, 1)
    leave_grad = leave_sides(grad_x1, grad_hbm, out_sems, 2)
    open_phase(opening, lambda row: bs[:, pl.ds(row, ROWS), :].astype(F32), spec)
    conv_phase(spec, filt, mix, unmix, waits, kept, conj_mul, leave_kept)
    g1 = gain[1:2, :][None]

    def write(at, row, value):
        rows = pl.ds(row, ROWS)
        back_middle = g1 * bs[:, rows, :].astype(F32) + value
        bf[:, rows, :] = back_middle * x1[:, rows, :].astype(F32)
        bx1[:, rows, :] = (back_middle * first[:, rows, :]).astype(BF16)
        leave_bf(at).start()

    close_phase(closing, spec, write)
    short_back_phase(bx1, taps, grad_x1, leave_grad)
    settle(leave_kept, kept.shape[0] // SIDE)
    settle(leave_bf, bf.shape[1] // ROWS)
    settle(leave_grad, kept.shape[0] // SIDE)


def back_first_body(
    which, opening, closing, gain, taps, bf, mix_hbm, unmix_hbm, filt_hbm, kept_hbm, grad_hbm,
    spec, bv, mix, unmix, filt, sems, out_sems, kept, grad_v
):
    waits = fetch([mix_hbm, unmix_hbm, filt_hbm.at[which]], [mix, unmix, filt], sems)
    leave_kept = leave_sides(kept, kept_hbm, out_sems, 0)
    leave_grad = leave_sides(grad_v, grad_hbm, out_sems, 1)
    open_phase(opening, lambda row: bf[:, pl.ds(row, ROWS), :], spec)
    conv_phase(spec, filt, mix, unmix, waits, kept, conj_mul, leave_kept)
    g0 = gain[0:1, :][None]

    def write(at, row, value):
        rows = pl.ds(row, ROWS)
        bv[:, rows, :] = (g0 * bf[:, rows, :] + value).astype(BF16)

    close_phase(closing, spec, write)
    short_back_phase(bv, taps, grad_v, leave_grad)
    settle(leave_kept, kept.shape[0] // SIDE)
    settle(leave_grad, kept.shape[0] // SIDE)


def grad_body(scale, closing, unmix_hbm, v_hbm, m_hbm, c_hbm, b_hbm, out_hbm, spec, closed, out, unmix, pieces, sems, out_sems):
    outer, inner, both = closed.shape
    lanes = both // 2
    steps = outer // SIDE
    slots = unmix.shape[0]

    def copies(at):
        rows, slot = pl.ds(at * SIDE, SIDE), lax.rem(at, slots)
        found = [pltpu.make_async_copy(unmix_hbm.at[rows], unmix.at[slot], sems.at[0, slot])]
        for which, source in enumerate((v_hbm, m_hbm, c_hbm, b_hbm)):
            target = pieces.at[which, slot]
            found.append(pltpu.make_async_copy(source.at[rows], target, sems.at[1 + which, slot]))
        return found

    for at in range(min(slots, steps)):
        for copy in copies(at):
            copy.start()

    def step(at, carry):
        slot = lax.rem(at, slots)
        for copy in copies(at):
            copy.wait()
        mixed = []
        for i in range(SIDE):
            left, right = [packed(conj_mul(halves(pieces[k, slot, i]), halves(pieces[2 + k, slot, i]))) for k in range(2)]
            mixed.append(jnp.concatenate([left, right], axis=1))
        done = [mul(unmix[slot, i], y) for i, y in enumerate(mixed)]
        put_columns(spec, [at * SIDE + i for i in range(SIDE)], done)

        @pl.when(at + slots < steps)
        def _():
            for copy in copies(at + slots):
                copy.start()

        return carry

    lax.fori_loop(0, steps, step, 0)

    def write(at, row, value):
        closed[:, pl.ds(row, ROWS), :] = value * scale

    close_phase(closing, spec, write)
    parts = out_sems.shape[0]
    span = outer // parts

    def leave(part):
        columns_of = pl.ds(pl.multiple_of(part * span * inner, inner), span * inner)
        return pltpu.make_async_copy(out.at[:, :, columns_of], out_hbm.at[:, :, columns_of], out_sems.at[part])

    def turn(part, carry):
        for q in range(span):
            p = part * span + q
            here = pl.ds(pl.multiple_of(p * inner, inner), inner)
            out[0, :, here] = jnp.transpose(closed[p, :, :lanes])
            out[1, :, here] = jnp.transpose(closed[p, :, lanes:])
        leave(part).start()
        return carry

    lax.fori_loop(0, parts, turn, 0)

    settle(leave, parts)


params = pltpu.CompilerParams(vmem_limit_bytes=58 << 20)
VMEM = pl.BlockSpec(memory_space=pltpu.VMEM)
ANY = pl.BlockSpec(memory_space=pl.ANY)


def table_buffer(outer):
    return pltpu.VMEM((outer, 2 * INNER, 2 * INNER), BF16)


def spectrum(outer, lanes):
    return (outer, 2 * INNER, lanes)


def cost(us):
    return pl.CostEstimate(flops=int(us * 0.8e6), bytes_accessed=int(us * 1e5), transcendentals=0)


def filter_spectra(tables, filters):
    opening, _, mix, _ = tables
    _, lanes, length = filters.shape
    outer = length // INNER
    steps = outer // SIDE
    shape = (2,) + spectrum(outer, lanes)
    return pl.pallas_call(
        filters_body,
        in_specs=[VMEM, ANY, ANY],
        out_specs=ANY,
        out_shape=jax.ShapeDtypeStruct(shape, BF16),
        scratch_shapes=[
            pltpu.VMEM((2 * outer, INNER, 2 * lanes), F32),
            pltpu.VMEM((outer, INNER, 2 * lanes), F32),
            pltpu.VMEM(filters.shape, F32),
            table_buffer(outer),
            pltpu.VMEM(shape, BF16),
            pltpu.SemaphoreType.DMA((1, steps)),
            pltpu.SemaphoreType.DMA((steps,)),
            pltpu.SemaphoreType.DMA((steps,)),
        ],
        compiler_params=params,
        cost_estimate=cost(24),
        name="filter_spectra",
    )(opening, mix, filters)


def conv_pass(name, body, which, tables, gain, taps, filt, signals, kinds, hold):
    opening, closing, mix, unmix = tables
    outer, inner, lanes = signals[0].shape
    shape = (outer, inner, lanes)
    spec = spectrum(outer, lanes)
    return pl.pallas_call(
        functools.partial(body, which),
        in_specs=[VMEM] * (4 + len(signals)) + [ANY] * 3,
        out_specs=[ANY] * (1 + len(kinds)),
        out_shape=[jax.ShapeDtypeStruct(spec, BF16)] + [jax.ShapeDtypeStruct(shape, kind) for kind in kinds],
        scratch_shapes=[pltpu.VMEM((2 * outer, inner, lanes), F32)]
        + [pltpu.VMEM(shape, hold)]
        + [table_buffer(outer), table_buffer(outer), pltpu.VMEM(spec, BF16)]
        + [pltpu.SemaphoreType.DMA((3, outer // SIDE))]
        + [pltpu.SemaphoreType.DMA((3, max(outer // SIDE, inner // ROWS)))]
        + [pltpu.VMEM(spec, BF16)]
        + [pltpu.VMEM(shape, kind) for kind in kinds],
        compiler_params=params,
        cost_estimate=cost(20),
        name=name,
    )(opening, closing, gain, taps, *signals, mix, unmix, filt)


def grad_pass(scale, tables, spec_v, spec_m, spec_c, spec_b):
    _, closing, _, unmix = tables
    outer, _, lanes = spec_v.shape
    length = outer * INNER
    slots = 3
    return pl.pallas_call(
        functools.partial(grad_body, scale),
        in_specs=[VMEM] + [ANY] * 5,
        out_specs=ANY,
        out_shape=jax.ShapeDtypeStruct((2, lanes, length), F32),
        scratch_shapes=[
            pltpu.VMEM((2 * outer, INNER, 2 * lanes), F32),
            pltpu.VMEM((outer, INNER, 2 * lanes), F32),
            pltpu.VMEM((2, lanes, length), F32),
            pltpu.VMEM((slots, SIDE, 2 * INNER, 2 * INNER), BF16),
            pltpu.VMEM((4, slots, SIDE, 2 * INNER, lanes), BF16),
            pltpu.SemaphoreType.DMA((5, slots)),
            pltpu.SemaphoreType.DMA((8,)),
        ],
        compiler_params=params,
        cost_estimate=cost(28),
        name="filter_grads",
    )(closing, unmix, spec_v, spec_m, spec_c, spec_b)


def split_body(source, target):
    count, _, width = target.shape
    for i in range(count):
        target[i] = source[0, :, i * width : (i + 1) * width]


def rows_of(frames):
    return min(frames, 256)


def flat_width(block):
    count, frames, width = block.shape
    return jnp.swapaxes(block, 0, 1).reshape(frames, count * width)


def split_flat(block, count):
    frames, local_width = block.shape
    return jnp.swapaxes(block.reshape(frames, count, local_width // count), 0, 1)


def split_width(block, count, at):
    _, frames, local_width = block.shape
    width = local_width // count
    if width % 128:
        return split_flat(block[at], count)
    rows = rows_of(frames)
    return pl.pallas_call(
        split_body,
        grid=(frames // rows,),
        in_specs=[pl.BlockSpec((1, rows, local_width), lambda i: (at, i, 0))],
        out_specs=pl.BlockSpec((count, rows, width), lambda i: (0, i, 0)),
        out_shape=jax.ShapeDtypeStruct((count, frames, width), block.dtype),
        compiler_params=params,
        cost_estimate=cost(2),
        name="split_width",
    )(block)


def join_body(a, b, flat, halo, taps, out, carry):
    count, rows, width = a.shape

    @pl.when(pl.program_id(0) == 0)
    def _():
        carry[...] = halo[...]

    for i in range(count):
        lanes = slice(i * width, (i + 1) * width)
        out[0, :, lanes] = a[i]
        out[1, :, lanes] = b[i]
        now = flat[:, lanes].astype(F32)
        wide = jnp.concatenate([now, carry[:, lanes]], axis=0)
        total = taps[0:1, lanes] * now
        for j in (1, 2):
            total = total + taps[j : j + 1, lanes] * wide[j : j + rows]
        out[2, :, lanes] = total.astype(BF16)
        carry[:, lanes] = now[:SUB]


def join_width(a, b, flat, halo, taps):
    count, frames, width = a.shape
    if width % 128:
        wide = jnp.concatenate([flat, halo], axis=0).astype(F32)
        third = sum(taps[j][None] * wide[j : j + frames] for j in range(3)).astype(BF16)
        return jnp.stack([flat_width(a), flat_width(b), third])
    rows = rows_of(frames)
    last = frames // rows - 1
    halo = jnp.pad(halo.astype(F32), ((0, SUB - halo.shape[0]), (0, 0)))
    split = pl.BlockSpec((count, rows, width), lambda i: (0, last - i, 0))
    return pl.pallas_call(
        join_body,
        grid=(frames // rows,),
        in_specs=[
            split,
            split,
            pl.BlockSpec((rows, count * width), lambda i: (last - i, 0)),
            pl.BlockSpec(halo.shape, lambda i: (0, 0)),
            pl.BlockSpec(taps.shape, lambda i: (0, 0)),
        ],
        out_specs=pl.BlockSpec((3, rows, count * width), lambda i: (0, last - i, 0)),
        out_shape=jax.ShapeDtypeStruct((3, frames, count * width), BF16),
        scratch_shapes=[pltpu.VMEM(halo.shape, F32)],
        compiler_params=params,
        cost_estimate=cost(5),
        name="join_width",
    )(a, b, flat, halo, taps)


def output_body(second, x2, weight, out, gated):
    count, frames, width = second.shape
    rows = min(frames, 512)

    @pl.when(pl.program_id(0) == 0)
    def _():
        for i in range(count):
            lanes = slice(i * width, (i + 1) * width)
            gated[:, lanes] = (x2[:, lanes].astype(F32) * second[i].astype(F32)).astype(BF16)

    def step(at, carry):
        here = pl.ds(pl.multiple_of(at * rows, rows), rows)
        out[here, :] = mul(gated[here, :], weight[...]).astype(BF16)
        return carry

    lax.fori_loop(0, frames // rows, step, 0)


def output_partial(second, x2, weight):
    count, frames, width = second.shape
    local_width, model = weight.shape
    if width % 128:
        gated = (x2.astype(F32) * flat_width(second).astype(F32)).astype(BF16)
        return mul(gated, weight).astype(BF16)
    cols = 512
    return pl.pallas_call(
        output_body,
        grid=(model // cols,),
        in_specs=[
            pl.BlockSpec(second.shape, lambda i: (0, 0, 0)),
            pl.BlockSpec(x2.shape, lambda i: (0, 0)),
            pl.BlockSpec((local_width, cols), lambda i: (0, i)),
        ],
        out_specs=pl.BlockSpec((frames, cols), lambda i: (0, i)),
        out_shape=jax.ShapeDtypeStruct((frames, model), BF16),
        scratch_shapes=[pltpu.VMEM((frames, local_width), BF16)],
        compiler_params=params,
        cost_estimate=cost(12),
        name="output_partial",
    )(second, x2, weight)


def back_gate_body(
    place, gathered, own, right1, left1, right2, left2, far, weight, x2, second, bs, bx2, blocks, sems
):
    pairs, frames, width = second.shape
    cut, depth = own.shape
    me = place[0]
    last = N_TP - 1

    def copy(source, slot):
        return pltpu.make_async_copy(source, blocks.at[slot], sems.at[slot])

    def fetch_one(slot, where, source, other):
        @pl.when(where)
        def _():
            copy(source, slot).start()

        @pl.when(jnp.logical_not(where))
        def _():
            copy(other, slot).start()

    def finish(here, full):
        full = full.astype(BF16).astype(F32)
        for i in range(pairs):
            lanes = slice(i * width, (i + 1) * width)
            bs[i, here, :] = (full[:, lanes] * x2[here, lanes].astype(F32)).astype(BF16)
            bx2[here, lanes] = (full[:, lanes] * second[i, here, :].astype(F32)).astype(BF16)

    def times(left, right):
        return lax.dot_general(left, right, (((1,), (1,)), ((), ())), preferred_element_type=F32)

    @pl.when(pl.program_id(0) == 0)
    def _():
        copy(own, 0).start()
        fetch_one(1, me == 0, far, right1)
        fetch_one(2, me == last, far, left1)
        fetch_one(3, me <= 1, left2, right2)
        for slot in range(N_TP):
            copy(own, slot).wait()

    rows = (frames - cut) // 2

    def step(at, carry):
        there = pl.ds(pl.multiple_of(at * rows, ROWS), rows)
        finish(pl.ds(pl.multiple_of(cut + at * rows, ROWS), rows), times(gathered[there, :], weight[...]))
        return carry

    lax.fori_loop(0, 2, step, 0)
    full = None
    for slot, block in enumerate(
        [
            me,
            jnp.where(me == 0, last, me - 1),
            jnp.where(me == last, 0, me + 1),
            jnp.where(me <= 1, me + 2, me - 2),
        ]
    ):
        there = pl.ds(pl.multiple_of(block * depth, depth), depth)
        part = times(blocks[slot], weight[:, there])
        full = part if full is None else full + part
    finish(pl.ds(0, cut), full)


def back_gate(gathered, landed, weight, x2, second):
    count, frames, width = second.shape
    local_width, model = weight.shape
    pairs = 2
    wide = pairs * width
    flat = pl.BlockSpec((frames, wide), lambda i: (0, i))
    split = pl.BlockSpec((pairs, frames, width), lambda i: (i, 0, 0))
    return pl.pallas_call(
        back_gate_body,
        grid=(count // pairs,),
        in_specs=[pl.BlockSpec(memory_space=pltpu.SMEM), pl.BlockSpec(gathered.shape, lambda i: (0, 0))]
        + [ANY] * 6
        + [pl.BlockSpec((wide, model), lambda i: (i, 0)), flat, split],
        out_specs=[split, flat],
        out_shape=[
            jax.ShapeDtypeStruct((count, frames, width), BF16),
            jax.ShapeDtypeStruct((frames, local_width), BF16),
        ],
        scratch_shapes=[pltpu.VMEM((N_TP,) + landed[0].shape, BF16), pltpu.SemaphoreType.DMA((N_TP,))],
        compiler_params=params,
        cost_estimate=cost(14),
        name="back_gate",
    )(lax.axis_index("tp").reshape(1), gathered, *landed, weight, x2, second)


def back_gate_plain(gathered, weight, x2, second):
    full = lax.dot_general(gathered, weight, (((1,), (1,)), ((), ())), preferred_element_type=F32)
    full = full.astype(BF16).astype(F32)
    bs = split_flat((full * x2.astype(F32)).astype(BF16), second.shape[0])
    return bs, (full * flat_width(second).astype(F32)).astype(BF16)


def send(block, *pairs):
    return lax.ppermute(block, "tp", pairs)


def after(value, *others):
    return lax.optimization_barrier((value, *others))[0]


def swap(block):
    return lax.all_to_all(block, "seq", split_axis=0, concat_axis=0, tiled=True)


def to_frames(block):
    count = lax.axis_size("seq")
    length, width = block.shape
    return swap(block.reshape(count, length // count, width))


def neighbour_rows(rows, shift):
    count = lax.axis_size("seq")
    pairs = [(i, i + shift) for i in range(count) if 0 <= i + shift < count]
    return lax.ppermute(rows, "seq", pairs)


def short_filter(block, before, taps):
    length = block.shape[0]
    wide = jnp.concatenate([before, block], axis=0).astype(F32)
    return sum(taps[j][None] * wide[2 - j : 2 - j + length] for j in range(3)).astype(BF16)


def local(projected, short_kernel, filters, skip_gain, out_weight, out_grad):
    _, frames, _, local_width = projected.shape
    _, width, length = filters.shape
    count = lax.axis_size("seq")
    outer = length // INNER
    grid3 = (outer, INNER, width)
    scale = float(length) ** -0.5
    mine = lax.axis_index("seq") * width
    taps = lax.dynamic_slice_in_dim(short_kernel, mine, width, axis=2)
    tables = transform_tables(outer)

    branches = jnp.transpose(projected[0], (1, 0, 2))
    before_x2 = neighbour_rows(branches[2, frames - 2 :], 1)
    raw_v = swap(after(split_width(branches, count, 0), before_x2)).reshape(grid3)
    cut = frames // 8
    direct = width % 128 == 0 and lax.axis_size("tp") == N_TP and cut % ROWS == 0
    own = out_grad[0]
    if direct:
        gathered = lax.all_gather(own[cut:], "tp", axis=1, tiled=True)
        own = own[:cut]
        near = send(own, (0, 1), (1, 2), (2, 3)), send(own, (1, 0), (2, 1), (3, 2))
        next_but_one = send(own, (0, 2), (1, 3)), send(own, (2, 0), (3, 1))
        far = send(own, (0, 3), (3, 0))
    else:
        gathered = lax.all_gather(own, "tp", axis=1, tiled=True)
        near = next_but_one = far = ()
    filt = filter_spectra(tables, filters)
    raw_v, filt, near = lax.optimization_barrier((raw_v, filt, near))
    raw_x1 = swap(after(split_width(branches, count, 1), raw_v)).reshape(grid3)

    spec_v, first = conv_pass("first", first_body, 0, tables, skip_gain, taps[0], filt, [raw_v], [F32], BF16)
    raw_x1, first, next_but_one = lax.optimization_barrier((raw_x1, first, next_but_one))
    spec_m, second, x1 = conv_pass(
        "second", second_body, 1, tables, skip_gain, taps[1], filt, [first, raw_x1], [BF16, BF16], F32
    )
    branch_x2, second, far = lax.optimization_barrier((branches[2], second, far))
    x2 = short_filter(branch_x2, before_x2, short_kernel[2])
    second = to_frames(second.reshape(length, width))
    partial = output_partial(second, x2, out_weight)
    output = lax.psum_scatter(partial, "tp", scatter_dimension=1, tiled=True)[None]

    gathered, _ = lax.optimization_barrier((gathered, partial))
    if direct:
        bs, bx2 = back_gate(gathered, (own, *near, *next_but_one, far), out_weight, x2, second)
    else:
        bs, bx2 = back_gate_plain(gathered, out_weight, x2, second)
    bs, after_x2 = lax.optimization_barrier((swap(bs).reshape(grid3), neighbour_rows(bx2[:2], -1)))
    spec_b, bf, grad_x1 = conv_pass(
        "back_second", back_second_body, 1, tables, skip_gain, taps[1], filt, [bs, first, x1], [F32, BF16], BF16
    )
    moved1 = to_frames(grad_x1.reshape(length, width))
    spec_c, grad_v = conv_pass(
        "back_first", back_first_body, 0, tables, skip_gain, taps[0], filt, [bf], [BF16], BF16
    )
    moved1, grad_v, spec_b = lax.optimization_barrier((moved1, grad_v, spec_b))
    moved0 = to_frames(grad_v.reshape(length, width))
    filter_grad = grad_pass(scale, tables, spec_v, spec_m, spec_c, spec_b)

    joined = join_width(moved0, moved1, bx2, after_x2, short_kernel[2])
    projected_grad = jnp.transpose(joined, (1, 0, 2))[None]
    return (output, projected_grad, filter_grad)


def solution(mesh):
    in_specs = (
        P(None, "seq", None, "tp"),
        P(None, None, "tp"),
        P(None, ("tp", "seq"), None),
        P(None, ("tp", "seq")),
        P("tp", None),
        P(None, "seq", "tp"),
    )
    out_specs = (P(None, "seq", "tp"), P(None, "seq", None, "tp"), P(None, ("tp", "seq"), None))
    return jax.shard_map(local, mesh=mesh, in_specs=in_specs, out_specs=out_specs, check_vma=False)
```

```python
import functools
import math

import jax
import jax.numpy as jnp
import ml_dtypes
import numpy as np
from jax import lax
from jax.experimental import pallas as pl
from jax.experimental.pallas import tpu as pltpu
from jax.sharding import PartitionSpec as P

F32 = jnp.float32
BF16 = jnp.bfloat16
INNER = 128
SUB = 8
ROWS = 16
SIDE = 8
N_TP = 4


def spread_table(outer, scale):
    freq = np.arange(2 * outer * SUB)[:, None]
    time = np.arange(outer * SUB)[None, :]
    row = freq // SUB
    turn = 4 * outer
    phase = (4 * (row % outer) + 1) * (time // SUB) + outer * (row // outer)
    value = np.cos((phase % turn) * (2.0 * math.pi / turn)) * scale
    return np.where(freq % SUB == time % SUB, value, 0.0)


def transform_tables(outer):
    total = outer * INNER
    ids = np.arange(INNER)
    twist = 2.0 * math.pi * (np.arange(outer)[:, None] + 0.25) * ids[None, :] / total
    inner = 2.0 * math.pi * (ids[:, None] * ids[None, :] % INNER) / INNER
    angle = twist[:, None, :] + inner[None]
    cos, sin = np.cos(angle), np.sin(angle)
    mix = np.concatenate(
        [np.concatenate([cos, sin], axis=2), np.concatenate([-sin, cos], axis=2)], axis=1
    )
    opening = spread_table(outer, 1.0)
    closing = spread_table(outer, 1.0 / total).T
    unmix = np.swapaxes(mix, 1, 2)
    return [jnp.asarray(np.ascontiguousarray(t).astype(ml_dtypes.bfloat16)) for t in (opening, closing, mix, unmix)]


def mul(a, b):
    return jnp.dot(a, b, preferred_element_type=F32)


def halves(spec):
    return spec[:INNER].astype(F32), spec[INNER:].astype(F32)


def cmul(a, b):
    (ar, ai), (br, bi) = a, b
    return ar * br - ai * bi, ar * bi + ai * br


def conj_mul(a, b):
    (ar, ai), (br, bi) = a, b
    return ar * br + ai * bi, ar * bi - ai * br


def packed(pair):
    return jnp.concatenate(pair, axis=0).astype(BF16)


def open_phase(opening, read, spec):
    twice, inner, lanes = spec.shape
    outer = twice // 2

    def step(at, carry):
        row = pl.multiple_of(at * ROWS, ROWS)
        signal = read(row)
        wide = jnp.concatenate([signal[:, :SUB], signal[:, SUB:]], axis=2)
        flat = wide.reshape(outer * SUB, 2 * lanes).astype(BF16)
        out = mul(opening[...], flat).reshape(twice, SUB, 2 * lanes)
        spec[:, pl.ds(row, SUB), :] = out[:, :, :lanes]
        spec[:, pl.ds(row + SUB, SUB), :] = out[:, :, lanes:]
        return carry

    lax.fori_loop(0, inner // ROWS, step, 0)


def close_phase(closing, spec, write):
    twice, inner, lanes = spec.shape
    outer = twice // 2

    def step(at, carry):
        row = pl.multiple_of(at * ROWS, ROWS)
        wide = jnp.concatenate([spec[:, pl.ds(row, SUB), :], spec[:, pl.ds(row + SUB, SUB), :]], axis=2)
        flat = wide.reshape(twice * SUB, 2 * lanes).astype(BF16)
        out = mul(closing[...], flat).reshape(outer, SUB, 2 * lanes)
        write(at, row, jnp.concatenate([out[:, :, :lanes], out[:, :, lanes:]], axis=1))
        return carry

    lax.fori_loop(0, inner // ROWS, step, 0)


def fetch(sources, buffers, sems):
    outer = buffers[0].shape[0]

    def piece(which, at):
        rows = pl.ds(at * SIDE, SIDE)
        return pltpu.make_async_copy(sources[which].at[rows], buffers[which].at[rows], sems.at[which, at])

    for at in range(outer // SIDE):
        for which in range(len(sources)):
            piece(which, at).start()
    return [lambda at, which=which: piece(which, at).wait() for which in range(len(sources))]


def columns(spec, ids):
    outer = spec.shape[0] // 2
    return [packed([spec[i], spec[outer + i]]) for i in ids]


def put_columns(spec, ids, values):
    outer = spec.shape[0] // 2
    for i, value in zip(ids, values):
        spec[i] = value[:INNER]
        spec[outer + i] = value[INNER:]


def short_phase(raw, taps, out):
    outer, inner, lanes = raw.shape

    def step(p, before):
        now = raw[p].astype(F32)
        wide = jnp.concatenate([before, now], axis=0)
        total = taps[0:1, :] * now
        for j in (1, 2):
            total = total + taps[j : j + 1, :] * wide[SUB - j : SUB - j + inner]
        out[p] = total.astype(BF16)
        return now[inner - SUB :]

    lax.fori_loop(0, outer, step, jnp.zeros((SUB, lanes), F32))


def short_back_phase(raw, taps, out, leave):
    outer, inner, lanes = raw.shape

    def step(at, after):
        p = outer - 1 - at
        now = raw[p].astype(F32)
        wide = jnp.concatenate([now, after], axis=0)
        total = taps[0:1, :] * now
        for j in (1, 2):
            total = total + taps[j : j + 1, :] * wide[j : j + inner]
        out[p] = total.astype(BF16)
        return now[:SUB]

    def group(at, after):
        for i in range(SIDE):
            after = step(at * SIDE + i, after)
        leave(outer // SIDE - 1 - at).start()
        return after

    lax.fori_loop(0, outer // SIDE, group, jnp.zeros((SUB, lanes), F32))


def leave_sides(buffer, target, sems, which):
    def copy(at):
        rows = pl.ds(at * SIDE, SIDE)
        return pltpu.make_async_copy(buffer.at[rows], target.at[rows], sems.at[which, at])

    return copy


def leave_rows(buffer, target, sems, which):
    def copy(at):
        rows = pl.ds(pl.multiple_of(at * ROWS, ROWS), ROWS)
        return pltpu.make_async_copy(buffer.at[:, rows], target.at[:, rows], sems.at[which, at])

    return copy


def settle(copy, steps):
    def step(at, carry):
        copy(at).wait()
        return carry

    lax.fori_loop(0, steps, step, 0)


def filters_body(opening, mix_hbm, filt_hbm, out_hbm, spec, sig, filt, mix, out, sems, filt_sems, out_sems):
    waits = fetch([mix_hbm], [mix], sems)
    outer, inner, both = sig.shape
    lanes = both // 2
    parts = outer // SIDE

    def arrive(part):
        frames = pl.ds(pl.multiple_of(part * SIDE * inner, SIDE * inner), SIDE * inner)
        return pltpu.make_async_copy(filt_hbm.at[:, :, frames], filt.at[:, :, frames], filt_sems.at[part])

    for part in range(parts):
        arrive(part).start()

    def turn(part, carry):
        arrive(part).wait()
        for q in range(SIDE):
            p = part * SIDE + q
            here = pl.ds(pl.multiple_of(p * inner, inner), inner)
            sig[p, :, :lanes] = jnp.transpose(filt[0, :, here])
            sig[p, :, lanes:] = jnp.transpose(filt[1, :, here])
        return carry

    lax.fori_loop(0, parts, turn, 0)
    open_phase(opening, lambda row: sig[:, pl.ds(row, ROWS), :], spec)

    def leave(at):
        rows = pl.ds(at * SIDE, SIDE)
        return pltpu.make_async_copy(out.at[:, rows], out_hbm.at[:, rows], out_sems.at[at])

    def step(at, carry):
        waits[0](at)
        ids = [at * SIDE + i for i in range(SIDE)]
        results = [mul(mix[i], col) for i, col in zip(ids, columns(spec, ids))]
        for i, value in zip(ids, results):
            out[0, i] = value[:, :lanes].astype(BF16)
            out[1, i] = value[:, lanes:].astype(BF16)
        leave(at).start()
        return carry

    lax.fori_loop(0, parts, step, 0)
    settle(leave, parts)


def conv_phase(spec, filt, mix, unmix, waits, kept, product, leave):
    def step(at, carry):
        for wait in waits:
            wait(at)
        ids = [at * SIDE + i for i in range(SIDE)]
        seen = [mul(mix[i], col) for i, col in zip(ids, columns(spec, ids))]
        mixed = [packed(product(halves(filt[i]), halves(x))) for i, x in zip(ids, seen)]
        done = [mul(unmix[i], y) for i, y in zip(ids, mixed)]
        for i, x in zip(ids, seen):
            kept[i] = x.astype(BF16)
        leave(at).start()
        put_columns(spec, ids, done)
        return carry

    lax.fori_loop(0, filt.shape[0] // SIDE, step, 0)


def first_body(
    which, opening, closing, gain, taps, raw, mix_hbm, unmix_hbm, filt_hbm, kept_hbm, first_hbm,
    spec, v, mix, unmix, filt, sems, out_sems, kept, first
):
    waits = fetch([mix_hbm, unmix_hbm, filt_hbm.at[which]], [mix, unmix, filt], sems)
    leave_kept = leave_sides(kept, kept_hbm, out_sems, 0)
    leave_first = leave_rows(first, first_hbm, out_sems, 1)
    short_phase(raw, taps, v)
    open_phase(opening, lambda row: v[:, pl.ds(row, ROWS), :].astype(F32), spec)
    conv_phase(spec, filt, mix, unmix, waits, kept, cmul, leave_kept)
    g0 = gain[0:1, :][None]

    def write(at, row, value):
        rows = pl.ds(row, ROWS)
        first[:, rows, :] = g0 * v[:, rows, :].astype(F32) + value
        leave_first(at).start()

    close_phase(closing, spec, write)
    settle(leave_kept, kept.shape[0] // SIDE)
    settle(leave_first, first.shape[1] // ROWS)


def second_body(
    which, opening, closing, gain, taps, first, raw, mix_hbm, unmix_hbm, filt_hbm, kept_hbm, second_hbm, x1_hbm,
    spec, mid, mix, unmix, filt, sems, out_sems, kept, second, x1
):
    waits = fetch([mix_hbm, unmix_hbm, filt_hbm.at[which]], [mix, unmix, filt], sems)
    leave_kept = leave_sides(kept, kept_hbm, out_sems, 0)
    leave_second = leave_rows(second, second_hbm, out_sems, 1)
    leave_x1 = pltpu.make_async_copy(x1, x1_hbm, out_sems.at[2, 0])
    short_phase(raw, taps, x1)
    leave_x1.start()

    def read(row):
        rows = pl.ds(row, ROWS)
        value = x1[:, rows, :].astype(F32) * first[:, rows, :]
        mid[:, rows, :] = value
        return value

    open_phase(opening, read, spec)
    conv_phase(spec, filt, mix, unmix, waits, kept, cmul, leave_kept)
    g1 = gain[1:2, :][None]

    def write(at, row, value):
        rows = pl.ds(row, ROWS)
        second[:, rows, :] = (g1 * mid[:, rows, :] + value).astype(BF16)
        leave_second(at).start()

    close_phase(closing, spec, write)
    leave_x1.wait()
    settle(leave_kept, kept.shape[0] // SIDE)
    settle(leave_second, second.shape[1] // ROWS)


def back_second_body(
    which, opening, closing, gain, taps, bs, first, x1, mix_hbm, unmix_hbm, filt_hbm, kept_hbm, bf_hbm, grad_hbm,
    spec, bx1, mix, unmix, filt, sems, out_sems, kept, bf, grad_x1
):
    waits = fetch([mix_hbm, unmix_hbm, filt_hbm.at[which]], [mix, unmix, filt], sems)
    leave_kept = leave_sides(kept, kept_hbm, out_sems, 0)
    leave_bf = leave_rows(bf, bf_hbm, out_sems, 1)
    leave_grad = leave_sides(grad_x1, grad_hbm, out_sems, 2)
    open_phase(opening, lambda row: bs[:, pl.ds(row, ROWS), :].astype(F32), spec)
    conv_phase(spec, filt, mix, unmix, waits, kept, conj_mul, leave_kept)
    g1 = gain[1:2, :][None]

    def write(at, row, value):
        rows = pl.ds(row, ROWS)
        back_middle = g1 * bs[:, rows, :].astype(F32) + value
        bf[:, rows, :] = back_middle * x1[:, rows, :].astype(F32)
        bx1[:, rows, :] = (back_middle * first[:, rows, :]).astype(BF16)
        leave_bf(at).start()

    close_phase(closing, spec, write)
    short_back_phase(bx1, taps, grad_x1, leave_grad)
    settle(leave_kept, kept.shape[0] // SIDE)
    settle(leave_bf, bf.shape[1] // ROWS)
    settle(leave_grad, kept.shape[0] // SIDE)


def back_first_body(
    which, opening, closing, gain, taps, bf, mix_hbm, unmix_hbm, filt_hbm, kept_hbm, grad_hbm,
    spec, bv, mix, unmix, filt, sems, out_sems, kept, grad_v
):
    waits = fetch([mix_hbm, unmix_hbm, filt_hbm.at[which]], [mix, unmix, filt], sems)
    leave_kept = leave_sides(kept, kept_hbm, out_sems, 0)
    leave_grad = leave_sides(grad_v, grad_hbm, out_sems, 1)
    open_phase(opening, lambda row: bf[:, pl.ds(row, ROWS), :], spec)
    conv_phase(spec, filt, mix, unmix, waits, kept, conj_mul, leave_kept)
    g0 = gain[0:1, :][None]

    def write(at, row, value):
        rows = pl.ds(row, ROWS)
        bv[:, rows, :] = (g0 * bf[:, rows, :] + value).astype(BF16)

    close_phase(closing, spec, write)
    short_back_phase(bv, taps, grad_v, leave_grad)
    settle(leave_kept, kept.shape[0] // SIDE)
    settle(leave_grad, kept.shape[0] // SIDE)


def grad_body(scale, closing, unmix_hbm, v_hbm, m_hbm, c_hbm, b_hbm, out_hbm, spec, closed, out, unmix, pieces, sems, out_sems):
    outer, inner, both = closed.shape
    lanes = both // 2
    steps = outer // SIDE
    slots = unmix.shape[0]

    def copies(at):
        rows, slot = pl.ds(at * SIDE, SIDE), lax.rem(at, slots)
        found = [pltpu.make_async_copy(unmix_hbm.at[rows], unmix.at[slot], sems.at[0, slot])]
        for which, source in enumerate((v_hbm, m_hbm, c_hbm, b_hbm)):
            target = pieces.at[which, slot]
            found.append(pltpu.make_async_copy(source.at[rows], target, sems.at[1 + which, slot]))
        return found

    for at in range(min(slots, steps)):
        for copy in copies(at):
            copy.start()

    def step(at, carry):
        slot = lax.rem(at, slots)
        for copy in copies(at):
            copy.wait()
        mixed = []
        for i in range(SIDE):
            left, right = [packed(conj_mul(halves(pieces[k, slot, i]), halves(pieces[2 + k, slot, i]))) for k in range(2)]
            mixed.append(jnp.concatenate([left, right], axis=1))
        done = [mul(unmix[slot, i], y) for i, y in enumerate(mixed)]
        put_columns(spec, [at * SIDE + i for i in range(SIDE)], done)

        @pl.when(at + slots < steps)
        def _():
            for copy in copies(at + slots):
                copy.start()

        return carry

    lax.fori_loop(0, steps, step, 0)

    def write(at, row, value):
        closed[:, pl.ds(row, ROWS), :] = value * scale

    close_phase(closing, spec, write)
    parts = out_sems.shape[0]
    span = outer // parts

    def leave(part):
        columns_of = pl.ds(pl.multiple_of(part * span * inner, inner), span * inner)
        return pltpu.make_async_copy(out.at[:, :, columns_of], out_hbm.at[:, :, columns_of], out_sems.at[part])

    def turn(part, carry):
        for q in range(span):
            p = part * span + q
            here = pl.ds(pl.multiple_of(p * inner, inner), inner)
            out[0, :, here] = jnp.transpose(closed[p, :, :lanes])
            out[1, :, here] = jnp.transpose(closed[p, :, lanes:])
        leave(part).start()
        return carry

    lax.fori_loop(0, parts, turn, 0)

    settle(leave, parts)


params = pltpu.CompilerParams(vmem_limit_bytes=58 << 20)
VMEM = pl.BlockSpec(memory_space=pltpu.VMEM)
ANY = pl.BlockSpec(memory_space=pl.ANY)


def table_buffer(outer):
    return pltpu.VMEM((outer, 2 * INNER, 2 * INNER), BF16)


def spectrum(outer, lanes):
    return (outer, 2 * INNER, lanes)


def cost(us):
    return pl.CostEstimate(flops=int(us * 0.8e6), bytes_accessed=int(us * 1e5), transcendentals=0)


def filter_spectra(tables, filters):
    opening, _, mix, _ = tables
    _, lanes, length = filters.shape
    outer = length // INNER
    steps = outer // SIDE
    shape = (2,) + spectrum(outer, lanes)
    return pl.pallas_call(
        filters_body,
        in_specs=[VMEM, ANY, ANY],
        out_specs=ANY,
        out_shape=jax.ShapeDtypeStruct(shape, BF16),
        scratch_shapes=[
            pltpu.VMEM((2 * outer, INNER, 2 * lanes), F32),
            pltpu.VMEM((outer, INNER, 2 * lanes), F32),
            pltpu.VMEM(filters.shape, F32),
            table_buffer(outer),
            pltpu.VMEM(shape, BF16),
            pltpu.SemaphoreType.DMA((1, steps)),
            pltpu.SemaphoreType.DMA((steps,)),
            pltpu.SemaphoreType.DMA((steps,)),
        ],
        compiler_params=params,
        cost_estimate=cost(24),
        name="filter_spectra",
    )(opening, mix, filters)


def conv_pass(name, body, which, tables, gain, taps, filt, signals, kinds, hold):
    opening, closing, mix, unmix = tables
    outer, inner, lanes = signals[0].shape
    shape = (outer, inner, lanes)
    spec = spectrum(outer, lanes)
    return pl.pallas_call(
        functools.partial(body, which),
        in_specs=[VMEM] * (4 + len(signals)) + [ANY] * 3,
        out_specs=[ANY] * (1 + len(kinds)),
        out_shape=[jax.ShapeDtypeStruct(spec, BF16)] + [jax.ShapeDtypeStruct(shape, kind) for kind in kinds],
        scratch_shapes=[pltpu.VMEM((2 * outer, inner, lanes), F32)]
        + [pltpu.VMEM(shape, hold)]
        + [table_buffer(outer), table_buffer(outer), pltpu.VMEM(spec, BF16)]
        + [pltpu.SemaphoreType.DMA((3, outer // SIDE))]
        + [pltpu.SemaphoreType.DMA((3, max(outer // SIDE, inner // ROWS)))]
        + [pltpu.VMEM(spec, BF16)]
        + [pltpu.VMEM(shape, kind) for kind in kinds],
        compiler_params=params,
        cost_estimate=cost(20),
        name=name,
    )(opening, closing, gain, taps, *signals, mix, unmix, filt)


def grad_pass(scale, tables, spec_v, spec_m, spec_c, spec_b):
    _, closing, _, unmix = tables
    outer, _, lanes = spec_v.shape
    length = outer * INNER
    slots = 3
    return pl.pallas_call(
        functools.partial(grad_body, scale),
        in_specs=[VMEM] + [ANY] * 5,
        out_specs=ANY,
        out_shape=jax.ShapeDtypeStruct((2, lanes, length), F32),
        scratch_shapes=[
            pltpu.VMEM((2 * outer, INNER, 2 * lanes), F32),
            pltpu.VMEM((outer, INNER, 2 * lanes), F32),
            pltpu.VMEM((2, lanes, length), F32),
            pltpu.VMEM((slots, SIDE, 2 * INNER, 2 * INNER), BF16),
            pltpu.VMEM((4, slots, SIDE, 2 * INNER, lanes), BF16),
            pltpu.SemaphoreType.DMA((5, slots)),
            pltpu.SemaphoreType.DMA((8,)),
        ],
        compiler_params=params,
        cost_estimate=cost(28),
        name="filter_grads",
    )(closing, unmix, spec_v, spec_m, spec_c, spec_b)


def split_body(source, target):
    count, _, width = target.shape
    for i in range(count):
        target[i] = source[0, :, i * width : (i + 1) * width]


def rows_of(frames):
    return min(frames, 256)


def flat_width(block):
    count, frames, width = block.shape
    return jnp.swapaxes(block, 0, 1).reshape(frames, count * width)


def split_flat(block, count):
    frames, local_width = block.shape
    return jnp.swapaxes(block.reshape(frames, count, local_width // count), 0, 1)


def split_width(block, count, at):
    _, frames, local_width = block.shape
    width = local_width // count
    if width % 128:
        return split_flat(block[at], count)
    rows = rows_of(frames)
    return pl.pallas_call(
        split_body,
        grid=(frames // rows,),
        in_specs=[pl.BlockSpec((1, rows, local_width), lambda i: (at, i, 0))],
        out_specs=pl.BlockSpec((count, rows, width), lambda i: (0, i, 0)),
        out_shape=jax.ShapeDtypeStruct((count, frames, width), block.dtype),
        compiler_params=params,
        cost_estimate=cost(2),
        name="split_width",
    )(block)


def filtered_body(flat, halo, taps, out, carry):
    rows, lanes = flat.shape
    width = min(lanes, 128)

    @pl.when(pl.program_id(0) == 0)
    def _():
        carry[...] = halo[...]

    for at in range(0, lanes, width):
        here = slice(at, at + width)
        now = flat[:, here].astype(F32)
        wide = jnp.concatenate([now, carry[:, here]], axis=0)
        total = taps[0:1, here] * now
        for j in (1, 2):
            total = total + taps[j : j + 1, here] * wide[j : j + rows]
        out[0, :, here] = total.astype(BF16)
        carry[:, here] = now[:SUB]


def filtered_branch(flat, halo, taps, at):
    frames, lanes = flat.shape
    rows = rows_of(frames)
    last = frames // rows - 1
    halo = jnp.pad(halo.astype(F32), ((0, SUB - halo.shape[0]), (0, 0)))
    return pl.pallas_call(
        filtered_body,
        grid=(frames // rows,),
        in_specs=[
            pl.BlockSpec((rows, lanes), lambda i: (last - i, 0)),
            pl.BlockSpec(halo.shape, lambda i: (0, 0)),
            pl.BlockSpec(taps.shape, lambda i: (0, 0)),
        ],
        out_specs=pl.BlockSpec((1, rows, lanes), lambda i: (at, last - i, 0)),
        out_shape=jax.ShapeDtypeStruct((3, frames, lanes), BF16),
        scratch_shapes=[pltpu.VMEM(halo.shape, F32)],
        compiler_params=params,
        cost_estimate=cost(3),
        name="filtered_branch",
    )(flat, halo, taps)


def place_body(block, _, out):
    count, rows, width = block.shape
    for i in range(count):
        out[0, :, i * width : (i + 1) * width] = block[i]


def place_branch(base, block, at):
    count, frames, width = block.shape
    if width % 128:
        return base.at[at].set(flat_width(block))
    rows = rows_of(frames)
    return pl.pallas_call(
        place_body,
        grid=(frames // rows,),
        in_specs=[pl.BlockSpec((count, rows, width), lambda i: (0, i, 0)), ANY],
        out_specs=pl.BlockSpec((1, rows, count * width), lambda i: (at, i, 0)),
        out_shape=jax.ShapeDtypeStruct(base.shape, base.dtype),
        input_output_aliases={1: 0},
        compiler_params=params,
        cost_estimate=cost(2),
        name="place_branch",
    )(block, base)


def output_body(low, second, x2, weight, out, gated):
    count, high, width = second.shape
    frames = high - low
    rows = next(r for r in (512, 448, frames) if frames % r == 0)

    @pl.when(pl.program_id(0) == 0)
    def _():
        for i in range(count):
            lanes = slice(i * width, (i + 1) * width)
            gated[:, lanes] = (x2[low:, lanes].astype(F32) * second[i, low:].astype(F32)).astype(BF16)

    def step(at, carry):
        here = pl.ds(pl.multiple_of(at * rows, ROWS), rows)
        out[here, :] = mul(gated[here, :], weight[...]).astype(BF16)
        return carry

    lax.fori_loop(0, frames // rows, step, 0)


def output_partial(second, x2, weight, low, high):
    count, frames, width = second.shape
    local_width, model = weight.shape
    if width % 128:
        gated = (x2.astype(F32) * flat_width(second).astype(F32)).astype(BF16)
        return mul(gated[low:high], weight).astype(BF16)
    cols = 512
    return pl.pallas_call(
        functools.partial(output_body, low),
        grid=(model // cols,),
        in_specs=[
            pl.BlockSpec((count, high, width), lambda i: (0, 0, 0)),
            pl.BlockSpec((high, local_width), lambda i: (0, 0)),
            pl.BlockSpec((local_width, cols), lambda i: (0, i)),
        ],
        out_specs=pl.BlockSpec((high - low, cols), lambda i: (0, i)),
        out_shape=jax.ShapeDtypeStruct((high - low, model), BF16),
        scratch_shapes=[pltpu.VMEM((high - low, local_width), BF16)],
        compiler_params=params,
        cost_estimate=cost(12),
        name="output_partial",
    )(second, x2, weight)


def back_gate_body(gathered, weight, x2, second, bs, bx2):
    pairs, frames, width = second.shape
    rows = min(frames, 512)

    def step(at, carry):
        here = pl.ds(pl.multiple_of(at * rows, rows), rows)
        full = lax.dot_general(
            gathered[here, :], weight[...], (((1,), (1,)), ((), ())), preferred_element_type=F32
        )
        full = full.astype(BF16).astype(F32)
        for i in range(pairs):
            lanes = slice(i * width, (i + 1) * width)
            bs[i, here, :] = (full[:, lanes] * x2[here, lanes].astype(F32)).astype(BF16)
            bx2[here, lanes] = (full[:, lanes] * second[i, here, :].astype(F32)).astype(BF16)
        return carry

    lax.fori_loop(0, frames // rows, step, 0)


def back_gate(gathered, weight, x2, second):
    count, frames, width = second.shape
    local_width, model = weight.shape
    if width % 128:
        full = lax.dot_general(gathered, weight, (((1,), (1,)), ((), ())), preferred_element_type=F32)
        full = full.astype(BF16).astype(F32)
        bs = split_flat((full * x2.astype(F32)).astype(BF16), count)
        return bs, (full * flat_width(second).astype(F32)).astype(BF16)
    pairs = 2
    wide = pairs * width
    flat = pl.BlockSpec((frames, wide), lambda i: (0, i))
    split = pl.BlockSpec((pairs, frames, width), lambda i: (i, 0, 0))
    return pl.pallas_call(
        back_gate_body,
        grid=(count // pairs,),
        in_specs=[
            pl.BlockSpec(gathered.shape, lambda i: (0, 0)),
            pl.BlockSpec((wide, model), lambda i: (i, 0)),
            flat,
            split,
        ],
        out_specs=[split, flat],
        out_shape=[
            jax.ShapeDtypeStruct((count, frames, width), BF16),
            jax.ShapeDtypeStruct((frames, local_width), BF16),
        ],
        compiler_params=params,
        cost_estimate=cost(14),
        name="back_gate",
    )(gathered, weight, x2, second)


def after(value, *others):
    return lax.optimization_barrier((value, *others))[0]


def send(block, *pairs):
    return lax.ppermute(block, "tp", pairs)


def added(*blocks):
    return sum(block.astype(F32) for block in blocks).astype(BF16)


def cut_columns(block, start, width):
    return lax.dynamic_slice_in_dim(block, start, width, axis=1)


def swap(block):
    return lax.all_to_all(block, "seq", split_axis=0, concat_axis=0, tiled=True)


def to_frames(block):
    count = lax.axis_size("seq")
    length, width = block.shape
    return swap(block.reshape(count, length // count, width))


def neighbour_rows(rows, shift):
    count = lax.axis_size("seq")
    pairs = [(i, i + shift) for i in range(count) if 0 <= i + shift < count]
    return lax.ppermute(rows, "seq", pairs)


def short_filter(block, before, taps):
    length = block.shape[0]
    wide = jnp.concatenate([before, block], axis=0).astype(F32)
    return sum(taps[j][None] * wide[2 - j : 2 - j + length] for j in range(3)).astype(BF16)


def local(projected, short_kernel, filters, skip_gain, out_weight, out_grad):
    _, frames, _, local_width = projected.shape
    _, width, length = filters.shape
    count = lax.axis_size("seq")
    outer = length // INNER
    grid3 = (outer, INNER, width)
    scale = float(length) ** -0.5
    mine = lax.axis_index("seq") * width
    taps = lax.dynamic_slice_in_dim(short_kernel, mine, width, axis=2)
    tables = transform_tables(outer)

    branches = jnp.transpose(projected[0], (1, 0, 2))
    before_x2 = neighbour_rows(branches[2, frames - 2 :], 1)
    raw_v = swap(after(split_width(branches, count, 0), before_x2)).reshape(grid3)
    gathered = lax.all_gather(out_grad[0], "tp", axis=1, tiled=True)
    filt = filter_spectra(tables, filters)
    raw_v = after(raw_v, filt)
    raw_x1 = swap(after(split_width(branches, count, 1), raw_v)).reshape(grid3)

    spec_v, first = conv_pass("first", first_body, 0, tables, skip_gain, taps[0], filt, [raw_v], [F32], BF16)
    raw_x1, first = lax.optimization_barrier((raw_x1, first))
    spec_m, second, x1 = conv_pass(
        "second", second_body, 1, tables, skip_gain, taps[1], filt, [first, raw_x1], [BF16, BF16], F32
    )
    branch_x2, second = lax.optimization_barrier((branches[2], second))
    x2 = short_filter(branch_x2, before_x2, short_kernel[2])
    second = to_frames(second.reshape(length, width))
    cut = frames // 8
    direct = width % 128 == 0 and lax.axis_size("tp") == N_TP and cut % ROWS == 0
    if direct:
        part = local_width
        me = lax.axis_index("tp")
        early = me == 1
        head = output_partial(second, x2, out_weight, 0, cut)
        handed = send(cut_columns(head, jnp.where(me == 0, part, 0), 3 * part), (0, 1), (3, 2))
        rest = output_partial(second, x2, out_weight, cut, frames)
        handed, rest = lax.optimization_barrier((handed, rest))
        crossing = send(
            added(
                cut_columns(head, jnp.where(early, 2 * part, 0), 2 * part),
                cut_columns(handed, jnp.where(early, part, 0), 2 * part),
            ),
            (1, 2),
            (2, 1),
        )
    else:
        rest = output_partial(second, x2, out_weight, 0, frames)
    output = lax.psum_scatter(rest, "tp", scatter_dimension=1, tiled=True)

    gathered, _ = lax.optimization_barrier((gathered, rest))
    bs, bx2 = back_gate(gathered, out_weight, x2, second)
    after_x2 = neighbour_rows(bx2[:2], -1)
    bs, after_x2 = lax.optimization_barrier((swap(bs).reshape(grid3), after_x2))
    spec_b, bf, grad_x1 = conv_pass(
        "back_second", back_second_body, 1, tables, skip_gain, taps[1], filt, [bs, first, x1], [F32, BF16], BF16
    )
    if direct:
        crossing, grad_x1 = lax.optimization_barrier((crossing, grad_x1))
        outward = send(
            added(
                cut_columns(head, jnp.where(early, 0, 3 * part), part),
                cut_columns(crossing, jnp.where(early, 0, part), part),
            ),
            (1, 0),
            (2, 3),
        )
    moved1 = to_frames(grad_x1.reshape(length, width))
    spec_c, grad_v = conv_pass(
        "back_first", back_first_body, 0, tables, skip_gain, taps[0], filt, [bf], [BF16], BF16
    )
    moved1, grad_v, spec_b = lax.optimization_barrier((moved1, grad_v, spec_b))
    bx2, grad_v = lax.optimization_barrier((bx2, grad_v))
    if direct:
        outward, grad_v = lax.optimization_barrier((outward, grad_v))
    moved0 = to_frames(grad_v.reshape(length, width))
    filter_grad = grad_pass(scale, tables, spec_v, spec_m, spec_c, spec_b)

    if width % 128:
        wide = jnp.concatenate([bx2, after_x2], axis=0).astype(F32)
        third = sum(short_kernel[2, j][None] * wide[j : j + frames] for j in range(3)).astype(BF16)
        joined = jnp.stack([third] * 3)
    else:
        joined = filtered_branch(bx2, after_x2, short_kernel[2], 2)
    joined = place_branch(joined, moved1, 1)
    if direct:
        early_rows = added(
            cut_columns(head, me * part, part),
            cut_columns(handed, jnp.where(early, 0, 2 * part), part),
            cut_columns(crossing, jnp.where(early, part, 0), part),
            outward,
        )
        output = jnp.concatenate([early_rows, output], axis=0)
    moved0, joined, _ = lax.optimization_barrier((moved0, joined, filter_grad))
    joined = place_branch(joined, moved0, 0)
    output = output[None]
    projected_grad = jnp.transpose(joined, (1, 0, 2))[None]
    return (output, projected_grad, filter_grad)


def solution(mesh):
    in_specs = (
        P(None, "seq", None, "tp"),
        P(None, None, "tp"),
        P(None, ("tp", "seq"), None),
        P(None, ("tp", "seq")),
        P("tp", None),
        P(None, "seq", "tp"),
    )
    out_specs = (P(None, "seq", "tp"), P(None, "seq", None, "tp"), P(None, ("tp", "seq"), None))
    return jax.shard_map(local, mesh=mesh, in_specs=in_specs, out_specs=out_specs, check_vma=False)
```

```python
import functools
import math

import jax
import jax.numpy as jnp
import ml_dtypes
import numpy as np
from jax import lax
from jax.experimental import pallas as pl
from jax.experimental.pallas import tpu as pltpu
from jax.sharding import PartitionSpec as P

F32 = jnp.float32
BF16 = jnp.bfloat16
INNER = 128
SUB = 8
ROWS = 16
SIDE = 8
N_TP = 4


def spread_table(outer, scale):
    freq = np.arange(2 * outer * SUB)[:, None]
    time = np.arange(outer * SUB)[None, :]
    row = freq // SUB
    turn = 4 * outer
    phase = (4 * (row % outer) + 1) * (time // SUB) + outer * (row // outer)
    value = np.cos((phase % turn) * (2.0 * math.pi / turn)) * scale
    return np.where(freq % SUB == time % SUB, value, 0.0)


def transform_tables(outer):
    total = outer * INNER
    ids = np.arange(INNER)
    twist = 2.0 * math.pi * (np.arange(outer)[:, None] + 0.25) * ids[None, :] / total
    inner = 2.0 * math.pi * (ids[:, None] * ids[None, :] % INNER) / INNER
    angle = twist[:, None, :] + inner[None]
    cos, sin = np.cos(angle), np.sin(angle)
    mix = np.concatenate(
        [np.concatenate([cos, sin], axis=2), np.concatenate([-sin, cos], axis=2)], axis=1
    )
    opening = spread_table(outer, 1.0)
    closing = spread_table(outer, 1.0 / total).T
    unmix = np.swapaxes(mix, 1, 2)
    return [jnp.asarray(np.ascontiguousarray(t).astype(ml_dtypes.bfloat16)) for t in (opening, closing, mix, unmix)]


def mul(a, b):
    return jnp.dot(a, b, preferred_element_type=F32)


def halves(spec):
    return spec[:INNER].astype(F32), spec[INNER:].astype(F32)


def cmul(a, b):
    (ar, ai), (br, bi) = a, b
    return ar * br - ai * bi, ar * bi + ai * br


def conj_mul(a, b):
    (ar, ai), (br, bi) = a, b
    return ar * br + ai * bi, ar * bi - ai * br


def packed(pair):
    return jnp.concatenate(pair, axis=0).astype(BF16)


def open_phase(opening, read, spec):
    twice, inner, lanes = spec.shape
    outer = twice // 2

    def step(at, carry):
        row = pl.multiple_of(at * ROWS, ROWS)
        signal = read(row)
        wide = jnp.concatenate([signal[:, :SUB], signal[:, SUB:]], axis=2)
        flat = wide.reshape(outer * SUB, 2 * lanes).astype(BF16)
        out = mul(opening[...], flat).reshape(twice, SUB, 2 * lanes)
        spec[:, pl.ds(row, SUB), :] = out[:, :, :lanes]
        spec[:, pl.ds(row + SUB, SUB), :] = out[:, :, lanes:]
        return carry

    lax.fori_loop(0, inner // ROWS, step, 0)


def close_phase(closing, spec, write):
    twice, inner, lanes = spec.shape
    outer = twice // 2

    def step(at, carry):
        row = pl.multiple_of(at * ROWS, ROWS)
        wide = jnp.concatenate([spec[:, pl.ds(row, SUB), :], spec[:, pl.ds(row + SUB, SUB), :]], axis=2)
        flat = wide.reshape(twice * SUB, 2 * lanes).astype(BF16)
        out = mul(closing[...], flat).reshape(outer, SUB, 2 * lanes)
        write(at, row, jnp.concatenate([out[:, :, :lanes], out[:, :, lanes:]], axis=1))
        return carry

    lax.fori_loop(0, inner // ROWS, step, 0)


def fetch(sources, buffers, sems):
    outer = buffers[0].shape[0]

    def piece(which, at):
        rows = pl.ds(at * SIDE, SIDE)
        return pltpu.make_async_copy(sources[which].at[rows], buffers[which].at[rows], sems.at[which, at])

    for at in range(outer // SIDE):
        for which in range(len(sources)):
            piece(which, at).start()
    return [lambda at, which=which: piece(which, at).wait() for which in range(len(sources))]


def columns(spec, ids):
    outer = spec.shape[0] // 2
    return [packed([spec[i], spec[outer + i]]) for i in ids]


def put_columns(spec, ids, values):
    outer = spec.shape[0] // 2
    for i, value in zip(ids, values):
        spec[i] = value[:INNER]
        spec[outer + i] = value[INNER:]


def short_phase(raw, taps, out):
    outer, inner, lanes = raw.shape

    def step(p, before):
        now = raw[p].astype(F32)
        wide = jnp.concatenate([before, now], axis=0)
        total = taps[0:1, :] * now
        for j in (1, 2):
            total = total + taps[j : j + 1, :] * wide[SUB - j : SUB - j + inner]
        out[p] = total.astype(BF16)
        return now[inner - SUB :]

    lax.fori_loop(0, outer, step, jnp.zeros((SUB, lanes), F32))


def short_back_phase(raw, taps, out, leave):
    outer, inner, lanes = raw.shape

    def step(at, after):
        p = outer - 1 - at
        now = raw[p].astype(F32)
        wide = jnp.concatenate([now, after], axis=0)
        total = taps[0:1, :] * now
        for j in (1, 2):
            total = total + taps[j : j + 1, :] * wide[j : j + inner]
        out[p] = total.astype(BF16)
        return now[:SUB]

    def group(at, after):
        for i in range(SIDE):
            after = step(at * SIDE + i, after)
        leave(outer // SIDE - 1 - at).start()
        return after

    lax.fori_loop(0, outer // SIDE, group, jnp.zeros((SUB, lanes), F32))


def leave_sides(buffer, target, sems, which):
    def copy(at):
        rows = pl.ds(at * SIDE, SIDE)
        return pltpu.make_async_copy(buffer.at[rows], target.at[rows], sems.at[which, at])

    return copy


def leave_rows(buffer, target, sems, which):
    def copy(at):
        rows = pl.ds(pl.multiple_of(at * ROWS, ROWS), ROWS)
        return pltpu.make_async_copy(buffer.at[:, rows], target.at[:, rows], sems.at[which, at])

    return copy


def settle(copy, steps):
    def step(at, carry):
        copy(at).wait()
        return carry

    lax.fori_loop(0, steps, step, 0)


def filters_body(opening, mix_hbm, filt_hbm, out_hbm, spec, sig, filt, mix, out, sems, filt_sems, out_sems):
    waits = fetch([mix_hbm], [mix], sems)
    outer, inner, both = sig.shape
    lanes = both // 2
    parts = outer // SIDE

    def arrive(part):
        frames = pl.ds(pl.multiple_of(part * SIDE * inner, SIDE * inner), SIDE * inner)
        return pltpu.make_async_copy(filt_hbm.at[:, :, frames], filt.at[:, :, frames], filt_sems.at[part])

    for part in range(parts):
        arrive(part).start()

    def turn(part, carry):
        arrive(part).wait()
        for q in range(SIDE):
            p = part * SIDE + q
            here = pl.ds(pl.multiple_of(p * inner, inner), inner)
            sig[p, :, :lanes] = jnp.transpose(filt[0, :, here])
            sig[p, :, lanes:] = jnp.transpose(filt[1, :, here])
        return carry

    lax.fori_loop(0, parts, turn, 0)
    open_phase(opening, lambda row: sig[:, pl.ds(row, ROWS), :], spec)

    def leave(at):
        rows = pl.ds(at * SIDE, SIDE)
        return pltpu.make_async_copy(out.at[:, rows], out_hbm.at[:, rows], out_sems.at[at])

    def step(at, carry):
        waits[0](at)
        ids = [at * SIDE + i for i in range(SIDE)]
        results = [mul(mix[i], col) for i, col in zip(ids, columns(spec, ids))]
        for i, value in zip(ids, results):
            out[0, i] = value[:, :lanes].astype(BF16)
            out[1, i] = value[:, lanes:].astype(BF16)
        leave(at).start()
        return carry

    lax.fori_loop(0, parts, step, 0)
    settle(leave, parts)


def conv_phase(spec, filt, mix, unmix, waits, kept, product, leave):
    def step(at, carry):
        for wait in waits:
            wait(at)
        ids = [at * SIDE + i for i in range(SIDE)]
        seen = [mul(mix[i], col) for i, col in zip(ids, columns(spec, ids))]
        mixed = [packed(product(halves(filt[i]), halves(x))) for i, x in zip(ids, seen)]
        done = [mul(unmix[i], y) for i, y in zip(ids, mixed)]
        for i, x in zip(ids, seen):
            kept[i] = x.astype(BF16)
        leave(at).start()
        put_columns(spec, ids, done)
        return carry

    lax.fori_loop(0, filt.shape[0] // SIDE, step, 0)


def first_body(
    which, opening, closing, gain, taps, raw, mix_hbm, unmix_hbm, filt_hbm, kept_hbm, first_hbm,
    spec, v, mix, unmix, filt, sems, out_sems, kept, first
):
    waits = fetch([mix_hbm, unmix_hbm, filt_hbm.at[which]], [mix, unmix, filt], sems)
    leave_kept = leave_sides(kept, kept_hbm, out_sems, 0)
    leave_first = leave_rows(first, first_hbm, out_sems, 1)
    short_phase(raw, taps, v)
    open_phase(opening, lambda row: v[:, pl.ds(row, ROWS), :].astype(F32), spec)
    conv_phase(spec, filt, mix, unmix, waits, kept, cmul, leave_kept)
    g0 = gain[0:1, :][None]

    def write(at, row, value):
        rows = pl.ds(row, ROWS)
        first[:, rows, :] = g0 * v[:, rows, :].astype(F32) + value
        leave_first(at).start()

    close_phase(closing, spec, write)
    settle(leave_kept, kept.shape[0] // SIDE)
    settle(leave_first, first.shape[1] // ROWS)


def second_body(
    which, opening, closing, gain, taps, first, raw, mix_hbm, unmix_hbm, filt_hbm, kept_hbm, second_hbm, x1_hbm,
    spec, mid, mix, unmix, filt, sems, out_sems, kept, second, x1
):
    waits = fetch([mix_hbm, unmix_hbm, filt_hbm.at[which]], [mix, unmix, filt], sems)
    leave_kept = leave_sides(kept, kept_hbm, out_sems, 0)
    leave_second = leave_rows(second, second_hbm, out_sems, 1)
    leave_x1 = pltpu.make_async_copy(x1, x1_hbm, out_sems.at[2, 0])
    short_phase(raw, taps, x1)
    leave_x1.start()

    def read(row):
        rows = pl.ds(row, ROWS)
        value = x1[:, rows, :].astype(F32) * first[:, rows, :]
        mid[:, rows, :] = value
        return value

    open_phase(opening, read, spec)
    conv_phase(spec, filt, mix, unmix, waits, kept, cmul, leave_kept)
    g1 = gain[1:2, :][None]

    def write(at, row, value):
        rows = pl.ds(row, ROWS)
        second[:, rows, :] = (g1 * mid[:, rows, :] + value).astype(BF16)
        leave_second(at).start()

    close_phase(closing, spec, write)
    leave_x1.wait()
    settle(leave_kept, kept.shape[0] // SIDE)
    settle(leave_second, second.shape[1] // ROWS)


def back_second_body(
    which, opening, closing, gain, taps, bs, first, x1, mix_hbm, unmix_hbm, filt_hbm, kept_hbm, bf_hbm, grad_hbm,
    spec, bx1, mix, unmix, filt, sems, out_sems, kept, bf, grad_x1
):
    waits = fetch([mix_hbm, unmix_hbm, filt_hbm.at[which]], [mix, unmix, filt], sems)
    leave_kept = leave_sides(kept, kept_hbm, out_sems, 0)
    leave_bf = leave_rows(bf, bf_hbm, out_sems, 1)
    leave_grad = leave_sides(grad_x1, grad_hbm, out_sems, 2)
    open_phase(opening, lambda row: bs[:, pl.ds(row, ROWS), :].astype(F32), spec)
    conv_phase(spec, filt, mix, unmix, waits, kept, conj_mul, leave_kept)
    g1 = gain[1:2, :][None]

    def write(at, row, value):
        rows = pl.ds(row, ROWS)
        back_middle = g1 * bs[:, rows, :].astype(F32) + value
        bf[:, rows, :] = back_middle * x1[:, rows, :].astype(F32)
        bx1[:, rows, :] = (back_middle * first[:, rows, :]).astype(BF16)
        leave_bf(at).start()

    close_phase(closing, spec, write)
    short_back_phase(bx1, taps, grad_x1, leave_grad)
    settle(leave_kept, kept.shape[0] // SIDE)
    settle(leave_bf, bf.shape[1] // ROWS)
    settle(leave_grad, kept.shape[0] // SIDE)


def back_first_body(
    which, opening, closing, gain, taps, bf, mix_hbm, unmix_hbm, filt_hbm, kept_hbm, grad_hbm,
    spec, bv, mix, unmix, filt, sems, out_sems, kept, grad_v
):
    waits = fetch([mix_hbm, unmix_hbm, filt_hbm.at[which]], [mix, unmix, filt], sems)
    leave_kept = leave_sides(kept, kept_hbm, out_sems, 0)
    leave_grad = leave_sides(grad_v, grad_hbm, out_sems, 1)
    open_phase(opening, lambda row: bf[:, pl.ds(row, ROWS), :], spec)
    conv_phase(spec, filt, mix, unmix, waits, kept, conj_mul, leave_kept)
    g0 = gain[0:1, :][None]

    def write(at, row, value):
        rows = pl.ds(row, ROWS)
        bv[:, rows, :] = (g0 * bf[:, rows, :] + value).astype(BF16)

    close_phase(closing, spec, write)
    short_back_phase(bv, taps, grad_v, leave_grad)
    settle(leave_kept, kept.shape[0] // SIDE)
    settle(leave_grad, kept.shape[0] // SIDE)


def grad_body(scale, closing, unmix_hbm, v_hbm, m_hbm, c_hbm, b_hbm, out_hbm, spec, closed, out, unmix, pieces, sems, out_sems):
    outer, inner, both = closed.shape
    lanes = both // 2
    steps = outer // SIDE
    slots = unmix.shape[0]

    def copies(at):
        rows, slot = pl.ds(at * SIDE, SIDE), lax.rem(at, slots)
        found = [pltpu.make_async_copy(unmix_hbm.at[rows], unmix.at[slot], sems.at[0, slot])]
        for which, source in enumerate((v_hbm, m_hbm, c_hbm, b_hbm)):
            target = pieces.at[which, slot]
            found.append(pltpu.make_async_copy(source.at[rows], target, sems.at[1 + which, slot]))
        return found

    for at in range(min(slots, steps)):
        for copy in copies(at):
            copy.start()

    def step(at, carry):
        slot = lax.rem(at, slots)
        for copy in copies(at):
            copy.wait()
        mixed = []
        for i in range(SIDE):
            left, right = [packed(conj_mul(halves(pieces[k, slot, i]), halves(pieces[2 + k, slot, i]))) for k in range(2)]
            mixed.append(jnp.concatenate([left, right], axis=1))
        done = [mul(unmix[slot, i], y) for i, y in enumerate(mixed)]
        put_columns(spec, [at * SIDE + i for i in range(SIDE)], done)

        @pl.when(at + slots < steps)
        def _():
            for copy in copies(at + slots):
                copy.start()

        return carry

    lax.fori_loop(0, steps, step, 0)

    def write(at, row, value):
        closed[:, pl.ds(row, ROWS), :] = value * scale

    close_phase(closing, spec, write)
    parts = out_sems.shape[0]
    span = outer // parts

    def leave(part):
        columns_of = pl.ds(pl.multiple_of(part * span * inner, inner), span * inner)
        return pltpu.make_async_copy(out.at[:, :, columns_of], out_hbm.at[:, :, columns_of], out_sems.at[part])

    def turn(part, carry):
        for q in range(span):
            p = part * span + q
            here = pl.ds(pl.multiple_of(p * inner, inner), inner)
            out[0, :, here] = jnp.transpose(closed[p, :, :lanes])
            out[1, :, here] = jnp.transpose(closed[p, :, lanes:])
        leave(part).start()
        return carry

    lax.fori_loop(0, parts, turn, 0)

    settle(leave, parts)


params = pltpu.CompilerParams(vmem_limit_bytes=58 << 20)
VMEM = pl.BlockSpec(memory_space=pltpu.VMEM)
ANY = pl.BlockSpec(memory_space=pl.ANY)


def table_buffer(outer):
    return pltpu.VMEM((outer, 2 * INNER, 2 * INNER), BF16)


def spectrum(outer, lanes):
    return (outer, 2 * INNER, lanes)


def cost(us):
    return pl.CostEstimate(flops=int(us * 0.8e6), bytes_accessed=int(us * 1e5), transcendentals=0)


def filter_spectra(tables, filters):
    opening, _, mix, _ = tables
    _, lanes, length = filters.shape
    outer = length // INNER
    steps = outer // SIDE
    shape = (2,) + spectrum(outer, lanes)
    return pl.pallas_call(
        filters_body,
        in_specs=[VMEM, ANY, ANY],
        out_specs=ANY,
        out_shape=jax.ShapeDtypeStruct(shape, BF16),
        scratch_shapes=[
            pltpu.VMEM((2 * outer, INNER, 2 * lanes), F32),
            pltpu.VMEM((outer, INNER, 2 * lanes), F32),
            pltpu.VMEM(filters.shape, F32),
            table_buffer(outer),
            pltpu.VMEM(shape, BF16),
            pltpu.SemaphoreType.DMA((1, steps)),
            pltpu.SemaphoreType.DMA((steps,)),
            pltpu.SemaphoreType.DMA((steps,)),
        ],
        compiler_params=params,
        cost_estimate=cost(24),
        name="filter_spectra",
    )(opening, mix, filters)


def conv_pass(name, body, which, tables, gain, taps, filt, signals, kinds, hold):
    opening, closing, mix, unmix = tables
    outer, inner, lanes = signals[0].shape
    shape = (outer, inner, lanes)
    spec = spectrum(outer, lanes)
    return pl.pallas_call(
        functools.partial(body, which),
        in_specs=[VMEM] * (4 + len(signals)) + [ANY] * 3,
        out_specs=[ANY] * (1 + len(kinds)),
        out_shape=[jax.ShapeDtypeStruct(spec, BF16)] + [jax.ShapeDtypeStruct(shape, kind) for kind in kinds],
        scratch_shapes=[pltpu.VMEM((2 * outer, inner, lanes), F32)]
        + [pltpu.VMEM(shape, hold)]
        + [table_buffer(outer), table_buffer(outer), pltpu.VMEM(spec, BF16)]
        + [pltpu.SemaphoreType.DMA((3, outer // SIDE))]
        + [pltpu.SemaphoreType.DMA((3, max(outer // SIDE, inner // ROWS)))]
        + [pltpu.VMEM(spec, BF16)]
        + [pltpu.VMEM(shape, kind) for kind in kinds],
        compiler_params=params,
        cost_estimate=cost(20),
        name=name,
    )(opening, closing, gain, taps, *signals, mix, unmix, filt)


def grad_pass(scale, tables, spec_v, spec_m, spec_c, spec_b):
    _, closing, _, unmix = tables
    outer, _, lanes = spec_v.shape
    length = outer * INNER
    slots = 3
    return pl.pallas_call(
        functools.partial(grad_body, scale),
        in_specs=[VMEM] + [ANY] * 5,
        out_specs=ANY,
        out_shape=jax.ShapeDtypeStruct((2, lanes, length), F32),
        scratch_shapes=[
            pltpu.VMEM((2 * outer, INNER, 2 * lanes), F32),
            pltpu.VMEM((outer, INNER, 2 * lanes), F32),
            pltpu.VMEM((2, lanes, length), F32),
            pltpu.VMEM((slots, SIDE, 2 * INNER, 2 * INNER), BF16),
            pltpu.VMEM((4, slots, SIDE, 2 * INNER, lanes), BF16),
            pltpu.SemaphoreType.DMA((5, slots)),
            pltpu.SemaphoreType.DMA((8,)),
        ],
        compiler_params=params,
        cost_estimate=cost(28),
        name="filter_grads",
    )(closing, unmix, spec_v, spec_m, spec_c, spec_b)


def split_body(source, target):
    count, _, width = target.shape
    for i in range(count):
        target[i] = source[0, :, i * width : (i + 1) * width]


def rows_of(frames):
    return min(frames, 256)


def flat_width(block):
    count, frames, width = block.shape
    return jnp.swapaxes(block, 0, 1).reshape(frames, count * width)


def split_flat(block, count):
    frames, local_width = block.shape
    return jnp.swapaxes(block.reshape(frames, count, local_width // count), 0, 1)


def split_width(block, count, at):
    _, frames, local_width = block.shape
    width = local_width // count
    if width % 128:
        return split_flat(block[at], count)
    rows = rows_of(frames)
    return pl.pallas_call(
        split_body,
        grid=(frames // rows,),
        in_specs=[pl.BlockSpec((1, rows, local_width), lambda i: (at, i, 0))],
        out_specs=pl.BlockSpec((count, rows, width), lambda i: (0, i, 0)),
        out_shape=jax.ShapeDtypeStruct((count, frames, width), block.dtype),
        compiler_params=params,
        cost_estimate=cost(2),
        name="split_width",
    )(block)


def join_body(a, b, flat, halo, taps, out, carry):
    count, rows, width = a.shape

    @pl.when(pl.program_id(0) == 0)
    def _():
        carry[...] = halo[...]

    for i in range(count):
        lanes = slice(i * width, (i + 1) * width)
        out[0, :, lanes] = a[i]
        out[1, :, lanes] = b[i]
        now = flat[:, lanes].astype(F32)
        wide = jnp.concatenate([now, carry[:, lanes]], axis=0)
        total = taps[0:1, lanes] * now
        for j in (1, 2):
            total = total + taps[j : j + 1, lanes] * wide[j : j + rows]
        out[2, :, lanes] = total.astype(BF16)
        carry[:, lanes] = now[:SUB]


def join_width(a, b, flat, halo, taps):
    count, frames, width = a.shape
    if width % 128:
        wide = jnp.concatenate([flat, halo], axis=0).astype(F32)
        third = sum(taps[j][None] * wide[j : j + frames] for j in range(3)).astype(BF16)
        return jnp.stack([flat_width(a), flat_width(b), third])
    rows = rows_of(frames)
    last = frames // rows - 1
    halo = jnp.pad(halo.astype(F32), ((0, SUB - halo.shape[0]), (0, 0)))
    split = pl.BlockSpec((count, rows, width), lambda i: (0, last - i, 0))
    return pl.pallas_call(
        join_body,
        grid=(frames // rows,),
        in_specs=[
            split,
            split,
            pl.BlockSpec((rows, count * width), lambda i: (last - i, 0)),
            pl.BlockSpec(halo.shape, lambda i: (0, 0)),
            pl.BlockSpec(taps.shape, lambda i: (0, 0)),
        ],
        out_specs=pl.BlockSpec((3, rows, count * width), lambda i: (0, last - i, 0)),
        out_shape=jax.ShapeDtypeStruct((3, frames, count * width), BF16),
        scratch_shapes=[pltpu.VMEM(halo.shape, F32)],
        compiler_params=params,
        cost_estimate=cost(5),
        name="join_width",
    )(a, b, flat, halo, taps)


def output_body(second, x2, weight, out, gated):
    count, frames, width = second.shape
    rows = min(frames, 512)

    @pl.when(pl.program_id(0) == 0)
    def _():
        for i in range(count):
            lanes = slice(i * width, (i + 1) * width)
            gated[:, lanes] = (x2[:, lanes].astype(F32) * second[i].astype(F32)).astype(BF16)

    def step(at, carry):
        here = pl.ds(pl.multiple_of(at * rows, rows), rows)
        out[0, here, :] = mul(gated[here, :], weight[...]).astype(BF16)
        return carry

    lax.fori_loop(0, frames // rows, step, 0)


def output_partial(second, x2, weight):
    count, frames, width = second.shape
    local_width, model = weight.shape
    if width % 128:
        gated = (x2.astype(F32) * flat_width(second).astype(F32)).astype(BF16)
        return split_flat(mul(gated, weight).astype(BF16), lax.axis_size("tp"))
    cols = 512
    part = model // lax.axis_size("tp")
    steps = part // cols
    return pl.pallas_call(
        output_body,
        grid=(model // cols,),
        in_specs=[
            pl.BlockSpec(second.shape, lambda i: (0, 0, 0)),
            pl.BlockSpec(x2.shape, lambda i: (0, 0)),
            pl.BlockSpec((local_width, cols), lambda i: (0, i)),
        ],
        out_specs=pl.BlockSpec((1, frames, cols), lambda i: (i // steps, 0, i % steps)),
        out_shape=jax.ShapeDtypeStruct((model // part, frames, part), BF16),
        scratch_shapes=[pltpu.VMEM((frames, local_width), BF16)],
        compiler_params=params,
        cost_estimate=cost(12),
        name="output_partial",
    )(second, x2, weight)


def back_gate_body(place, own, right1, left1, right2, left2, far, weight, x2, second, bs, bx2, blocks, sems):
    pairs, frames, width = second.shape
    rows = min(frames, 512)
    depth = own.shape[1]
    me = place[0]
    last = N_TP - 1

    def copy(source, slot):
        return pltpu.make_async_copy(source, blocks.at[slot], sems.at[slot])

    def fetch_one(slot, where, source, other):
        @pl.when(where)
        def _():
            copy(source, slot).start()

        @pl.when(jnp.logical_not(where))
        def _():
            copy(other, slot).start()

    @pl.when(pl.program_id(0) == 0)
    def _():
        copy(own, 0).start()
        fetch_one(1, me == 0, far, right1)
        fetch_one(2, me == last, far, left1)
        fetch_one(3, me <= 1, left2, right2)
        for slot in range(4):
            copy(own, slot).wait()

    at_depth = [
        me,
        jnp.where(me == 0, last, me - 1),
        jnp.where(me == last, 0, me + 1),
        jnp.where(me <= 1, me + 2, me - 2),
    ]

    def step(at, carry):
        here = pl.ds(pl.multiple_of(at * rows, rows), rows)
        full = None
        for slot in range(4):
            there = pl.ds(pl.multiple_of(at_depth[slot] * depth, depth), depth)
            part = lax.dot_general(
                blocks[slot, here, :], weight[:, there], (((1,), (1,)), ((), ())), preferred_element_type=F32
            )
            full = part if full is None else full + part
        full = full.astype(BF16).astype(F32)
        for i in range(pairs):
            lanes = slice(i * width, (i + 1) * width)
            bs[i, here, :] = (full[:, lanes] * x2[here, lanes].astype(F32)).astype(BF16)
            bx2[here, lanes] = (full[:, lanes] * second[i, here, :].astype(F32)).astype(BF16)
        return carry

    lax.fori_loop(0, frames // rows, step, 0)


def back_gate(landed, weight, x2, second):
    count, frames, width = second.shape
    local_width, model = weight.shape
    pairs = 2
    wide = pairs * width
    flat = pl.BlockSpec((frames, wide), lambda i: (0, i))
    split = pl.BlockSpec((pairs, frames, width), lambda i: (i, 0, 0))
    return pl.pallas_call(
        back_gate_body,
        grid=(count // pairs,),
        in_specs=[pl.BlockSpec(memory_space=pltpu.SMEM)]
        + [ANY] * 6
        + [pl.BlockSpec((wide, model), lambda i: (i, 0)), flat, split],
        out_specs=[split, flat],
        out_shape=[
            jax.ShapeDtypeStruct((count, frames, width), BF16),
            jax.ShapeDtypeStruct((frames, local_width), BF16),
        ],
        scratch_shapes=[pltpu.VMEM((4,) + landed[0].shape, BF16), pltpu.SemaphoreType.DMA((4,))],
        compiler_params=params,
        cost_estimate=cost(14),
        name="back_gate",
    )(lax.axis_index("tp").reshape(1), *landed, weight, x2, second)


def back_gate_plain(gathered, weight, x2, second):
    full = lax.dot_general(gathered, weight, (((1,), (1,)), ((), ())), preferred_element_type=F32)
    full = full.astype(BF16).astype(F32)
    bs = split_flat((full * x2.astype(F32)).astype(BF16), second.shape[0])
    return bs, (full * flat_width(second).astype(F32)).astype(BF16)


def send(block, *pairs):
    return lax.ppermute(block, "tp", pairs)


def picked(blocks, at):
    return lax.dynamic_index_in_dim(blocks, at, axis=0, keepdims=False)


def added(*blocks):
    return sum(block.astype(F32) for block in blocks).astype(BF16)


def after(value, *others):
    return lax.optimization_barrier((value, *others))[0]


def swap(block):
    return lax.all_to_all(block, "seq", split_axis=0, concat_axis=0, tiled=True)


def to_frames(block):
    count = lax.axis_size("seq")
    length, width = block.shape
    return swap(block.reshape(count, length // count, width))


def neighbour_rows(rows, shift):
    count = lax.axis_size("seq")
    pairs = [(i, i + shift) for i in range(count) if 0 <= i + shift < count]
    return lax.ppermute(rows, "seq", pairs)


def short_filter(block, before, taps):
    length = block.shape[0]
    wide = jnp.concatenate([before, block], axis=0).astype(F32)
    return sum(taps[j][None] * wide[2 - j : 2 - j + length] for j in range(3)).astype(BF16)


def local(projected, short_kernel, filters, skip_gain, out_weight, out_grad):
    _, frames, _, local_width = projected.shape
    _, width, length = filters.shape
    count = lax.axis_size("seq")
    outer = length // INNER
    grid3 = (outer, INNER, width)
    scale = float(length) ** -0.5
    mine = lax.axis_index("seq") * width
    taps = lax.dynamic_slice_in_dim(short_kernel, mine, width, axis=2)
    tables = transform_tables(outer)

    branches = jnp.transpose(projected[0], (1, 0, 2))
    before_x2 = neighbour_rows(branches[2, frames - 2 :], 1)
    raw_v = swap(after(split_width(branches, count, 0), before_x2)).reshape(grid3)
    own = out_grad[0]
    me = lax.axis_index("tp")
    chain = width % 128 == 0 and lax.axis_size("tp") == N_TP
    if chain:
        right1 = send(own, (0, 1), (1, 2), (2, 3))
        left1 = send(own, (1, 0), (2, 1), (3, 2))
    filt = filter_spectra(tables, filters)
    raw_v = after(raw_v, filt)
    raw_x1 = swap(after(split_width(branches, count, 1), raw_v)).reshape(grid3)

    spec_v, first = conv_pass("first", first_body, 0, tables, skip_gain, taps[0], filt, [raw_v], [F32], BF16)
    if chain:
        raw_x1, first, right1, left1, own = lax.optimization_barrier((raw_x1, first, right1, left1, own))
        right2 = send(right1, (1, 2), (2, 3))
        left2 = send(left1, (2, 1), (1, 0))
        far = send(own, (0, 3), (3, 0))
    else:
        raw_x1, first = lax.optimization_barrier((raw_x1, first))
    spec_m, second, x1 = conv_pass(
        "second", second_body, 1, tables, skip_gain, taps[1], filt, [first, raw_x1], [BF16, BF16], F32
    )
    branch_x2, second = lax.optimization_barrier((branches[2], second))
    if chain:
        far, branch_x2 = lax.optimization_barrier((far, branch_x2))
    x2 = short_filter(branch_x2, before_x2, short_kernel[2])
    second = to_frames(second.reshape(length, width))
    partial = output_partial(second, x2, out_weight)
    if chain:
        ends = ((0, 1), (3, 2))
        across = ((1, 2), (2, 1))
        handed1 = send(picked(partial, jnp.where(me == 0, 3, 0)), *ends)
        right2, left2, partial = lax.optimization_barrier((right2, left2, partial))
        bs, bx2 = back_gate([own, right1, left1, right2, left2, far], out_weight, x2, second)
        handed1, bx2 = lax.optimization_barrier((handed1, bx2))
        crossed1 = send(added(picked(partial, jnp.where(me == 1, 3, 0)), handed1), *across)
        handed2 = send(after(picked(partial, jnp.where(me == 0, 2, 1)), handed1), *ends)
    else:
        bs, bx2 = back_gate_plain(lax.all_gather(own, "tp", axis=1, tiled=True), out_weight, x2, second)
        flat = flat_width(partial)
        output = lax.psum_scatter(flat, "tp", scatter_dimension=1, tiled=True)
    bs, after_x2 = lax.optimization_barrier((swap(bs).reshape(grid3), neighbour_rows(bx2[:2], -1)))
    spec_b, bf, grad_x1 = conv_pass(
        "back_second", back_second_body, 1, tables, skip_gain, taps[1], filt, [bs, first, x1], [F32, BF16], BF16
    )
    moved1 = to_frames(grad_x1.reshape(length, width))
    if chain:
        handed2, crossed1, bf = lax.optimization_barrier((handed2, crossed1, bf))
        crossed2 = send(added(picked(partial, jnp.where(me == 1, 2, 1)), handed2), *across)
        outward = send(added(picked(partial, jnp.where(me == 2, 3, 0)), crossed1), (1, 0), (2, 3))
        handed3 = send(after(picked(partial, jnp.where(me == 0, 1, 2)), handed2), *ends)
    spec_c, grad_v = conv_pass(
        "back_first", back_first_body, 0, tables, skip_gain, taps[0], filt, [bf], [BF16], BF16
    )
    moved1, grad_v, spec_b = lax.optimization_barrier((moved1, grad_v, spec_b))
    moved0 = to_frames(grad_v.reshape(length, width))
    filter_grad = grad_pass(scale, tables, spec_v, spec_m, spec_c, spec_b)

    if chain:
        crossed2, outward, handed3, filter_grad = lax.optimization_barrier((crossed2, outward, handed3, filter_grad))
        output = added(picked(partial, me), crossed2, handed3, outward)
    output = output[None]
    joined = join_width(moved0, moved1, bx2, after_x2, short_kernel[2])
    projected_grad = jnp.transpose(joined, (1, 0, 2))[None]
    return (output, projected_grad, filter_grad)


def solution(mesh):
    in_specs = (
        P(None, "seq", None, "tp"),
        P(None, None, "tp"),
        P(None, ("tp", "seq"), None),
        P(None, ("tp", "seq")),
        P("tp", None),
        P(None, "seq", "tp"),
    )
    out_specs = (P(None, "seq", "tp"), P(None, "seq", None, "tp"), P(None, ("tp", "seq"), None))
    return jax.shard_map(local, mesh=mesh, in_specs=in_specs, out_specs=out_specs, check_vma=False)
```

```python
import functools
import math

import jax
import jax.numpy as jnp
import ml_dtypes
import numpy as np
from jax import lax
from jax.experimental import pallas as pl
from jax.experimental.pallas import tpu as pltpu
from jax.sharding import PartitionSpec as P

F32 = jnp.float32
BF16 = jnp.bfloat16
INNER = 128
SUB = 8
ROWS = 16
SIDE = 8


def spread_table(outer, scale):
    freq = np.arange(2 * outer * SUB)[:, None]
    time = np.arange(outer * SUB)[None, :]
    row = freq // SUB
    turn = 4 * outer
    phase = (4 * (row % outer) + 1) * (time // SUB) + outer * (row // outer)
    value = np.cos((phase % turn) * (2.0 * math.pi / turn)) * scale
    return np.where(freq % SUB == time % SUB, value, 0.0)


def transform_tables(outer):
    total = outer * INNER
    ids = np.arange(INNER)
    twist = 2.0 * math.pi * (np.arange(outer)[:, None] + 0.25) * ids[None, :] / total
    inner = 2.0 * math.pi * (ids[:, None] * ids[None, :] % INNER) / INNER
    angle = twist[:, None, :] + inner[None]
    cos, sin = np.cos(angle), np.sin(angle)
    mix = np.concatenate(
        [np.concatenate([cos, sin], axis=2), np.concatenate([-sin, cos], axis=2)], axis=1
    )
    opening = spread_table(outer, 1.0)
    closing = spread_table(outer, 1.0 / total).T
    unmix = np.swapaxes(mix, 1, 2)
    return [jnp.asarray(np.ascontiguousarray(t).astype(ml_dtypes.bfloat16)) for t in (opening, closing, mix, unmix)]


def mul(a, b):
    return jnp.dot(a, b, preferred_element_type=F32)


def halves(spec):
    return spec[:INNER].astype(F32), spec[INNER:].astype(F32)


def cmul(a, b):
    (ar, ai), (br, bi) = a, b
    return ar * br - ai * bi, ar * bi + ai * br


def conj_mul(a, b):
    (ar, ai), (br, bi) = a, b
    return ar * br + ai * bi, ar * bi - ai * br


def packed(pair):
    return jnp.concatenate(pair, axis=0).astype(BF16)


def open_phase(opening, read, spec):
    twice, inner, lanes = spec.shape
    outer = twice // 2

    def step(at, carry):
        row = pl.multiple_of(at * ROWS, ROWS)
        signal = read(row)
        wide = jnp.concatenate([signal[:, :SUB], signal[:, SUB:]], axis=2)
        flat = wide.reshape(outer * SUB, 2 * lanes).astype(BF16)
        out = mul(opening[...], flat).reshape(twice, SUB, 2 * lanes)
        spec[:, pl.ds(row, SUB), :] = out[:, :, :lanes]
        spec[:, pl.ds(row + SUB, SUB), :] = out[:, :, lanes:]
        return carry

    lax.fori_loop(0, inner // ROWS, step, 0)


def close_phase(closing, spec, write):
    twice, inner, lanes = spec.shape
    outer = twice // 2

    def step(at, carry):
        row = pl.multiple_of(at * ROWS, ROWS)
        wide = jnp.concatenate([spec[:, pl.ds(row, SUB), :], spec[:, pl.ds(row + SUB, SUB), :]], axis=2)
        flat = wide.reshape(twice * SUB, 2 * lanes).astype(BF16)
        out = mul(closing[...], flat).reshape(outer, SUB, 2 * lanes)
        write(at, row, jnp.concatenate([out[:, :, :lanes], out[:, :, lanes:]], axis=1))
        return carry

    lax.fori_loop(0, inner // ROWS, step, 0)


def fetch(sources, buffers, sems):
    outer = buffers[0].shape[0]

    def piece(which, at):
        rows = pl.ds(at * SIDE, SIDE)
        return pltpu.make_async_copy(sources[which].at[rows], buffers[which].at[rows], sems.at[which, at])

    for at in range(outer // SIDE):
        for which in range(len(sources)):
            piece(which, at).start()
    return [lambda at, which=which: piece(which, at).wait() for which in range(len(sources))]


def columns(spec, ids):
    outer = spec.shape[0] // 2
    return [packed([spec[i], spec[outer + i]]) for i in ids]


def put_columns(spec, ids, values):
    outer = spec.shape[0] // 2
    for i, value in zip(ids, values):
        spec[i] = value[:INNER]
        spec[outer + i] = value[INNER:]


def short_phase(raw, taps, out):
    outer, inner, lanes = raw.shape

    def step(p, before):
        now = raw[p].astype(F32)
        wide = jnp.concatenate([before, now], axis=0)
        total = taps[0:1, :] * now
        for j in (1, 2):
            total = total + taps[j : j + 1, :] * wide[SUB - j : SUB - j + inner]
        out[p] = total.astype(BF16)
        return now[inner - SUB :]

    lax.fori_loop(0, outer, step, jnp.zeros((SUB, lanes), F32))


def short_back_phase(raw, taps, out, leave):
    outer, inner, lanes = raw.shape

    def step(at, after):
        p = outer - 1 - at
        now = raw[p].astype(F32)
        wide = jnp.concatenate([now, after], axis=0)
        total = taps[0:1, :] * now
        for j in (1, 2):
            total = total + taps[j : j + 1, :] * wide[j : j + inner]
        out[p] = total.astype(BF16)
        return now[:SUB]

    def group(at, after):
        for i in range(SIDE):
            after = step(at * SIDE + i, after)
        leave(outer // SIDE - 1 - at).start()
        return after

    lax.fori_loop(0, outer // SIDE, group, jnp.zeros((SUB, lanes), F32))


def leave_sides(buffer, target, sems, which):
    def copy(at):
        rows = pl.ds(at * SIDE, SIDE)
        return pltpu.make_async_copy(buffer.at[rows], target.at[rows], sems.at[which, at])

    return copy


def leave_rows(buffer, target, sems, which):
    def copy(at):
        rows = pl.ds(pl.multiple_of(at * ROWS, ROWS), ROWS)
        return pltpu.make_async_copy(buffer.at[:, rows], target.at[:, rows], sems.at[which, at])

    return copy


def settle(copy, steps):
    def step(at, carry):
        copy(at).wait()
        return carry

    lax.fori_loop(0, steps, step, 0)


def filters_body(opening, mix_hbm, filt_hbm, out_hbm, spec, sig, filt, mix, out, sems, filt_sems, out_sems):
    waits = fetch([mix_hbm], [mix], sems)
    outer, inner, both = sig.shape
    lanes = both // 2
    parts = outer // SIDE

    def arrive(part):
        frames = pl.ds(pl.multiple_of(part * SIDE * inner, SIDE * inner), SIDE * inner)
        return pltpu.make_async_copy(filt_hbm.at[:, :, frames], filt.at[:, :, frames], filt_sems.at[part])

    for part in range(parts):
        arrive(part).start()

    def turn(part, carry):
        arrive(part).wait()
        for q in range(SIDE):
            p = part * SIDE + q
            here = pl.ds(pl.multiple_of(p * inner, inner), inner)
            sig[p, :, :lanes] = jnp.transpose(filt[0, :, here])
            sig[p, :, lanes:] = jnp.transpose(filt[1, :, here])
        return carry

    lax.fori_loop(0, parts, turn, 0)
    open_phase(opening, lambda row: sig[:, pl.ds(row, ROWS), :], spec)

    def leave(at):
        rows = pl.ds(at * SIDE, SIDE)
        return pltpu.make_async_copy(out.at[:, rows], out_hbm.at[:, rows], out_sems.at[at])

    def step(at, carry):
        waits[0](at)
        ids = [at * SIDE + i for i in range(SIDE)]
        results = [mul(mix[i], col) for i, col in zip(ids, columns(spec, ids))]
        for i, value in zip(ids, results):
            out[0, i] = value[:, :lanes].astype(BF16)
            out[1, i] = value[:, lanes:].astype(BF16)
        leave(at).start()
        return carry

    lax.fori_loop(0, parts, step, 0)
    settle(leave, parts)


def conv_phase(spec, filt, mix, unmix, waits, kept, product, leave):
    def step(at, carry):
        for wait in waits:
            wait(at)
        ids = [at * SIDE + i for i in range(SIDE)]
        seen = [mul(mix[i], col) for i, col in zip(ids, columns(spec, ids))]
        mixed = [packed(product(halves(filt[i]), halves(x))) for i, x in zip(ids, seen)]
        done = [mul(unmix[i], y) for i, y in zip(ids, mixed)]
        for i, x in zip(ids, seen):
            kept[i] = x.astype(BF16)
        leave(at).start()
        put_columns(spec, ids, done)
        return carry

    lax.fori_loop(0, filt.shape[0] // SIDE, step, 0)


def first_body(
    which, opening, closing, gain, taps, raw, mix_hbm, unmix_hbm, filt_hbm, kept_hbm, first_hbm,
    spec, v, mix, unmix, filt, sems, out_sems, kept, first
):
    waits = fetch([mix_hbm, unmix_hbm, filt_hbm.at[which]], [mix, unmix, filt], sems)
    leave_kept = leave_sides(kept, kept_hbm, out_sems, 0)
    leave_first = leave_rows(first, first_hbm, out_sems, 1)
    short_phase(raw, taps, v)
    open_phase(opening, lambda row: v[:, pl.ds(row, ROWS), :].astype(F32), spec)
    conv_phase(spec, filt, mix, unmix, waits, kept, cmul, leave_kept)
    g0 = gain[0:1, :][None]

    def write(at, row, value):
        rows = pl.ds(row, ROWS)
        first[:, rows, :] = g0 * v[:, rows, :].astype(F32) + value
        leave_first(at).start()

    close_phase(closing, spec, write)
    settle(leave_kept, kept.shape[0] // SIDE)
    settle(leave_first, first.shape[1] // ROWS)


def second_body(
    which, opening, closing, gain, taps, first, raw, mix_hbm, unmix_hbm, filt_hbm, kept_hbm, second_hbm, x1_hbm,
    spec, mid, mix, unmix, filt, sems, out_sems, kept, second, x1
):
    waits = fetch([mix_hbm, unmix_hbm, filt_hbm.at[which]], [mix, unmix, filt], sems)
    leave_kept = leave_sides(kept, kept_hbm, out_sems, 0)
    leave_second = leave_rows(second, second_hbm, out_sems, 1)
    leave_x1 = pltpu.make_async_copy(x1, x1_hbm, out_sems.at[2, 0])
    short_phase(raw, taps, x1)
    leave_x1.start()

    def read(row):
        rows = pl.ds(row, ROWS)
        value = x1[:, rows, :].astype(F32) * first[:, rows, :]
        mid[:, rows, :] = value
        return value

    open_phase(opening, read, spec)
    conv_phase(spec, filt, mix, unmix, waits, kept, cmul, leave_kept)
    g1 = gain[1:2, :][None]

    def write(at, row, value):
        rows = pl.ds(row, ROWS)
        second[:, rows, :] = (g1 * mid[:, rows, :] + value).astype(BF16)
        leave_second(at).start()

    close_phase(closing, spec, write)
    leave_x1.wait()
    settle(leave_kept, kept.shape[0] // SIDE)
    settle(leave_second, second.shape[1] // ROWS)


def back_second_body(
    which, opening, closing, gain, taps, bs, first, x1, mix_hbm, unmix_hbm, filt_hbm, kept_hbm, bf_hbm, grad_hbm,
    spec, bx1, mix, unmix, filt, sems, out_sems, kept, bf, grad_x1
):
    waits = fetch([mix_hbm, unmix_hbm, filt_hbm.at[which]], [mix, unmix, filt], sems)
    leave_kept = leave_sides(kept, kept_hbm, out_sems, 0)
    leave_bf = leave_rows(bf, bf_hbm, out_sems, 1)
    leave_grad = leave_sides(grad_x1, grad_hbm, out_sems, 2)
    open_phase(opening, lambda row: bs[:, pl.ds(row, ROWS), :].astype(F32), spec)
    conv_phase(spec, filt, mix, unmix, waits, kept, conj_mul, leave_kept)
    g1 = gain[1:2, :][None]

    def write(at, row, value):
        rows = pl.ds(row, ROWS)
        back_middle = g1 * bs[:, rows, :].astype(F32) + value
        bf[:, rows, :] = back_middle * x1[:, rows, :].astype(F32)
        bx1[:, rows, :] = (back_middle * first[:, rows, :]).astype(BF16)
        leave_bf(at).start()

    close_phase(closing, spec, write)
    short_back_phase(bx1, taps, grad_x1, leave_grad)
    settle(leave_kept, kept.shape[0] // SIDE)
    settle(leave_bf, bf.shape[1] // ROWS)
    settle(leave_grad, kept.shape[0] // SIDE)


def back_first_body(
    which, opening, closing, gain, taps, bf, mix_hbm, unmix_hbm, filt_hbm, kept_hbm, grad_hbm,
    spec, bv, mix, unmix, filt, sems, out_sems, kept, grad_v
):
    waits = fetch([mix_hbm, unmix_hbm, filt_hbm.at[which]], [mix, unmix, filt], sems)
    leave_kept = leave_sides(kept, kept_hbm, out_sems, 0)
    leave_grad = leave_sides(grad_v, grad_hbm, out_sems, 1)
    open_phase(opening, lambda row: bf[:, pl.ds(row, ROWS), :], spec)
    conv_phase(spec, filt, mix, unmix, waits, kept, conj_mul, leave_kept)
    g0 = gain[0:1, :][None]

    def write(at, row, value):
        rows = pl.ds(row, ROWS)
        bv[:, rows, :] = (g0 * bf[:, rows, :] + value).astype(BF16)

    close_phase(closing, spec, write)
    short_back_phase(bv, taps, grad_v, leave_grad)
    settle(leave_kept, kept.shape[0] // SIDE)
    settle(leave_grad, kept.shape[0] // SIDE)


def grad_body(scale, closing, unmix_hbm, v_hbm, m_hbm, c_hbm, b_hbm, out_hbm, spec, closed, out, unmix, pieces, sems, out_sems):
    outer, inner, both = closed.shape
    lanes = both // 2
    steps = outer // SIDE
    slots = unmix.shape[0]

    def copies(at):
        rows, slot = pl.ds(at * SIDE, SIDE), lax.rem(at, slots)
        found = [pltpu.make_async_copy(unmix_hbm.at[rows], unmix.at[slot], sems.at[0, slot])]
        for which, source in enumerate((v_hbm, m_hbm, c_hbm, b_hbm)):
            target = pieces.at[which, slot]
            found.append(pltpu.make_async_copy(source.at[rows], target, sems.at[1 + which, slot]))
        return found

    for at in range(min(slots, steps)):
        for copy in copies(at):
            copy.start()

    def step(at, carry):
        slot = lax.rem(at, slots)
        for copy in copies(at):
            copy.wait()
        mixed = []
        for i in range(SIDE):
            left, right = [packed(conj_mul(halves(pieces[k, slot, i]), halves(pieces[2 + k, slot, i]))) for k in range(2)]
            mixed.append(jnp.concatenate([left, right], axis=1))
        done = [mul(unmix[slot, i], y) for i, y in enumerate(mixed)]
        put_columns(spec, [at * SIDE + i for i in range(SIDE)], done)

        @pl.when(at + slots < steps)
        def _():
            for copy in copies(at + slots):
                copy.start()

        return carry

    lax.fori_loop(0, steps, step, 0)

    def write(at, row, value):
        closed[:, pl.ds(row, ROWS), :] = value * scale

    close_phase(closing, spec, write)
    parts = out_sems.shape[0]
    span = outer // parts

    def leave(part):
        columns_of = pl.ds(pl.multiple_of(part * span * inner, inner), span * inner)
        return pltpu.make_async_copy(out.at[:, :, columns_of], out_hbm.at[:, :, columns_of], out_sems.at[part])

    def turn(part, carry):
        for q in range(span):
            p = part * span + q
            here = pl.ds(pl.multiple_of(p * inner, inner), inner)
            out[0, :, here] = jnp.transpose(closed[p, :, :lanes])
            out[1, :, here] = jnp.transpose(closed[p, :, lanes:])
        leave(part).start()
        return carry

    lax.fori_loop(0, parts, turn, 0)

    settle(leave, parts)


params = pltpu.CompilerParams(vmem_limit_bytes=58 << 20)
VMEM = pl.BlockSpec(memory_space=pltpu.VMEM)
ANY = pl.BlockSpec(memory_space=pl.ANY)


def table_buffer(outer):
    return pltpu.VMEM((outer, 2 * INNER, 2 * INNER), BF16)


def spectrum(outer, lanes):
    return (outer, 2 * INNER, lanes)


def cost(us):
    return pl.CostEstimate(flops=int(us * 0.8e6), bytes_accessed=int(us * 1e5), transcendentals=0)


def filter_spectra(tables, filters):
    opening, _, mix, _ = tables
    _, lanes, length = filters.shape
    outer = length // INNER
    steps = outer // SIDE
    shape = (2,) + spectrum(outer, lanes)
    return pl.pallas_call(
        filters_body,
        in_specs=[VMEM, ANY, ANY],
        out_specs=ANY,
        out_shape=jax.ShapeDtypeStruct(shape, BF16),
        scratch_shapes=[
            pltpu.VMEM((2 * outer, INNER, 2 * lanes), F32),
            pltpu.VMEM((outer, INNER, 2 * lanes), F32),
            pltpu.VMEM(filters.shape, F32),
            table_buffer(outer),
            pltpu.VMEM(shape, BF16),
            pltpu.SemaphoreType.DMA((1, steps)),
            pltpu.SemaphoreType.DMA((steps,)),
            pltpu.SemaphoreType.DMA((steps,)),
        ],
        compiler_params=params,
        cost_estimate=cost(24),
        name="filter_spectra",
    )(opening, mix, filters)


def conv_pass(name, body, which, tables, gain, taps, filt, signals, kinds, hold):
    opening, closing, mix, unmix = tables
    outer, inner, lanes = signals[0].shape
    shape = (outer, inner, lanes)
    spec = spectrum(outer, lanes)
    return pl.pallas_call(
        functools.partial(body, which),
        in_specs=[VMEM] * (4 + len(signals)) + [ANY] * 3,
        out_specs=[ANY] * (1 + len(kinds)),
        out_shape=[jax.ShapeDtypeStruct(spec, BF16)] + [jax.ShapeDtypeStruct(shape, kind) for kind in kinds],
        scratch_shapes=[pltpu.VMEM((2 * outer, inner, lanes), F32)]
        + [pltpu.VMEM(shape, hold)]
        + [table_buffer(outer), table_buffer(outer), pltpu.VMEM(spec, BF16)]
        + [pltpu.SemaphoreType.DMA((3, outer // SIDE))]
        + [pltpu.SemaphoreType.DMA((3, max(outer // SIDE, inner // ROWS)))]
        + [pltpu.VMEM(spec, BF16)]
        + [pltpu.VMEM(shape, kind) for kind in kinds],
        compiler_params=params,
        cost_estimate=cost(20),
        name=name,
    )(opening, closing, gain, taps, *signals, mix, unmix, filt)


def grad_pass(scale, tables, spec_v, spec_m, spec_c, spec_b):
    _, closing, _, unmix = tables
    outer, _, lanes = spec_v.shape
    length = outer * INNER
    slots = 3
    return pl.pallas_call(
        functools.partial(grad_body, scale),
        in_specs=[VMEM] + [ANY] * 5,
        out_specs=ANY,
        out_shape=jax.ShapeDtypeStruct((2, lanes, length), F32),
        scratch_shapes=[
            pltpu.VMEM((2 * outer, INNER, 2 * lanes), F32),
            pltpu.VMEM((outer, INNER, 2 * lanes), F32),
            pltpu.VMEM((2, lanes, length), F32),
            pltpu.VMEM((slots, SIDE, 2 * INNER, 2 * INNER), BF16),
            pltpu.VMEM((4, slots, SIDE, 2 * INNER, lanes), BF16),
            pltpu.SemaphoreType.DMA((5, slots)),
            pltpu.SemaphoreType.DMA((8,)),
        ],
        compiler_params=params,
        cost_estimate=cost(28),
        name="filter_grads",
    )(closing, unmix, spec_v, spec_m, spec_c, spec_b)


def split_body(source, target):
    count, _, width = target.shape
    for i in range(count):
        target[i] = source[0, :, i * width : (i + 1) * width]


def rows_of(frames):
    return min(frames, 256)


def flat_width(block):
    count, frames, width = block.shape
    return jnp.swapaxes(block, 0, 1).reshape(frames, count * width)


def split_flat(block, count):
    frames, local_width = block.shape
    return jnp.swapaxes(block.reshape(frames, count, local_width // count), 0, 1)


def split_width(block, count, at):
    _, frames, local_width = block.shape
    width = local_width // count
    if width % 128:
        return split_flat(block[at], count)
    rows = rows_of(frames)
    return pl.pallas_call(
        split_body,
        grid=(frames // rows,),
        in_specs=[pl.BlockSpec((1, rows, local_width), lambda i: (at, i, 0))],
        out_specs=pl.BlockSpec((count, rows, width), lambda i: (0, i, 0)),
        out_shape=jax.ShapeDtypeStruct((count, frames, width), block.dtype),
        compiler_params=params,
        cost_estimate=cost(2),
        name="split_width",
    )(block)


def join_body(a, b, flat, halo, taps, out, carry):
    count, rows, width = a.shape

    @pl.when(pl.program_id(0) == 0)
    def _():
        carry[...] = halo[...]

    for i in range(count):
        lanes = slice(i * width, (i + 1) * width)
        out[0, :, lanes] = a[i]
        out[1, :, lanes] = b[i]
        now = flat[:, lanes].astype(F32)
        wide = jnp.concatenate([now, carry[:, lanes]], axis=0)
        total = taps[0:1, lanes] * now
        for j in (1, 2):
            total = total + taps[j : j + 1, lanes] * wide[j : j + rows]
        out[2, :, lanes] = total.astype(BF16)
        carry[:, lanes] = now[:SUB]


def join_width(a, b, flat, halo, taps):
    count, frames, width = a.shape
    if width % 128:
        wide = jnp.concatenate([flat, halo], axis=0).astype(F32)
        third = sum(taps[j][None] * wide[j : j + frames] for j in range(3)).astype(BF16)
        return jnp.stack([flat_width(a), flat_width(b), third])
    rows = rows_of(frames)
    last = frames // rows - 1
    halo = jnp.pad(halo.astype(F32), ((0, SUB - halo.shape[0]), (0, 0)))
    split = pl.BlockSpec((count, rows, width), lambda i: (0, last - i, 0))
    return pl.pallas_call(
        join_body,
        grid=(frames // rows,),
        in_specs=[
            split,
            split,
            pl.BlockSpec((rows, count * width), lambda i: (last - i, 0)),
            pl.BlockSpec(halo.shape, lambda i: (0, 0)),
            pl.BlockSpec(taps.shape, lambda i: (0, 0)),
        ],
        out_specs=pl.BlockSpec((3, rows, count * width), lambda i: (0, last - i, 0)),
        out_shape=jax.ShapeDtypeStruct((3, frames, count * width), BF16),
        scratch_shapes=[pltpu.VMEM(halo.shape, F32)],
        compiler_params=params,
        cost_estimate=cost(5),
        name="join_width",
    )(a, b, flat, halo, taps)


def output_body(second, x2, weight, out, gated):
    count, frames, width = second.shape
    rows = min(frames, 512)

    @pl.when(pl.program_id(0) == 0)
    def _():
        for i in range(count):
            lanes = slice(i * width, (i + 1) * width)
            gated[:, lanes] = (x2[:, lanes].astype(F32) * second[i].astype(F32)).astype(BF16)

    def step(at, carry):
        here = pl.ds(pl.multiple_of(at * rows, rows), rows)
        out[0, here, :] = mul(gated[here, :], weight[...]).astype(BF16)
        return carry

    lax.fori_loop(0, frames // rows, step, 0)


def output_partial(second, x2, weight):
    count, frames, width = second.shape
    local_width, model = weight.shape
    if width % 128:
        gated = (x2.astype(F32) * flat_width(second).astype(F32)).astype(BF16)
        return split_flat(mul(gated, weight).astype(BF16), lax.axis_size("tp"))
    cols = 512
    part = model // lax.axis_size("tp")
    steps = part // cols
    return pl.pallas_call(
        output_body,
        grid=(model // cols,),
        in_specs=[
            pl.BlockSpec(second.shape, lambda i: (0, 0, 0)),
            pl.BlockSpec(x2.shape, lambda i: (0, 0)),
            pl.BlockSpec((local_width, cols), lambda i: (0, i)),
        ],
        out_specs=pl.BlockSpec((1, frames, cols), lambda i: (i // steps, 0, i % steps)),
        out_shape=jax.ShapeDtypeStruct((model // part, frames, part), BF16),
        scratch_shapes=[pltpu.VMEM((frames, local_width), BF16)],
        compiler_params=params,
        cost_estimate=cost(12),
        name="output_partial",
    )(second, x2, weight)


def back_gate_body(gathered, weight, x2, second, bs, bx2):
    pairs, frames, width = second.shape
    rows = min(frames, 512)

    def step(at, carry):
        here = pl.ds(pl.multiple_of(at * rows, rows), rows)
        full = lax.dot_general(
            gathered[here, :], weight[...], (((1,), (1,)), ((), ())), preferred_element_type=F32
        )
        full = full.astype(BF16).astype(F32)
        for i in range(pairs):
            lanes = slice(i * width, (i + 1) * width)
            bs[i, here, :] = (full[:, lanes] * x2[here, lanes].astype(F32)).astype(BF16)
            bx2[here, lanes] = (full[:, lanes] * second[i, here, :].astype(F32)).astype(BF16)
        return carry

    lax.fori_loop(0, frames // rows, step, 0)


def back_gate(gathered, weight, x2, second):
    count, frames, width = second.shape
    local_width, model = weight.shape
    if width % 128:
        full = lax.dot_general(gathered, weight, (((1,), (1,)), ((), ())), preferred_element_type=F32)
        full = full.astype(BF16).astype(F32)
        bs = split_flat((full * x2.astype(F32)).astype(BF16), count)
        return bs, (full * flat_width(second).astype(F32)).astype(BF16)
    pairs = 2
    wide = pairs * width
    flat = pl.BlockSpec((frames, wide), lambda i: (0, i))
    split = pl.BlockSpec((pairs, frames, width), lambda i: (i, 0, 0))
    return pl.pallas_call(
        back_gate_body,
        grid=(count // pairs,),
        in_specs=[
            pl.BlockSpec(gathered.shape, lambda i: (0, 0)),
            pl.BlockSpec((wide, model), lambda i: (i, 0)),
            flat,
            split,
        ],
        out_specs=[split, flat],
        out_shape=[
            jax.ShapeDtypeStruct((count, frames, width), BF16),
            jax.ShapeDtypeStruct((frames, local_width), BF16),
        ],
        compiler_params=params,
        cost_estimate=cost(14),
        name="back_gate",
    )(gathered, weight, x2, second)


def after(value, *others):
    return lax.optimization_barrier((value, *others))[0]


def swap(block):
    return lax.all_to_all(block, "seq", split_axis=0, concat_axis=0, tiled=True)


def to_frames(block):
    count = lax.axis_size("seq")
    length, width = block.shape
    return swap(block.reshape(count, length // count, width))


def neighbour_rows(rows, shift):
    count = lax.axis_size("seq")
    pairs = [(i, i + shift) for i in range(count) if 0 <= i + shift < count]
    return lax.ppermute(rows, "seq", pairs)


def short_filter(block, before, taps):
    length = block.shape[0]
    wide = jnp.concatenate([before, block], axis=0).astype(F32)
    return sum(taps[j][None] * wide[2 - j : 2 - j + length] for j in range(3)).astype(BF16)


def local(projected, short_kernel, filters, skip_gain, out_weight, out_grad):
    _, frames, _, local_width = projected.shape
    _, width, length = filters.shape
    count = lax.axis_size("seq")
    outer = length // INNER
    grid3 = (outer, INNER, width)
    scale = float(length) ** -0.5
    mine = lax.axis_index("seq") * width
    taps = lax.dynamic_slice_in_dim(short_kernel, mine, width, axis=2)
    tables = transform_tables(outer)

    branches = jnp.transpose(projected[0], (1, 0, 2))
    before_x2 = neighbour_rows(branches[2, frames - 2 :], 1)
    raw_v = swap(after(split_width(branches, count, 0), before_x2)).reshape(grid3)
    gathered = lax.all_gather(out_grad[0], "tp", axis=1, tiled=True)
    filt = filter_spectra(tables, filters)
    raw_v = after(raw_v, filt)
    raw_x1 = swap(after(split_width(branches, count, 1), raw_v)).reshape(grid3)

    spec_v, first = conv_pass("first", first_body, 0, tables, skip_gain, taps[0], filt, [raw_v], [F32], BF16)
    raw_x1, first = lax.optimization_barrier((raw_x1, first))
    spec_m, second, x1 = conv_pass(
        "second", second_body, 1, tables, skip_gain, taps[1], filt, [first, raw_x1], [BF16, BF16], F32
    )
    branch_x2, second = lax.optimization_barrier((branches[2], second))
    x2 = short_filter(branch_x2, before_x2, short_kernel[2])
    second = to_frames(second.reshape(length, width))
    partial = output_partial(second, x2, out_weight)
    output = lax.psum_scatter(partial, "tp", scatter_dimension=0, tiled=True)

    gathered, _ = lax.optimization_barrier((gathered, partial))
    bs, bx2 = back_gate(gathered, out_weight, x2, second)
    bs, after_x2 = lax.optimization_barrier((swap(bs).reshape(grid3), neighbour_rows(bx2[:2], -1)))
    spec_b, bf, grad_x1 = conv_pass(
        "back_second", back_second_body, 1, tables, skip_gain, taps[1], filt, [bs, first, x1], [F32, BF16], BF16
    )
    moved1 = to_frames(grad_x1.reshape(length, width))
    spec_c, grad_v = conv_pass(
        "back_first", back_first_body, 0, tables, skip_gain, taps[0], filt, [bf], [BF16], BF16
    )
    moved1, grad_v, spec_b = lax.optimization_barrier((moved1, grad_v, spec_b))
    moved0 = to_frames(grad_v.reshape(length, width))
    filter_grad = grad_pass(scale, tables, spec_v, spec_m, spec_c, spec_b)

    joined = join_width(moved0, moved1, bx2, after_x2, short_kernel[2])
    projected_grad = jnp.transpose(joined, (1, 0, 2))[None]
    return (output, projected_grad, filter_grad)


def solution(mesh):
    in_specs = (
        P(None, "seq", None, "tp"),
        P(None, None, "tp"),
        P(None, ("tp", "seq"), None),
        P(None, ("tp", "seq")),
        P("tp", None),
        P(None, "seq", "tp"),
    )
    out_specs = (P(None, "seq", "tp"), P(None, "seq", None, "tp"), P(None, ("tp", "seq"), None))
    return jax.shard_map(local, mesh=mesh, in_specs=in_specs, out_specs=out_specs, check_vma=False)
```
